256 devices in a mesh: row: 16 (over z_lo, x, core), col: 16 (over z_hi, y).
Axes of the slice: x: 4, y: 4, z: 8 (z_hi: 4, z_lo: 2; z = z_hi * 2 + z_lo), core: 2. Of those that a mesh axis runs over, the one named last changes fastest.
Arguments:
- blocks_inverse: bfloat16 [12288, 12288], P('row', 'col'), as said below
- factor_rows: bfloat16 [2, 6144, 256], P(None, 'row'), may hold values from -0.15234375 to 0.15234375
- block_lists: int32 [2, 48], replicated, may hold values from 0 to 95, as said below
- diag_inverse: float32 [2, 256, 256], replicated, as said below
Outputs:
- column_inverse: float32 [2, 12288, 256], P(None, 'row')
- mirror_inverse: float32 [2, 256, 12288], P(None, None, 'col')
- diagonal_inverse: float32 [2, 256, 256], replicated
The draws below stay inside these ranges and needn't reach their ends.
Inputs may be any that keep to these rules, and one draw needn't show every extreme that they name: blocks_inverse is exactly symmetric and positive definite. block_lists[s, m] is 2 * m or 2 * m + 1. diag_inverse[s] is symmetric.
All inputs are finite; a program needn't handle non-finite values.
Results may differ from the reference program's by a relative error of at most 0.0003.
Values may be sent and summed in bfloat16 or wider, within the bound.
A program may use at most 64 MiB of HBM per device.

```python
import jax
import jax.numpy as jnp
from jax import lax

BS = 128
NBLK = 96
W = 256
NSUP = 2
LISTED = 48


def draw_blocks_inverse(key, part):
    order_rows = NBLK * BS
    key_one, key_two = jax.random.split(key)
    random_part = jax.random.normal(key_one, (order_rows, order_rows), jnp.float32)
    symmetric = (random_part + random_part.T) * (0.7 / (2.0 * order_rows) ** 0.5)
    diagonal = jax.random.uniform(key_two, (order_rows,), jnp.float32, 1.6, 3.2)
    positions = jnp.arange(order_rows)
    symmetric = symmetric.at[positions, positions].add(diagonal)
    return symmetric.astype(jnp.bfloat16)


def draw_block_lists(key, part):
    choose_bits = jax.random.randint(key, (NSUP, NBLK // 2), 0, 2, dtype=jnp.int32)
    return (2 * jnp.arange(NBLK // 2, dtype=jnp.int32)[None, :] + choose_bits).astype(jnp.int32)


def draw_diag_inverse(key, part):
    key_one, key_two = jax.random.split(key)
    random_part = jax.random.normal(key_one, (NSUP, W, W), jnp.float32)
    symmetric = (random_part + jnp.swapaxes(random_part, 1, 2)) * (0.1 / 2.0 ** 0.5)
    diagonal = jax.random.uniform(key_two, (NSUP, W), jnp.float32, 4.0, 8.0)
    return symmetric + diagonal[:, :, None] * jnp.eye(W, dtype=jnp.float32)[None, :, :]


def level_of(key, shape, pieces, low, largest):
    gain = 1.0
    for position, parts in pieces:
        draws = jax.random.uniform(jax.random.fold_in(jax.random.fold_in(key, 6), position), (parts,), jnp.float32, low / len(pieces), largest / len(pieces))
        gain = gain * jnp.repeat(jnp.exp(draws), shape[position] // parts).reshape((-1,) + (1,) * (len(shape) - 1 - position))
    return gain


def centred(stream_key, dims, width, most, cuts=(), held_as=jnp.bfloat16):
    result = jax.random.normal(stream_key, dims, jnp.float32) * width
    if len(cuts) > 0:
        result = level_of(stream_key, dims, cuts, -0.22, 0.18) * result
    return jnp.clip(result, min=-most, max=most).astype(held_as)


def setup_inputs(seed: int = 0) -> dict:
    key_list = jax.random.split(jax.random.key(seed), 5)
    blocks_inverse = draw_blocks_inverse(jax.random.fold_in(key_list[4], 71), 0)
    factor_rows = centred(key_list[1], (NSUP, LISTED * BS, W), (2.0 / (LISTED * BS) ** 0.5), 0.15234375, ((1, 16),))
    block_lists = draw_block_lists(jax.random.fold_in(key_list[4], 71), 0)
    diag_inverse = draw_diag_inverse(jax.random.fold_in(key_list[4], 71), 0)
    return {"blocks_inverse": blocks_inverse, "factor_rows": factor_rows, "block_lists": block_lists, "diag_inverse": diag_inverse}


def reference(blocks_inverse, factor_rows, block_lists, diag_inverse):
    order_rows = NBLK * BS
    pairs = NBLK // 2
    pair_first = 2 * jnp.arange(pairs, dtype=jnp.int32)
    column_list = []
    diagonal_list = []
    for sup_index in range(NSUP):
        bits = (block_lists[sup_index] - pair_first).astype(jnp.int32)
        grouped_rows = blocks_inverse.reshape(pairs, 2, BS, order_rows)
        picked_rows = jnp.where(bits[:, None, None] == 0, grouped_rows[:, 0], grouped_rows[:, 1]).reshape(pairs * BS, order_rows)
        grouped_cols = picked_rows.reshape(pairs * BS, pairs, 2, BS)
        inner_block = jnp.where(bits[None, :, None] == 0, grouped_cols[:, :, 0], grouped_cols[:, :, 1]).reshape(pairs * BS, pairs * BS)
        inverse_column = jnp.dot(inner_block.astype(jnp.float32), factor_rows[sup_index].astype(jnp.float32), precision=lax.Precision.HIGHEST)
        packed = inverse_column.reshape(pairs, 1, BS, W)
        which = bits[:, None, None, None] == jnp.arange(2, dtype=jnp.int32)[None, :, None, None]
        dense_column = -jnp.where(which, packed, jnp.zeros((), jnp.float32)).reshape(order_rows, W)
        column_list.append(dense_column)
        factor_wide = factor_rows[sup_index].astype(jnp.float32)
        diagonal_list.append(diag_inverse[sup_index] + jnp.dot(factor_wide.T, inverse_column, precision=lax.Precision.HIGHEST))
    column_inverse = jnp.stack(column_list)
    mirror_inverse = jnp.transpose(column_inverse, (0, 2, 1))
    return column_inverse, mirror_inverse, jnp.stack(diagonal_list)
```

```python
import jax
import jax.numpy as jnp
from jax import lax
from jax.experimental import pallas as pl
from jax.experimental.pallas import tpu as pltpu
from jax.sharding import PartitionSpec as P

BS = 128
W = 256
CHIPS = 8
PIECE = 48
MESH = pl.DeviceIdType.MESH
F32 = jnp.float32
BF16 = jnp.bfloat16


def dot_t(a, b):
    return lax.dot_general(a, b, (((0,), (0,)), ((), ())), preferred_element_type=F32)


def comm_kernel(
    lists, a_hbm, f_hbm, diag, pc, pr, dout,
    a_v, f_v, asel, fp, pp, pcv, prv, half, rs, dp, dr, d1, dy, dz, dg,
    ld_sem, fs_send, fs_recv, on_send, on_recv, rs_send, rs_recv,
    ag_send, ag_recv, rl_send, rl_recv, tp_send, tp_recv, zs_send, zs_recv,
    ys_send, ys_recv, dr_send, dr_recv, dy_send, dy_recv, dz_send, dz_recv,
    dh_send, dh_recv, dg_send, dg_recv, do_send, do_recv,
):
    r = lax.axis_index("row")
    c = lax.axis_index("col")
    k = lax.rem(r, 2)
    j = r // 2
    y = lax.rem(c, 4)
    zh = c // 4
    mate = r + 1 - 2 * k
    ck = lax.rem(c, 2)
    cj = c // 2

    def chip(d):
        return lax.rem(j + d, CHIPS)

    def rcopy(src, dst, ssem, rsem, row, col):
        return pltpu.make_async_remote_copy(
            src_ref=src, dst_ref=dst, send_sem=ssem, recv_sem=rsem,
            device_id=(row, col), device_id_type=MESH,
        )

    barrier = pltpu.get_barrier_semaphore()

    @pl.when(r != c)
    def _():
        pl.semaphore_signal(barrier, inc=1, device_id=(c, r), device_id_type=MESH)

    for d in range(1, 4):
        zo = lax.rem(zh + d, 4)
        yo = lax.rem(y + d, 4)
        pl.semaphore_signal(barrier, inc=1, device_id=(r, zo * 4 + y), device_id_type=MESH)
        pl.semaphore_signal(barrier, inc=1, device_id=(r, zh * 4 + yo), device_id_type=MESH)

    def greet(d, carry):
        pl.semaphore_signal(barrier, inc=1, device_id=(lax.rem(r + d, 16), c), device_id_type=MESH)
        return carry

    lax.fori_loop(1, 16, greet, 0)

    load_a = pltpu.make_async_copy(a_hbm, a_v, ld_sem.at[0])
    load_f = pltpu.make_async_copy(f_hbm, f_v, ld_sem.at[1])
    load_a.start()
    load_f.start()
    load_a.wait()
    load_f.wait()

    def partial(s):
        for p in range(3):
            rb = lists[s, r * 3 + p] - 2 * (r * 3 + p)
            picked = jnp.where(
                rb == 0, a_v[p * 256 : p * 256 + 128, :], a_v[p * 256 + 128 : p * 256 + 256, :]
            )
            for q in range(3):
                cb = lists[s, c * 3 + q] - 2 * (c * 3 + q)
                asel[p * 128 : p * 128 + 128, q * 128 : q * 128 + 128] = jnp.where(
                    cb == 0, picked[:, q * 256 : q * 256 + 128], picked[:, q * 256 + 128 : q * 256 + 256]
                )
        got = dot_t(asel[...], f_v[s])
        pp[s] = got.reshape(CHIPS, PIECE, W)

    partial(1 - k)

    pl.semaphore_wait(barrier, jnp.where(r == c, 21, 22))

    swap = rcopy(pp.at[1 - k], half, on_send, on_recv, mate, c)
    swap.start()

    def fcopy(o):
        return rcopy(
            f_hbm.at[lax.rem(o, 2), pl.ds(pl.multiple_of((o // 2) * PIECE, PIECE), PIECE)],
            fp, fs_send.at[o], fs_recv, o, c,
        )

    @pl.when(r == c)
    def _():
        def scatter(d, carry):
            fcopy(lax.rem(r + d, 16)).start()
            return carry

        lax.fori_loop(1, 16, scatter, 0)
        fp[...] = f_v[k, pl.ds(pl.multiple_of(j * PIECE, PIECE), PIECE), :]

    partial(k)
    swap.wait_recv()

    pp[k] = pp[k] + half[...]

    def rs_copy(d, slot):
        o = chip(d)
        return rcopy(pp.at[k, o], rs.at[slot], rs_send.at[o], rs_recv.at[slot], 2 * o + k, c)

    def rs_start(d, carry):
        rs_copy(d, j).start()
        return carry

    lax.fori_loop(1, CHIPS, rs_start, 0)
    total = pp[k, j]
    for d in range(1, CHIPS):
        o = chip(CHIPS - d)
        rs_copy(d, o).wait_recv()
        total = total + rs[o]
    pcv[k, j] = total

    mine = k * CHIPS + j
    here = ck * CHIPS + cj
    cross = rcopy(pcv.at[k, j], prv.at[mine], tp_send, tp_recv, c, r)

    @pl.when(r != c)
    def _():
        cross.start()

    @pl.when(r == c)
    def _():
        prv[mine] = total

    def ag_copy(d, slot):
        return rcopy(pcv.at[k, slot], pcv.at[k, slot], ag_send.at[chip(d)], ag_recv.at[slot], 2 * chip(d) + k, c)

    def ag_start(d, carry):
        ag_copy(d, j).start()
        return carry

    lax.fori_loop(1, CHIPS, ag_start, 0)

    @pl.when(r != c)
    def _():
        fcopy(r).wait_recv()

    high = total.astype(BF16)
    low = (total - high.astype(F32)).astype(BF16)
    factor = fp[...]
    dp[...] = (dot_t(factor, high) + dot_t(factor, low)).reshape(CHIPS, 32, W)

    def dr_copy(d, slot):
        o = chip(d)
        return rcopy(dp.at[o], dr.at[slot], dr_send.at[o], dr_recv.at[slot], 2 * o + k, c)

    def dr_start(d, carry):
        dr_copy(d, j).start()
        return carry

    lax.fori_loop(1, CHIPS, dr_start, 0)

    def rl_copy(s, slot):
        return rcopy(pcv.at[s, slot], pcv.at[s, slot], rl_send.at[slot], rl_recv.at[slot], mate, c)

    rl_copy(k, j).start()

    def relay(d, carry):
        o = chip(CHIPS - d)
        ag_copy(d, o).wait_recv()
        rl_copy(k, o).start()
        return carry

    lax.fori_loop(1, CHIPS, relay, 0)

    dsum = dp[j]
    for d in range(1, CHIPS):
        o = chip(CHIPS - d)
        dr_copy(d, o).wait_recv()
        dsum = dsum + dr[o]
    d1[...] = dsum.reshape(4, 8, W)

    def line_y(d):
        return zh * 4 + lax.rem(y + d, 4)

    def line_z(d):
        return lax.rem(zh + d, 4) * 4 + y

    def dy_copy(d, slot):
        o = lax.rem(y + d, 4)
        return rcopy(d1.at[o], dy.at[slot], dy_send.at[o], dy_recv.at[slot], r, line_y(d))

    for d in range(1, 4):
        dy_copy(d, y).start()

    @pl.when(r != c)
    def _():
        rcopy(pcv.at[k, j], prv.at[here], tp_send, tp_recv, c, r).wait_recv()

    def slot_of(col):
        return lax.rem(col, 2) * CHIPS + col // 2

    def zs_copy(d, col):
        slot = slot_of(col)
        return rcopy(prv.at[slot], prv.at[slot], zs_send.at[lax.rem(zh + d, 4)], zs_recv.at[col // 4], r, line_z(d))

    for d in range(1, 4):
        zs_copy(d, c).start()

    def ys_copy(d, z, col):
        slot = slot_of(col)
        return rcopy(
            prv.at[slot], prv.at[slot], ys_send.at[z, lax.rem(y + d, 4)], ys_recv.at[z, lax.rem(col, 4)], r, line_y(d)
        )

    for d in range(1, 4):
        ys_copy(d, zh, c).start()

    dsum = d1[y]
    for d in range(1, 4):
        o = lax.rem(y + 4 - d, 4)
        dy_copy(d, o).wait_recv()
        dsum = dsum + dy[o]
    dz[zh] = dsum

    def dz_copy(d, slot):
        return rcopy(dz.at[slot], dz.at[slot], dz_send.at[lax.rem(zh + d, 4)], dz_recv.at[slot], r, line_z(d))

    for d in range(1, 4):
        dz_copy(d, zh).start()

    for d in range(1, 4):
        o = lax.rem(zh + 4 - d, 4)
        zs_copy(d, o * 4 + y).wait_recv()
        for e in range(1, 4):
            ys_copy(e, o, o * 4 + y).start()

    for d in range(1, 4):
        dz_copy(d, lax.rem(zh + 4 - d, 4)).wait_recv()
    dg[k, j, y] = (dz[0] + dz[1]) + (dz[2] + dz[3])

    def dh_copy(d, slot):
        return rcopy(
            dg.at[k, j, slot], dg.at[k, j, slot], dh_send.at[lax.rem(y + d, 4)], dh_recv.at[slot], r, line_y(d)
        )

    for d in range(1, 4):
        dh_copy(d, y).start()
    for d in range(1, 4):
        dh_copy(d, lax.rem(y + 4 - d, 4)).wait_recv()

    def dg_copy(d, slot):
        return rcopy(dg.at[k, slot], dg.at[k, slot], dg_send.at[chip(d)], dg_recv.at[slot], 2 * chip(d) + k, c)

    def dg_start(d, carry):
        dg_copy(d, j).start()
        return carry

    lax.fori_loop(1, CHIPS, dg_start, 0)

    for d in range(8):
        rl_copy(1 - k, d).wait_recv()
    pc[...] = pcv[...]
    for z in range(4):
        for d in range(1, 4):
            ys_copy(d, z, z * 4 + lax.rem(y + 4 - d, 4)).wait_recv()
    pr[...] = prv[...]

    def dg_wait(d, carry):
        dg_copy(d, chip(CHIPS - d)).wait_recv()
        return carry

    lax.fori_loop(1, CHIPS, dg_wait, 0)
    last = rcopy(dg.at[k], dg.at[k], do_send, do_recv, mate, c)
    last.start()
    rcopy(dg.at[1 - k], dg.at[1 - k], do_send, do_recv, mate, c).wait_recv()
    dout[...] = diag[...] + dg[...].reshape(2, W, W)

    last.wait_send()
    swap.wait_send()

    @pl.when(r != c)
    def _():
        cross.wait_send()

    @pl.when(r == c)
    def _():
        def scattered(d, carry):
            fcopy(lax.rem(r + d, 16)).wait_send()
            return carry

        lax.fori_loop(1, 16, scattered, 0)

    def drain(d, carry):
        rs_copy(d, j).wait_send()
        ag_copy(d, j).wait_send()
        dr_copy(d, j).wait_send()
        dg_copy(d, j).wait_send()
        return carry

    lax.fori_loop(1, CHIPS, drain, 0)
    for d in range(CHIPS):
        rl_copy(k, d).wait_send()
    for d in range(1, 4):
        dy_copy(d, y).wait_send()
        dz_copy(d, zh).wait_send()
        dh_copy(d, y).wait_send()
        zs_copy(d, c).wait_send()
        for z in range(4):
            ys_copy(d, z, z * 4 + y).wait_send()


def exchange(blocks_inverse, factor_rows, block_lists, diag_inverse):
    dma = pltpu.SemaphoreType.DMA
    vmem = pl.BlockSpec(memory_space=pltpu.VMEM)
    return pl.pallas_call(
        comm_kernel,
        out_shape=(
            jax.ShapeDtypeStruct((2, CHIPS, PIECE, W), F32),
            jax.ShapeDtypeStruct((16, PIECE, W), F32),
            jax.ShapeDtypeStruct((2, W, W), F32),
        ),
        in_specs=[
            pl.BlockSpec(memory_space=pltpu.SMEM),
            pl.BlockSpec(memory_space=pl.ANY),
            pl.BlockSpec(memory_space=pl.ANY),
            vmem,
        ],
        out_specs=(vmem, vmem, vmem),
        scratch_shapes=[
            pltpu.VMEM((768, 768), BF16),
            pltpu.VMEM((2, 384, W), BF16),
            pltpu.VMEM((384, 384), BF16),
            pltpu.VMEM((PIECE, W), BF16),
            pltpu.VMEM((2, CHIPS, PIECE, W), F32),
            pltpu.VMEM((2, CHIPS, PIECE, W), F32),
            pltpu.VMEM((16, PIECE, W), F32),
            pltpu.VMEM((CHIPS, PIECE, W), F32),
            pltpu.VMEM((CHIPS, PIECE, W), F32),
            pltpu.VMEM((CHIPS, 32, W), F32),
            pltpu.VMEM((CHIPS, 32, W), F32),
            pltpu.VMEM((4, 8, W), F32),
            pltpu.VMEM((4, 8, W), F32),
            pltpu.VMEM((4, 8, W), F32),
            pltpu.VMEM((2, CHIPS, 4, 8, W), F32),
            dma((2,)), dma((16,)), dma, dma, dma, dma((8,)), dma((8,)),
            dma((8,)), dma((8,)), dma((8,)), dma((8,)), dma, dma, dma((4,)), dma((4,)),
            dma((4, 4)), dma((4, 4)), dma((8,)), dma((8,)), dma((4,)), dma((4,)), dma((4,)), dma((4,)),
            dma((4,)), dma((4,)), dma((8,)), dma((8,)), dma, dma,
        ],
        compiler_params=pltpu.CompilerParams(collective_id=0, has_side_effects=True),
        name="exchange",
    )(block_lists, blocks_inverse, factor_rows, diag_inverse)


def expand(packed, bits):
    grouped = packed.reshape(2, 3, 1, BS, W)
    which = bits[:, :, None, None, None] == jnp.arange(2, dtype=jnp.int32)[None, None, :, None, None]
    return jnp.where(which, -grouped, 0.0).reshape(2, 768, W)


def pair_bits(block_lists, index):
    mine = lax.dynamic_slice_in_dim(block_lists, index * 3, 3, 1)
    return mine - 2 * (index * 3 + jnp.arange(3, dtype=jnp.int32))[None, :]


def local(blocks_inverse, factor_rows, block_lists, diag_inverse):
    col_packed, row_packed, diagonal = exchange(blocks_inverse, factor_rows, block_lists, diag_inverse)
    column = expand(row_packed, pair_bits(block_lists, lax.axis_index("row")))
    mirror = jnp.transpose(expand(col_packed, pair_bits(block_lists, lax.axis_index("col"))), (0, 2, 1))
    return column, mirror, diagonal


def solution(mesh):
    return jax.shard_map(
        local,
        mesh=mesh,
        in_specs=(P("row", "col"), P(None, "row", None), P(), P()),
        out_specs=(P(None, "row", None), P(None, None, "col"), P()),
        check_vma=False,
    )
```

```python
import jax
import jax.numpy as jnp
from jax import lax
from jax.experimental import pallas as pl
from jax.experimental.pallas import tpu as pltpu
from jax.sharding import PartitionSpec as P

BS = 128
W = 256
CHIPS = 8
PIECE = 48
MESH = pl.DeviceIdType.MESH
F32 = jnp.float32
BF16 = jnp.bfloat16


def dot_t(a, b):
    return lax.dot_general(a, b, (((0,), (0,)), ((), ())), preferred_element_type=F32)


def comm_kernel(
    lists, a_hbm, f_hbm, pc, pr, dout,
    a_v, f_v, asel, fp, pp, pcv, prv, half, rs, dp, dr, dz, dg,
    ld_sem, fs_send, fs_recv, on_send, on_recv, rs_send, rs_recv,
    ag_send, ag_recv, rl_send, rl_recv, tp_send, tp_recv, zs_send, zs_recv,
    ys_send, ys_recv, dr_send, dr_recv, dz_send, dz_recv,
    dg_send, dg_recv, do_send, do_recv, out_sem,
):
    r = lax.axis_index("row")
    c = lax.axis_index("col")
    k = lax.rem(r, 2)
    j = r // 2
    y = lax.rem(c, 4)
    zh = c // 4
    x = lax.rem(j, 4)
    zl = j // 4
    z = zh * 2 + zl
    q = x * 4 + y
    mate = r + 1 - 2 * k
    ck = lax.rem(c, 2)
    cj = c // 2

    def chip(d):
        return lax.rem(j + d, CHIPS)

    def rcopy(src, dst, ssem, rsem, row, col):
        return pltpu.make_async_remote_copy(
            src_ref=src, dst_ref=dst, send_sem=ssem, recv_sem=rsem,
            device_id=(row, col), device_id_type=MESH,
        )

    barrier = pltpu.get_barrier_semaphore()

    @pl.when(r != c)
    def _():
        pl.semaphore_signal(barrier, inc=1, device_id=(c, r), device_id_type=MESH)

    def greet_z(d, carry):
        zo = lax.rem(zh + d // 2, 4)
        pl.semaphore_signal(
            barrier, inc=1, device_id=(lax.rem(d, 2) * 8 + lax.rem(r, 8), zo * 4 + y), device_id_type=MESH
        )
        return carry

    lax.fori_loop(2, 8, greet_z, 0)

    def greet_y(d, carry):
        yo = lax.rem(y + d // 4, 4)
        pl.semaphore_signal(
            barrier, inc=1, device_id=(zl * 8 + lax.rem(d, 4) * 2 + k, zh * 4 + yo), device_id_type=MESH
        )
        return carry

    lax.fori_loop(4, 16, greet_y, 0)

    def greet(d, carry):
        pl.semaphore_signal(barrier, inc=1, device_id=(lax.rem(r + d, 16), c), device_id_type=MESH)
        return carry

    lax.fori_loop(1, 16, greet, 0)

    load_a = pltpu.make_async_copy(a_hbm, a_v, ld_sem.at[0])
    load_f = pltpu.make_async_copy(f_hbm, f_v, ld_sem.at[1])
    load_a.start()
    load_f.start()
    load_a.wait()
    load_f.wait()

    def partial(s):
        for p in range(3):
            rb = lists[s, r * 3 + p] - 2 * (r * 3 + p)
            picked = jnp.where(
                rb == 0, a_v[p * 256 : p * 256 + 128, :], a_v[p * 256 + 128 : p * 256 + 256, :]
            )
            for q in range(3):
                cb = lists[s, c * 3 + q] - 2 * (c * 3 + q)
                asel[p * 128 : p * 128 + 128, q * 128 : q * 128 + 128] = jnp.where(
                    cb == 0, picked[:, q * 256 : q * 256 + 128], picked[:, q * 256 + 128 : q * 256 + 256]
                )
        got = dot_t(asel[...], f_v[s])
        pp[s] = got.reshape(CHIPS, PIECE, W)

    partial(1 - k)

    pl.semaphore_wait(barrier, jnp.where(r == c, 33, 34))

    swap = rcopy(pp.at[1 - k], half, on_send, on_recv, mate, c)
    swap.start()

    def fcopy(o):
        return rcopy(
            f_hbm.at[lax.rem(o, 2), pl.ds(pl.multiple_of((o // 2) * PIECE, PIECE), PIECE)],
            fp, fs_send.at[o], fs_recv, o, c,
        )

    @pl.when(r == c)
    def _():
        def scatter(d, carry):
            fcopy(lax.rem(r + d, 16)).start()
            return carry

        lax.fori_loop(1, 16, scatter, 0)
        fp[...] = f_v[k, pl.ds(pl.multiple_of(j * PIECE, PIECE), PIECE), :]

    partial(k)
    swap.wait_recv()

    pp[k] = pp[k] + half[...]

    def rs_copy(d, slot):
        o = chip(d)
        return rcopy(pp.at[k, o], rs.at[slot], rs_send.at[o], rs_recv.at[slot], 2 * o + k, c)

    def rs_start(d, carry):
        rs_copy(d, j).start()
        return carry

    lax.fori_loop(1, CHIPS, rs_start, 0)
    total = pp[k, j]
    for d in range(1, CHIPS):
        o = chip(CHIPS - d)
        rs_copy(d, o).wait_recv()
        total = total + rs[o]
    pcv[k, j] = total

    mine = k * CHIPS + j
    here = ck * CHIPS + cj
    cross = rcopy(pcv.at[k, j], prv.at[mine], tp_send, tp_recv, c, r)

    @pl.when(r != c)
    def _():
        cross.start()

    @pl.when(r == c)
    def _():
        prv[mine] = total

    def ag_copy(d, slot):
        return rcopy(pcv.at[k, slot], pcv.at[k, slot], ag_send.at[chip(d)], ag_recv.at[slot], 2 * chip(d) + k, c)

    def ag_start(d, carry):
        ag_copy(d, j).start()
        return carry

    lax.fori_loop(1, CHIPS, ag_start, 0)

    @pl.when(r != c)
    def _():
        fcopy(r).wait_recv()

    high = total.astype(BF16)
    low = (total - high.astype(F32)).astype(BF16)
    left = fp[:, :128]
    right = fp[:, 128:]
    top = dot_t(left, high) + dot_t(left, low)
    dp[0:128, :] = top[:, :128]
    dp[128:256, :] = top[:, 128:]
    dp[256:384, :] = dot_t(right, high[:, 128:]) + dot_t(right, low[:, 128:])

    def around(d):
        return lax.rem(q + d, 16)

    def rows24(o):
        return pl.ds(pl.multiple_of(o * 24, 8), 24)

    def dr_copy(d, slot):
        o = around(d)
        return rcopy(
            dp.at[rows24(o)], dr.at[slot], dr_send.at[o], dr_recv.at[slot],
            zl * 8 + (o // 4) * 2 + k, zh * 4 + lax.rem(o, 4),
        )

    def dr_start(d, carry):
        dr_copy(d, q).start()
        return carry

    lax.fori_loop(1, 16, dr_start, 0)

    def rl_copy(s, slot):
        return rcopy(pcv.at[s, slot], pcv.at[s, slot], rl_send.at[slot], rl_recv.at[slot], mate, c)

    rl_copy(k, j).start()

    def relay(d, carry):
        o = chip(CHIPS - d)
        ag_copy(d, o).wait_recv()
        rl_copy(k, o).start()
        return carry

    lax.fori_loop(1, CHIPS, relay, 0)

    def dr_add(d, acc):
        o = around(16 - d)
        dr_copy(d, o).wait_recv()
        return acc + dr[o]

    dz[z] = lax.fori_loop(1, 16, dr_add, dp[rows24(q), :])

    def dz_copy(d, slot):
        o = lax.rem(z + d, 8)
        return rcopy(
            dz.at[slot], dz.at[slot], dz_send.at[o], dz_recv.at[slot],
            lax.rem(o, 2) * 8 + lax.rem(r, 8), (o // 2) * 4 + y,
        )

    def dz_start(d, carry):
        dz_copy(d, z).start()
        return carry

    lax.fori_loop(1, 8, dz_start, 0)

    def line_y(d):
        return zh * 4 + lax.rem(y + d, 4)

    def line_z(d):
        return lax.rem(zh + d, 4) * 4 + y

    @pl.when(r != c)
    def _():
        rcopy(pcv.at[k, j], prv.at[here], tp_send, tp_recv, c, r).wait_recv()

    def slot_of(col):
        return lax.rem(col, 2) * CHIPS + col // 2

    def zs_copy(d, col):
        slot = slot_of(col)
        return rcopy(prv.at[slot], prv.at[slot], zs_send.at[lax.rem(zh + d, 4)], zs_recv.at[col // 4], r, line_z(d))

    for d in range(1, 4):
        zs_copy(d, c).start()

    def ys_copy(d, w, col):
        slot = slot_of(col)
        return rcopy(
            prv.at[slot], prv.at[slot], ys_send.at[w, lax.rem(y + d, 4)], ys_recv.at[w, lax.rem(col, 4)], r, line_y(d)
        )

    for d in range(1, 4):
        ys_copy(d, zh, c).start()

    for d in range(1, 4):
        o = lax.rem(zh + 4 - d, 4)
        zs_copy(d, o * 4 + y).wait_recv()
        for e in range(1, 4):
            ys_copy(e, o, o * 4 + y).start()

    def dz_wait(d, carry):
        dz_copy(d, lax.rem(z + 8 - d, 8)).wait_recv()
        return carry

    lax.fori_loop(1, 8, dz_wait, 0)
    dg[k, rows24(q), :] = ((dz[0] + dz[1]) + (dz[2] + dz[3])) + ((dz[4] + dz[5]) + (dz[6] + dz[7]))

    def dg_copy(d, slot):
        o = around(d)
        return rcopy(
            dg.at[k, rows24(slot)], dg.at[k, rows24(slot)], dg_send.at[o], dg_recv.at[slot],
            zl * 8 + (o // 4) * 2 + k, zh * 4 + lax.rem(o, 4),
        )

    def do_copy(s, slot):
        return rcopy(dg.at[s, rows24(slot)], dg.at[s, rows24(slot)], do_send.at[slot], do_recv.at[slot], mate, c)

    def dg_start(d, carry):
        dg_copy(d, q).start()
        return carry

    lax.fori_loop(1, 16, dg_start, 0)
    do_copy(k, q).start()

    for d in range(8):
        rl_copy(1 - k, d).wait_recv()
    out_pc = pltpu.make_async_copy(pcv, pc, out_sem.at[0])
    out_pc.start()
    for w in range(4):
        for d in range(1, 4):
            ys_copy(d, w, w * 4 + lax.rem(y + 4 - d, 4)).wait_recv()
    out_pr = pltpu.make_async_copy(prv, pr, out_sem.at[1])
    out_pr.start()

    def dg_relay(d, carry):
        o = around(16 - d)
        dg_copy(d, o).wait_recv()
        do_copy(k, o).start()
        return carry

    lax.fori_loop(1, 16, dg_relay, 0)

    def do_wait(d, carry):
        do_copy(1 - k, d).wait_recv()
        return carry

    lax.fori_loop(0, 16, do_wait, 0)
    out_d = pltpu.make_async_copy(dg, dout, out_sem.at[2])
    out_d.start()

    swap.wait_send()

    @pl.when(r != c)
    def _():
        cross.wait_send()

    @pl.when(r == c)
    def _():
        def scattered(d, carry):
            fcopy(lax.rem(r + d, 16)).wait_send()
            return carry

        lax.fori_loop(1, 16, scattered, 0)

    def drain(d, carry):
        rs_copy(d, j).wait_send()
        ag_copy(d, j).wait_send()
        dz_copy(d, z).wait_send()
        return carry

    lax.fori_loop(1, CHIPS, drain, 0)
    for d in range(CHIPS):
        rl_copy(k, d).wait_send()
    for d in range(1, 4):
        zs_copy(d, c).wait_send()
        for w in range(4):
            ys_copy(d, w, w * 4 + y).wait_send()

    def drain_plane(d, carry):
        dr_copy(d, q).wait_send()
        dg_copy(d, q).wait_send()
        return carry

    lax.fori_loop(1, 16, drain_plane, 0)

    def drain_relay(d, carry):
        do_copy(k, d).wait_send()
        return carry

    lax.fori_loop(0, 16, drain_relay, 0)
    out_pc.wait()
    out_pr.wait()
    out_d.wait()


def exchange(blocks_inverse, factor_rows, block_lists):
    dma = pltpu.SemaphoreType.DMA
    hbm = pl.BlockSpec(memory_space=pl.ANY)
    return pl.pallas_call(
        comm_kernel,
        out_shape=(
            jax.ShapeDtypeStruct((2, CHIPS, PIECE, W), F32),
            jax.ShapeDtypeStruct((16, PIECE, W), F32),
            jax.ShapeDtypeStruct((2, 384, 128), F32),
        ),
        in_specs=[pl.BlockSpec(memory_space=pltpu.SMEM), hbm, hbm],
        out_specs=(hbm, hbm, hbm),
        scratch_shapes=[
            pltpu.VMEM((768, 768), BF16),
            pltpu.VMEM((2, 384, W), BF16),
            pltpu.VMEM((384, 384), BF16),
            pltpu.VMEM((PIECE, W), BF16),
            pltpu.VMEM((2, CHIPS, PIECE, W), F32),
            pltpu.VMEM((2, CHIPS, PIECE, W), F32),
            pltpu.VMEM((16, PIECE, W), F32),
            pltpu.VMEM((CHIPS, PIECE, W), F32),
            pltpu.VMEM((CHIPS, PIECE, W), F32),
            pltpu.VMEM((384, 128), F32),
            pltpu.VMEM((16, 24, 128), F32),
            pltpu.VMEM((8, 24, 128), F32),
            pltpu.VMEM((2, 384, 128), F32),
            dma((2,)), dma((16,)), dma, dma, dma, dma((8,)), dma((8,)),
            dma((8,)), dma((8,)), dma((8,)), dma((8,)), dma, dma, dma((4,)), dma((4,)),
            dma((4, 4)), dma((4, 4)), dma((16,)), dma((16,)), dma((8,)), dma((8,)),
            dma((16,)), dma((16,)), dma((16,)), dma((16,)), dma((3,)),
        ],
        compiler_params=pltpu.CompilerParams(collective_id=0, has_side_effects=True),
        name="exchange",
    )(block_lists, blocks_inverse, factor_rows)


def expand_kernel(lists, pc, pr, dg, diag, column, mirror, diagonal, col_in, row_in, dg_in, diag_in, row_out, col_out, zero, d_out, in_sem, z_sem, o_sem):
    r = lax.axis_index("row")
    c = lax.axis_index("col")
    loads = [
        pltpu.make_async_copy(pr, row_in, in_sem.at[0]),
        pltpu.make_async_copy(pc, col_in, in_sem.at[1]),
        pltpu.make_async_copy(dg, dg_in, in_sem.at[2]),
        pltpu.make_async_copy(diag, diag_in, in_sem.at[3]),
    ]
    for load in loads:
        load.start()
    zero[...] = jnp.zeros_like(zero)
    stores = []

    def put(src, dst, sem):
        copy = pltpu.make_async_copy(src, dst, sem)
        copy.start()
        stores.append(copy)

    def span(block):
        return pl.ds(pl.multiple_of(block * BS, BS), BS)

    row_at = {}
    col_at = {}
    for s in range(2):
        for p in range(3):
            row_at[s, p] = lists[s, r * 3 + p] - 2 * (r * 3 + p)
            col_at[s, p] = lists[s, c * 3 + p] - 2 * (c * 3 + p)
            put(zero.at[0:128, :], column.at[s, span(2 * p + 1 - row_at[s, p])], z_sem.at[0, s, p])
            put(zero.at[:, 0:128], mirror.at[s, :, span(2 * p + 1 - col_at[s, p])], z_sem.at[1, s, p])
    loads[0].wait()
    for s in range(2):
        for p in range(3):
            row_out[s, p] = -row_in[s, p * BS : p * BS + BS, :]
            put(row_out.at[s, p], column.at[s, span(2 * p + row_at[s, p])], o_sem.at[0, s, p])
    loads[1].wait()
    for s in range(2):
        for p in range(3):
            col_out[s, p] = -jnp.transpose(col_in[s, p * BS : p * BS + BS, :])
            put(col_out.at[s, p], mirror.at[s, :, span(2 * p + col_at[s, p])], o_sem.at[1, s, p])
    loads[2].wait()
    loads[3].wait()
    for s in range(2):
        upper = dg_in[s, 128:256, :]
        d_out[s, 0:128, 0:128] = diag_in[s, 0:128, 0:128] + dg_in[s, 0:128, :]
        d_out[s, 0:128, 128:256] = diag_in[s, 0:128, 128:256] + upper
        d_out[s, 128:256, 0:128] = diag_in[s, 128:256, 0:128] + jnp.transpose(upper)
        d_out[s, 128:256, 128:256] = diag_in[s, 128:256, 128:256] + dg_in[s, 256:384, :]
    put(d_out, diagonal, in_sem.at[4])
    for store in stores:
        store.wait()


def expand(block_lists, col_packed, row_packed, upper, diag_inverse):
    dma = pltpu.SemaphoreType.DMA
    hbm = pl.BlockSpec(memory_space=pl.ANY)
    return pl.pallas_call(
        expand_kernel,
        out_shape=(
            jax.ShapeDtypeStruct((2, 768, W), F32),
            jax.ShapeDtypeStruct((2, W, 768), F32),
            jax.ShapeDtypeStruct((2, W, W), F32),
        ),
        in_specs=[pl.BlockSpec(memory_space=pltpu.SMEM)] + [hbm] * 4,
        out_specs=(hbm, hbm, hbm),
        scratch_shapes=[
            pltpu.VMEM((2, 384, W), F32),
            pltpu.VMEM((2, 384, W), F32),
            pltpu.VMEM((2, 384, 128), F32),
            pltpu.VMEM((2, W, W), F32),
            pltpu.VMEM((2, 3, BS, W), F32),
            pltpu.VMEM((2, 3, W, BS), F32),
            pltpu.VMEM((W, W), F32),
            pltpu.VMEM((2, W, W), F32),
            dma((5,)), dma((2, 2, 3)), dma((2, 2, 3)),
        ],
        name="expand",
    )(block_lists, col_packed, row_packed, upper, diag_inverse)


def local(blocks_inverse, factor_rows, block_lists, diag_inverse):
    col_packed, row_packed, upper = exchange(blocks_inverse, factor_rows, block_lists)
    return expand(
        block_lists, col_packed.reshape(2, 384, W), row_packed.reshape(2, 384, W), upper, diag_inverse
    )


def solution(mesh):
    return jax.shard_map(
        local,
        mesh=mesh,
        in_specs=(P("row", "col"), P(None, "row", None), P(), P()),
        out_specs=(P(None, "row", None), P(None, None, "col"), P()),
        check_vma=False,
    )
```

```python
import jax
import jax.numpy as jnp
from jax import lax
from jax.experimental import pallas as pl
from jax.experimental.pallas import tpu as pltpu
from jax.sharding import PartitionSpec as P

BS = 128
W = 256
CHIPS = 8
PIECE = 48
CODED = 112
TOP = 32000.0
MESH = pl.DeviceIdType.MESH
F32 = jnp.float32
BF16 = jnp.bfloat16


def dot_t(a, b):
    return lax.dot_general(a, b, (((0,), (0,)), ((), ())), preferred_element_type=F32)


def encode(piece):
    parts = []
    steps = []
    for half in range(2):
        part = piece[:, half * 128 : half * 128 + 128]
        most = jnp.max(jnp.abs(part), axis=0, keepdims=True)
        level = jnp.clip(jnp.ceil(8.0 * jnp.log2(jnp.maximum(most, 1e-30))), -800.0, 1000.0)
        factor = jnp.exp2(level * -0.125) * TOP
        parts.append(jnp.round(part * factor).astype(jnp.int32).astype(jnp.int16))
        steps.append(jnp.broadcast_to(level, (8, 128)))
    steps = jnp.concatenate(steps, axis=0).astype(jnp.int32).astype(jnp.int16)
    return jnp.concatenate(parts + [steps], axis=0)


def decode_half(coded, half):
    level = coded[96:112, :].astype(jnp.int32).astype(F32)[8 * half : 8 * half + 1, :]
    step = jnp.exp2(level * 0.125) * (-1.0 / TOP)
    return coded[PIECE * half : PIECE * half + PIECE, :].astype(jnp.int32).astype(F32) * step


def comm_kernel(
    lists, a_hbm, f_hbm, pc, pr, dout,
    a_v, f_v, asel, fp, pp, pcv, prv, half, rs, dp, dr, dz, dg, pcf, prf, pct,
    ld_sem, fs_send, fs_recv, on_send, on_recv, rs_send, rs_recv,
    ag_send, ag_recv, rl_send, rl_recv, tp_send, tp_recv, zs_send, zs_recv,
    ys_send, ys_recv, dr_send, dr_recv, dz_send, dz_recv,
    dg_send, dg_recv, do_send, do_recv, out_sem,
):
    r = lax.axis_index("row")
    c = lax.axis_index("col")
    k = lax.rem(r, 2)
    j = r // 2
    y = lax.rem(c, 4)
    zh = c // 4
    x = lax.rem(j, 4)
    zl = j // 4
    z = zh * 2 + zl
    q = x * 4 + y
    mate = r + 1 - 2 * k
    ck = lax.rem(c, 2)
    cj = c // 2

    def chip(d):
        return lax.rem(j + d, CHIPS)

    def rcopy(src, dst, ssem, rsem, row, col):
        return pltpu.make_async_remote_copy(
            src_ref=src, dst_ref=dst, send_sem=ssem, recv_sem=rsem,
            device_id=(row, col), device_id_type=MESH,
        )

    barrier = pltpu.get_barrier_semaphore()

    @pl.when(r != c)
    def _():
        pl.semaphore_signal(barrier, inc=1, device_id=(c, r), device_id_type=MESH)

    def greet_z(d, carry):
        zo = lax.rem(zh + d // 2, 4)
        pl.semaphore_signal(
            barrier, inc=1, device_id=(lax.rem(d, 2) * 8 + lax.rem(r, 8), zo * 4 + y), device_id_type=MESH
        )
        return carry

    lax.fori_loop(2, 8, greet_z, 0)

    def greet_y(d, carry):
        yo = lax.rem(y + d // 4, 4)
        pl.semaphore_signal(
            barrier, inc=1, device_id=(zl * 8 + lax.rem(d, 4) * 2 + k, zh * 4 + yo), device_id_type=MESH
        )
        return carry

    lax.fori_loop(4, 16, greet_y, 0)

    def greet(d, carry):
        pl.semaphore_signal(barrier, inc=1, device_id=(lax.rem(r + d, 16), c), device_id_type=MESH)
        return carry

    lax.fori_loop(1, 16, greet, 0)

    load_a = pltpu.make_async_copy(a_hbm, a_v, ld_sem.at[0])
    load_f = pltpu.make_async_copy(f_hbm, f_v, ld_sem.at[1])
    load_a.start()
    load_f.start()
    load_a.wait()
    load_f.wait()

    def partial(s):
        for p in range(3):
            rb = lists[s, r * 3 + p] - 2 * (r * 3 + p)
            picked = jnp.where(
                rb == 0, a_v[p * 256 : p * 256 + 128, :], a_v[p * 256 + 128 : p * 256 + 256, :]
            )
            for q in range(3):
                cb = lists[s, c * 3 + q] - 2 * (c * 3 + q)
                asel[p * 128 : p * 128 + 128, q * 128 : q * 128 + 128] = jnp.where(
                    cb == 0, picked[:, q * 256 : q * 256 + 128], picked[:, q * 256 + 128 : q * 256 + 256]
                )
        got = dot_t(asel[...], f_v[s])
        pp[s] = got.reshape(CHIPS, PIECE, W)

    partial(1 - k)

    pl.semaphore_wait(barrier, jnp.where(r == c, 33, 34))

    swap = rcopy(pp.at[1 - k], half, on_send, on_recv, mate, c)
    swap.start()

    def fcopy(o):
        return rcopy(
            f_hbm.at[lax.rem(o, 2), pl.ds(pl.multiple_of((o // 2) * PIECE, PIECE), PIECE)],
            fp, fs_send.at[o], fs_recv, o, c,
        )

    @pl.when(r == c)
    def _():
        def scatter(d, carry):
            fcopy(lax.rem(r + d, 16)).start()
            return carry

        lax.fori_loop(1, 16, scatter, 0)
        fp[...] = f_v[k, pl.ds(pl.multiple_of(j * PIECE, PIECE), PIECE), :]

    partial(k)
    swap.wait_recv()

    pp[k] = pp[k] + half[...]

    def rs_copy(d, slot):
        o = chip(d)
        return rcopy(pp.at[k, o], rs.at[slot], rs_send.at[o], rs_recv.at[slot], 2 * o + k, c)

    def rs_start(d, carry):
        rs_copy(d, j).start()
        return carry

    lax.fori_loop(1, CHIPS, rs_start, 0)
    total = pp[k, j]
    for d in range(1, CHIPS):
        o = chip(CHIPS - d)
        rs_copy(d, o).wait_recv()
        total = total + rs[o]
    @pl.when(r != c)
    def _():
        fcopy(r).wait_recv()

    high = total.astype(BF16)
    low = (total - high.astype(F32)).astype(BF16)
    left = fp[:, :128]
    right = fp[:, 128:]
    top = dot_t(left, high) + dot_t(left, low)
    dp[0:128, :] = top[:, :128]
    dp[128:256, :] = top[:, 128:]
    dp[256:384, :] = dot_t(right, high[:, 128:]) + dot_t(right, low[:, 128:])

    def around(d):
        return lax.rem(q + d, 16)

    def rows24(o):
        return pl.ds(pl.multiple_of(o * 24, 8), 24)

    def dr_copy(d, slot):
        o = around(d)
        return rcopy(
            dp.at[rows24(o)], dr.at[slot], dr_send.at[o], dr_recv.at[slot],
            zl * 8 + (o // 4) * 2 + k, zh * 4 + lax.rem(o, 4),
        )

    def dr_start(d, carry):
        dr_copy(d, q).start()
        return carry

    lax.fori_loop(1, 16, dr_start, 0)

    pcv[k, j] = encode(total)

    mine = k * CHIPS + j
    here = ck * CHIPS + cj
    cross = rcopy(pcv.at[k, j], prv.at[mine], tp_send, tp_recv, c, r)

    @pl.when(r != c)
    def _():
        cross.start()

    @pl.when(r == c)
    def _():
        prv[mine] = encode(total)

    def ag_copy(d, slot):
        return rcopy(pcv.at[k, slot], pcv.at[k, slot], ag_send.at[chip(d)], ag_recv.at[slot], 2 * chip(d) + k, c)

    def ag_start(d, carry):
        ag_copy(d, j).start()
        return carry

    lax.fori_loop(1, CHIPS, ag_start, 0)

    def rl_copy(s, slot):
        return rcopy(pcv.at[s, slot], pcv.at[s, slot], rl_send.at[slot], rl_recv.at[slot], mate, c)

    rl_copy(k, j).start()

    def relay(d, carry):
        o = chip(CHIPS - d)
        ag_copy(d, o).wait_recv()
        rl_copy(k, o).start()
        return carry

    lax.fori_loop(1, CHIPS, relay, 0)

    def dr_add(d, acc):
        o = around(16 - d)
        dr_copy(d, o).wait_recv()
        return acc + dr[o]

    dz[z] = lax.fori_loop(1, 16, dr_add, dp[rows24(q), :])

    def dz_copy(d, slot):
        o = lax.rem(z + d, 8)
        return rcopy(
            dz.at[slot], dz.at[slot], dz_send.at[o], dz_recv.at[slot],
            lax.rem(o, 2) * 8 + lax.rem(r, 8), (o // 2) * 4 + y,
        )

    def dz_start(d, carry):
        dz_copy(d, z).start()
        return carry

    lax.fori_loop(1, 8, dz_start, 0)

    def line_y(d):
        return zh * 4 + lax.rem(y + d, 4)

    def line_z(d):
        return lax.rem(zh + d, 4) * 4 + y

    @pl.when(r != c)
    def _():
        rcopy(pcv.at[k, j], prv.at[here], tp_send, tp_recv, c, r).wait_recv()

    def slot_of(col):
        return lax.rem(col, 2) * CHIPS + col // 2

    def zs_copy(d, col):
        slot = slot_of(col)
        return rcopy(prv.at[slot], prv.at[slot], zs_send.at[lax.rem(zh + d, 4)], zs_recv.at[col // 4], r, line_z(d))

    for d in range(1, 4):
        zs_copy(d, c).start()

    def ys_copy(d, w, col):
        slot = slot_of(col)
        return rcopy(
            prv.at[slot], prv.at[slot], ys_send.at[w, lax.rem(y + d, 4)], ys_recv.at[w, lax.rem(col, 4)], r, line_y(d)
        )

    for d in range(1, 4):
        ys_copy(d, zh, c).start()

    for d in range(1, 4):
        o = lax.rem(zh + 4 - d, 4)
        zs_copy(d, o * 4 + y).wait_recv()
        for e in range(1, 4):
            ys_copy(e, o, o * 4 + y).start()

    def dz_wait(d, carry):
        dz_copy(d, lax.rem(z + 8 - d, 8)).wait_recv()
        return carry

    lax.fori_loop(1, 8, dz_wait, 0)
    dg[k, rows24(q), :] = ((dz[0] + dz[1]) + (dz[2] + dz[3])) + ((dz[4] + dz[5]) + (dz[6] + dz[7]))

    def dg_copy(d, slot):
        o = around(d)
        return rcopy(
            dg.at[k, rows24(slot)], dg.at[k, rows24(slot)], dg_send.at[o], dg_recv.at[slot],
            zl * 8 + (o // 4) * 2 + k, zh * 4 + lax.rem(o, 4),
        )

    def do_copy(s, slot):
        return rcopy(dg.at[s, rows24(slot)], dg.at[s, rows24(slot)], do_send.at[slot], do_recv.at[slot], mate, c)

    def dg_start(d, carry):
        dg_copy(d, q).start()
        return carry

    lax.fori_loop(1, 16, dg_start, 0)
    do_copy(k, q).start()

    for d in range(8):
        rl_copy(1 - k, d).wait_recv()

    def open_pc(o, carry):
        rows = pl.ds(pl.multiple_of(lax.rem(o, 8) * PIECE, 8), PIECE)
        coded = pcv[o // 8, lax.rem(o, 8)]
        pcf[o // 8, rows, 0:128] = decode_half(coded, 0)
        pcf[o // 8, rows, 128:256] = decode_half(coded, 1)
        return carry

    lax.fori_loop(0, 16, open_pc, 0)
    for s in range(2):
        for p in range(3):
            pct[s, :, p * BS : p * BS + BS] = jnp.transpose(pcf[s, p * BS : p * BS + BS, :])
    out_pc = pltpu.make_async_copy(pct, pc, out_sem.at[0])
    out_pc.start()
    for w in range(4):
        for d in range(1, 4):
            ys_copy(d, w, w * 4 + lax.rem(y + 4 - d, 4)).wait_recv()

    def open_pr(o, carry):
        rows = pl.ds(pl.multiple_of(lax.rem(o, 8) * PIECE, 8), PIECE)
        coded = prv[o]
        prf[o // 8, rows, 0:128] = decode_half(coded, 0)
        prf[o // 8, rows, 128:256] = decode_half(coded, 1)
        return carry

    lax.fori_loop(0, 16, open_pr, 0)
    out_pr = pltpu.make_async_copy(prf, pr, out_sem.at[1])
    out_pr.start()

    def dg_relay(d, carry):
        o = around(16 - d)
        dg_copy(d, o).wait_recv()
        do_copy(k, o).start()
        return carry

    lax.fori_loop(1, 16, dg_relay, 0)

    def do_wait(d, carry):
        do_copy(1 - k, d).wait_recv()
        return carry

    lax.fori_loop(0, 16, do_wait, 0)
    out_d = pltpu.make_async_copy(dg, dout, out_sem.at[2])
    out_d.start()

    swap.wait_send()

    @pl.when(r != c)
    def _():
        cross.wait_send()

    @pl.when(r == c)
    def _():
        def scattered(d, carry):
            fcopy(lax.rem(r + d, 16)).wait_send()
            return carry

        lax.fori_loop(1, 16, scattered, 0)

    def drain(d, carry):
        rs_copy(d, j).wait_send()
        ag_copy(d, j).wait_send()
        dz_copy(d, z).wait_send()
        return carry

    lax.fori_loop(1, CHIPS, drain, 0)
    for d in range(CHIPS):
        rl_copy(k, d).wait_send()
    for d in range(1, 4):
        zs_copy(d, c).wait_send()
        for w in range(4):
            ys_copy(d, w, w * 4 + y).wait_send()

    def drain_plane(d, carry):
        dr_copy(d, q).wait_send()
        dg_copy(d, q).wait_send()
        return carry

    lax.fori_loop(1, 16, drain_plane, 0)

    def drain_relay(d, carry):
        do_copy(k, d).wait_send()
        return carry

    lax.fori_loop(0, 16, drain_relay, 0)
    out_pc.wait()
    out_pr.wait()
    out_d.wait()


def exchange(blocks_inverse, factor_rows, block_lists):
    dma = pltpu.SemaphoreType.DMA
    hbm = pl.BlockSpec(memory_space=pl.ANY)
    return pl.pallas_call(
        comm_kernel,
        out_shape=(
            jax.ShapeDtypeStruct((2, W, 384), F32),
            jax.ShapeDtypeStruct((2, 384, W), F32),
            jax.ShapeDtypeStruct((2, 384, 128), F32),
        ),
        in_specs=[pl.BlockSpec(memory_space=pltpu.SMEM), hbm, hbm],
        out_specs=(hbm, hbm, hbm),
        scratch_shapes=[
            pltpu.VMEM((768, 768), BF16),
            pltpu.VMEM((2, 384, W), BF16),
            pltpu.VMEM((384, 384), BF16),
            pltpu.VMEM((PIECE, W), BF16),
            pltpu.VMEM((2, CHIPS, PIECE, W), F32),
            pltpu.VMEM((2, CHIPS, CODED, 128), jnp.int16),
            pltpu.VMEM((16, CODED, 128), jnp.int16),
            pltpu.VMEM((CHIPS, PIECE, W), F32),
            pltpu.VMEM((CHIPS, PIECE, W), F32),
            pltpu.VMEM((384, 128), F32),
            pltpu.VMEM((16, 24, 128), F32),
            pltpu.VMEM((8, 24, 128), F32),
            pltpu.VMEM((2, 384, 128), F32),
            pltpu.VMEM((2, 384, W), F32),
            pltpu.VMEM((2, 384, W), F32),
            pltpu.VMEM((2, W, 384), F32),
            dma((2,)), dma((16,)), dma, dma, dma, dma((8,)), dma((8,)),
            dma((8,)), dma((8,)), dma((8,)), dma((8,)), dma, dma, dma((4,)), dma((4,)),
            dma((4, 4)), dma((4, 4)), dma((16,)), dma((16,)), dma((8,)), dma((8,)),
            dma((16,)), dma((16,)), dma((16,)), dma((16,)), dma((3,)),
        ],
        compiler_params=pltpu.CompilerParams(collective_id=0, has_side_effects=True),
        name="exchange",
    )(block_lists, blocks_inverse, factor_rows)


def expand_kernel(
    lists, pc, pr, dg, diag, column, mirror, diagonal, col_in, row_in, dg_in, diag_in, zero, d_out,
    r_sem, c_sem, d_sem, z_sem, o_sem,
):
    r = lax.axis_index("row")
    c = lax.axis_index("col")
    stores = []

    def begin(src, dst, sem):
        copy = pltpu.make_async_copy(src, dst, sem)
        copy.start()
        return copy

    def span(block):
        return pl.ds(pl.multiple_of(block * BS, BS), BS)

    loads_d = [begin(dg, dg_in, d_sem.at[0]), begin(diag, diag_in, d_sem.at[1])]
    loads = {}
    for s in range(2):
        for p in range(3):
            loads[0, s, p] = begin(pr.at[s, p * BS : p * BS + BS, :], row_in.at[s, p], r_sem.at[s, p])
            loads[1, s, p] = begin(pc.at[s, :, p * BS : p * BS + BS], col_in.at[s, p], c_sem.at[s, p])
    zero[...] = jnp.zeros_like(zero)
    row_at = {}
    col_at = {}
    for s in range(2):
        for p in range(3):
            row_at[s, p] = lists[s, r * 3 + p] - 2 * (r * 3 + p)
            col_at[s, p] = lists[s, c * 3 + p] - 2 * (c * 3 + p)
            stores.append(begin(zero.at[0:128, :], column.at[s, span(2 * p + 1 - row_at[s, p])], z_sem.at[0, s, p]))
            stores.append(begin(zero.at[:, 0:128], mirror.at[s, :, span(2 * p + 1 - col_at[s, p])], z_sem.at[1, s, p]))
    for load in loads_d:
        load.wait()
    for s in range(2):
        upper = dg_in[s, 128:256, :]
        d_out[s, 0:128, 0:128] = diag_in[s, 0:128, 0:128] + dg_in[s, 0:128, :]
        d_out[s, 0:128, 128:256] = diag_in[s, 0:128, 128:256] + upper
        d_out[s, 128:256, 0:128] = diag_in[s, 128:256, 0:128] + jnp.transpose(upper)
        d_out[s, 128:256, 128:256] = diag_in[s, 128:256, 128:256] + dg_in[s, 256:384, :]
    stores.append(begin(d_out, diagonal, d_sem.at[2]))
    for s in range(2):
        for p in range(3):
            loads[0, s, p].wait()
            stores.append(begin(row_in.at[s, p], column.at[s, span(2 * p + row_at[s, p])], o_sem.at[0, s, p]))
            loads[1, s, p].wait()
            stores.append(begin(col_in.at[s, p], mirror.at[s, :, span(2 * p + col_at[s, p])], o_sem.at[1, s, p]))
    for store in stores:
        store.wait()


def expand(block_lists, col_packed, row_packed, upper, diag_inverse):
    dma = pltpu.SemaphoreType.DMA
    hbm = pl.BlockSpec(memory_space=pl.ANY)
    return pl.pallas_call(
        expand_kernel,
        out_shape=(
            jax.ShapeDtypeStruct((2, 768, W), F32),
            jax.ShapeDtypeStruct((2, W, 768), F32),
            jax.ShapeDtypeStruct((2, W, W), F32),
        ),
        in_specs=[pl.BlockSpec(memory_space=pltpu.SMEM)] + [hbm] * 4,
        out_specs=(hbm, hbm, hbm),
        scratch_shapes=[
            pltpu.VMEM((2, 3, W, BS), F32),
            pltpu.VMEM((2, 3, BS, W), F32),
            pltpu.VMEM((2, 384, 128), F32),
            pltpu.VMEM((2, W, W), F32),
            pltpu.VMEM((W, W), F32),
            pltpu.VMEM((2, W, W), F32),
            dma((2, 3)), dma((2, 3)), dma((3,)), dma((2, 2, 3)), dma((2, 2, 3)),
        ],
        name="expand",
    )(block_lists, col_packed, row_packed, upper, diag_inverse)


def local(blocks_inverse, factor_rows, block_lists, diag_inverse):
    col_packed, row_packed, upper = exchange(blocks_inverse, factor_rows, block_lists)
    return expand(
        block_lists, col_packed, row_packed, upper, diag_inverse
    )


def solution(mesh):
    return jax.shard_map(
        local,
        mesh=mesh,
        in_specs=(P("row", "col"), P(None, "row", None), P(), P()),
        out_specs=(P(None, "row", None), P(None, None, "col"), P()),
        check_vma=False,
    )
```

```python
import jax
import jax.numpy as jnp
from jax import lax
from jax.experimental import pallas as pl
from jax.experimental.pallas import tpu as pltpu
from jax.sharding import PartitionSpec as P

BS = 128
W = 256
CHIPS = 8
PIECE = 48
CODED = 112
TOP = 32000.0
MESH = pl.DeviceIdType.MESH
F32 = jnp.float32
BF16 = jnp.bfloat16


def dot_t(a, b):
    return lax.dot_general(a, b, (((0,), (0,)), ((), ())), preferred_element_type=F32)


def encode(piece):
    parts = []
    steps = []
    for half in range(2):
        part = piece[:, half * 128 : half * 128 + 128]
        most = jnp.max(jnp.abs(part), axis=0, keepdims=True)
        level = jnp.clip(jnp.ceil(8.0 * jnp.log2(jnp.maximum(most, 1e-30))), -800.0, 1000.0)
        factor = jnp.exp2(level * -0.125) * TOP
        parts.append(jnp.round(part * factor).astype(jnp.int32).astype(jnp.int16))
        steps.append(jnp.broadcast_to(level, (8, 128)))
    steps = jnp.concatenate(steps, axis=0).astype(jnp.int32).astype(jnp.int16)
    return jnp.concatenate(parts + [steps], axis=0)


def decode_half(coded, half):
    level = coded[96:112, :].astype(jnp.int32).astype(F32)[8 * half : 8 * half + 1, :]
    step = jnp.exp2(level * 0.125) * (-1.0 / TOP)
    return coded[PIECE * half : PIECE * half + PIECE, :].astype(jnp.int32).astype(F32) * step


def comm_kernel(
    lists, a_hbm, f_hbm, pc, pr, dout,
    a_v, f_v, asel, fp, pp, pcv, prv, half, rs, dp, dr, dz, dg, pcf, prf, pct,
    ld_sem, fs_send, fs_recv, on_send, on_recv, rs_send, rs_recv,
    ag_send, ag_recv, rl_send, rl_recv, tp_send, tp_recv, zs_send, zs_recv,
    ys_send, ys_recv, dr_send, dr_recv, dz_send, dz_recv,
    dg_send, dg_recv, do_send, do_recv, out_sem, met_line, met_mate,
):
    r = lax.axis_index("row")
    c = lax.axis_index("col")
    k = lax.rem(r, 2)
    j = r // 2
    y = lax.rem(c, 4)
    zh = c // 4
    x = lax.rem(j, 4)
    zl = j // 4
    z = zh * 2 + zl
    q = x * 4 + y
    mate = r + 1 - 2 * k
    ck = lax.rem(c, 2)
    cj = c // 2

    def chip(d):
        return lax.rem(j + d, CHIPS)

    def rcopy(src, dst, ssem, rsem, row, col):
        return pltpu.make_async_remote_copy(
            src_ref=src, dst_ref=dst, send_sem=ssem, recv_sem=rsem,
            device_id=(row, col), device_id_type=MESH,
        )

    barrier = pltpu.get_barrier_semaphore()

    def line_y(d):
        return zh * 4 + lax.rem(y + d, 4)

    def line_z(d):
        return lax.rem(zh + d, 4) * 4 + y

    for d in range(1, 4):
        pl.semaphore_signal(barrier, inc=1, device_id=(r, line_z(d)), device_id_type=MESH)
        pl.semaphore_signal(barrier, inc=1, device_id=(r, line_y(d)), device_id_type=MESH)

    def greet(d, carry):
        pl.semaphore_signal(barrier, inc=1, device_id=(lax.rem(r + d, 16), c), device_id_type=MESH)
        return carry

    lax.fori_loop(1, 16, greet, 0)

    load_a = pltpu.make_async_copy(a_hbm, a_v, ld_sem.at[0])
    load_f = pltpu.make_async_copy(f_hbm, f_v, ld_sem.at[1])
    load_a.start()
    load_f.start()
    load_a.wait()
    load_f.wait()

    def partial(s):
        for p in range(3):
            rb = lists[s, r * 3 + p] - 2 * (r * 3 + p)
            picked = jnp.where(
                rb == 0, a_v[p * 256 : p * 256 + 128, :], a_v[p * 256 + 128 : p * 256 + 256, :]
            )
            for q in range(3):
                cb = lists[s, c * 3 + q] - 2 * (c * 3 + q)
                asel[p * 128 : p * 128 + 128, q * 128 : q * 128 + 128] = jnp.where(
                    cb == 0, picked[:, q * 256 : q * 256 + 128], picked[:, q * 256 + 128 : q * 256 + 256]
                )
        got = dot_t(asel[...], f_v[s])
        pp[s] = got.reshape(CHIPS, PIECE, W)

    partial(1 - k)

    pl.semaphore_wait(barrier, 21)

    for d in range(1, 4):
        pl.semaphore_signal(met_line, inc=1, device_id=(r, line_y(d)), device_id_type=MESH)

    swap = rcopy(pp.at[1 - k], half, on_send, on_recv, mate, c)
    swap.start()

    def fcopy(o):
        return rcopy(
            f_hbm.at[lax.rem(o, 2), pl.ds(pl.multiple_of((o // 2) * PIECE, PIECE), PIECE)],
            fp, fs_send.at[o], fs_recv, o, c,
        )

    @pl.when(r == c)
    def _():
        def scatter(d, carry):
            fcopy(lax.rem(r + d, 16)).start()
            return carry

        lax.fori_loop(1, 16, scatter, 0)
        fp[...] = f_v[k, pl.ds(pl.multiple_of(j * PIECE, PIECE), PIECE), :]

    partial(k)
    pl.semaphore_wait(met_line, 3)
    pl.semaphore_signal(met_mate, inc=1, device_id=(mate, c), device_id_type=MESH)
    swap.wait_recv()
    pl.semaphore_wait(met_mate, 1)

    pp[k] = pp[k] + half[...]

    def rs_copy(d, slot):
        o = chip(d)
        return rcopy(pp.at[k, o], rs.at[slot], rs_send.at[o], rs_recv.at[slot], 2 * o + k, c)

    def rs_start(d, carry):
        rs_copy(d, j).start()
        return carry

    lax.fori_loop(1, CHIPS, rs_start, 0)
    total = pp[k, j]
    for d in range(1, CHIPS):
        o = chip(CHIPS - d)
        rs_copy(d, o).wait_recv()
        total = total + rs[o]
    @pl.when(r != c)
    def _():
        fcopy(r).wait_recv()

    high = total.astype(BF16)
    low = (total - high.astype(F32)).astype(BF16)
    left = fp[:, :128]
    right = fp[:, 128:]
    top = dot_t(left, high) + dot_t(left, low)
    dp[0:128, :] = top[:, :128]
    dp[128:256, :] = top[:, 128:]
    dp[256:384, :] = dot_t(right, high[:, 128:]) + dot_t(right, low[:, 128:])

    def around(d):
        return lax.rem(q + d, 16)

    def rows24(o):
        return pl.ds(pl.multiple_of(o * 24, 8), 24)

    def dr_copy(d, slot):
        o = around(d)
        return rcopy(
            dp.at[rows24(o)], dr.at[slot], dr_send.at[o], dr_recv.at[slot],
            zl * 8 + (o // 4) * 2 + k, zh * 4 + lax.rem(o, 4),
        )

    def dr_start(d, carry):
        dr_copy(d, q).start()
        return carry

    lax.fori_loop(1, 16, dr_start, 0)

    pcv[k, j] = encode(total)

    mine = k * CHIPS + j
    here = ck * CHIPS + cj
    cross = rcopy(pcv.at[k, j], prv.at[mine], tp_send, tp_recv, c, r)

    @pl.when(r != c)
    def _():
        cross.start()

    @pl.when(r == c)
    def _():
        prv[mine] = encode(total)

    def ag_copy(d, slot):
        return rcopy(pcv.at[k, slot], pcv.at[k, slot], ag_send.at[chip(d)], ag_recv.at[slot], 2 * chip(d) + k, c)

    def ag_start(d, carry):
        ag_copy(d, j).start()
        return carry

    lax.fori_loop(1, CHIPS, ag_start, 0)

    def dr_add(d, acc):
        o = around(16 - d)
        dr_copy(d, o).wait_recv()
        return acc + dr[o]

    dz[z] = lax.fori_loop(1, 16, dr_add, dp[rows24(q), :])

    def dz_copy(d, slot):
        o = lax.rem(z + d, 8)
        return rcopy(
            dz.at[slot], dz.at[slot], dz_send.at[o], dz_recv.at[slot],
            lax.rem(o, 2) * 8 + lax.rem(r, 8), (o // 2) * 4 + y,
        )

    def dz_start(d, carry):
        dz_copy(d, z).start()
        return carry

    lax.fori_loop(1, 8, dz_start, 0)

    @pl.when(r != c)
    def _():
        rcopy(pcv.at[k, j], prv.at[here], tp_send, tp_recv, c, r).wait_recv()

    def slot_of(col):
        return lax.rem(col, 2) * CHIPS + col // 2

    def zs_copy(d, col):
        slot = slot_of(col)
        return rcopy(prv.at[slot], prv.at[slot], zs_send.at[lax.rem(zh + d, 4)], zs_recv.at[col // 4], r, line_z(d))

    for d in range(1, 4):
        zs_copy(d, c).start()

    def ys_copy(d, w, col):
        slot = slot_of(col)
        return rcopy(
            prv.at[slot], prv.at[slot], ys_send.at[w, lax.rem(y + d, 4)], ys_recv.at[w, lax.rem(col, 4)], r, line_y(d)
        )

    for d in range(1, 4):
        ys_copy(d, zh, c).start()

    def rl_copy(s, slot):
        return rcopy(pcv.at[s, slot], pcv.at[s, slot], rl_send.at[slot], rl_recv.at[slot], mate, c)

    rl_copy(k, j).start()

    def relay(d, carry):
        o = chip(CHIPS - d)
        ag_copy(d, o).wait_recv()
        rl_copy(k, o).start()
        return carry

    lax.fori_loop(1, CHIPS, relay, 0)

    def dz_wait(d, carry):
        dz_copy(d, lax.rem(z + 8 - d, 8)).wait_recv()
        return carry

    lax.fori_loop(1, 8, dz_wait, 0)
    dg[k, rows24(q), :] = ((dz[0] + dz[1]) + (dz[2] + dz[3])) + ((dz[4] + dz[5]) + (dz[6] + dz[7]))

    def dg_copy(d, slot):
        o = around(d)
        return rcopy(
            dg.at[k, rows24(slot)], dg.at[k, rows24(slot)], dg_send.at[o], dg_recv.at[slot],
            zl * 8 + (o // 4) * 2 + k, zh * 4 + lax.rem(o, 4),
        )

    def do_copy(s, slot):
        return rcopy(dg.at[s, rows24(slot)], dg.at[s, rows24(slot)], do_send.at[slot], do_recv.at[slot], mate, c)

    def dg_start(d, carry):
        dg_copy(d, q).start()
        return carry

    lax.fori_loop(1, 16, dg_start, 0)
    do_copy(k, q).start()

    for d in range(1, 4):
        o = lax.rem(zh + 4 - d, 4)
        zs_copy(d, o * 4 + y).wait_recv()
        for e in range(1, 4):
            ys_copy(e, o, o * 4 + y).start()

    for d in range(8):
        rl_copy(1 - k, d).wait_recv()

    def open_pc(o, carry):
        rows = pl.ds(pl.multiple_of(lax.rem(o, 8) * PIECE, 8), PIECE)
        coded = pcv[o // 8, lax.rem(o, 8)]
        pcf[o // 8, rows, 0:128] = decode_half(coded, 0)
        pcf[o // 8, rows, 128:256] = decode_half(coded, 1)
        return carry

    lax.fori_loop(0, 16, open_pc, 0)
    for s in range(2):
        for p in range(3):
            pct[s, p] = jnp.transpose(pcf[s, p * BS : p * BS + BS, :])
    out_pc = pltpu.make_async_copy(pct, pc, out_sem.at[0])
    out_pc.start()
    for w in range(4):
        for d in range(1, 4):
            ys_copy(d, w, w * 4 + lax.rem(y + 4 - d, 4)).wait_recv()

    def open_pr(o, carry):
        rows = pl.ds(pl.multiple_of(lax.rem(o, 8) * PIECE, 8), PIECE)
        coded = prv[o]
        prf[o // 8, rows, 0:128] = decode_half(coded, 0)
        prf[o // 8, rows, 128:256] = decode_half(coded, 1)
        return carry

    lax.fori_loop(0, 16, open_pr, 0)
    out_pr = pltpu.make_async_copy(prf, pr, out_sem.at[1])
    out_pr.start()

    def dg_relay(d, carry):
        o = around(16 - d)
        dg_copy(d, o).wait_recv()
        do_copy(k, o).start()
        return carry

    lax.fori_loop(1, 16, dg_relay, 0)

    def do_wait(d, carry):
        do_copy(1 - k, d).wait_recv()
        return carry

    lax.fori_loop(0, 16, do_wait, 0)
    out_d = pltpu.make_async_copy(dg, dout, out_sem.at[2])
    out_d.start()

    swap.wait_send()

    @pl.when(r != c)
    def _():
        cross.wait_send()

    @pl.when(r == c)
    def _():
        def scattered(d, carry):
            fcopy(lax.rem(r + d, 16)).wait_send()
            return carry

        lax.fori_loop(1, 16, scattered, 0)

    def drain(d, carry):
        rs_copy(d, j).wait_send()
        ag_copy(d, j).wait_send()
        dz_copy(d, z).wait_send()
        return carry

    lax.fori_loop(1, CHIPS, drain, 0)
    for d in range(CHIPS):
        rl_copy(k, d).wait_send()
    for d in range(1, 4):
        zs_copy(d, c).wait_send()
        for w in range(4):
            ys_copy(d, w, w * 4 + y).wait_send()

    def drain_plane(d, carry):
        dr_copy(d, q).wait_send()
        dg_copy(d, q).wait_send()
        return carry

    lax.fori_loop(1, 16, drain_plane, 0)

    def drain_relay(d, carry):
        do_copy(k, d).wait_send()
        return carry

    lax.fori_loop(0, 16, drain_relay, 0)
    out_pc.wait()
    out_pr.wait()
    out_d.wait()


def exchange(blocks_inverse, factor_rows, block_lists):
    dma = pltpu.SemaphoreType.DMA
    hbm = pl.BlockSpec(memory_space=pl.ANY)
    return pl.pallas_call(
        comm_kernel,
        out_shape=(
            jax.ShapeDtypeStruct((2, 3, W, BS), F32),
            jax.ShapeDtypeStruct((2, 384, W), F32),
            jax.ShapeDtypeStruct((2, 384, 128), F32),
        ),
        in_specs=[pl.BlockSpec(memory_space=pltpu.SMEM), hbm, hbm],
        out_specs=(hbm, hbm, hbm),
        scratch_shapes=[
            pltpu.VMEM((768, 768), BF16),
            pltpu.VMEM((2, 384, W), BF16),
            pltpu.VMEM((384, 384), BF16),
            pltpu.VMEM((PIECE, W), BF16),
            pltpu.VMEM((2, CHIPS, PIECE, W), F32),
            pltpu.VMEM((2, CHIPS, CODED, 128), jnp.int16),
            pltpu.VMEM((16, CODED, 128), jnp.int16),
            pltpu.VMEM((CHIPS, PIECE, W), F32),
            pltpu.VMEM((CHIPS, PIECE, W), F32),
            pltpu.VMEM((384, 128), F32),
            pltpu.VMEM((16, 24, 128), F32),
            pltpu.VMEM((8, 24, 128), F32),
            pltpu.VMEM((2, 384, 128), F32),
            pltpu.VMEM((2, 384, W), F32),
            pltpu.VMEM((2, 384, W), F32),
            pltpu.VMEM((2, 3, W, BS), F32),
            dma((2,)), dma((16,)), dma, dma, dma, dma((8,)), dma((8,)),
            dma((8,)), dma((8,)), dma((8,)), dma((8,)), dma, dma, dma((4,)), dma((4,)),
            dma((4, 4)), dma((4, 4)), dma((16,)), dma((16,)), dma((8,)), dma((8,)),
            dma((16,)), dma((16,)), dma((16,)), dma((16,)), dma((3,)),
            pltpu.SemaphoreType.REGULAR, pltpu.SemaphoreType.REGULAR,
        ],
        compiler_params=pltpu.CompilerParams(collective_id=0, has_side_effects=True),
        name="exchange",
    )(block_lists, blocks_inverse, factor_rows)


def expand_kernel(
    lists, pc, pr, dg, diag, column, mirror, diagonal, col_in, row_in, dg_in, diag_in, zero, d_out,
    r_sem, c_sem, d_sem, z_sem, o_sem,
):
    r = lax.axis_index("row")
    c = lax.axis_index("col")
    stores = []

    def begin(src, dst, sem):
        copy = pltpu.make_async_copy(src, dst, sem)
        copy.start()
        return copy

    def span(block):
        return pl.ds(pl.multiple_of(block * BS, BS), BS)

    loads_d = [begin(dg, dg_in, d_sem.at[0]), begin(diag, diag_in, d_sem.at[1])]
    loads = {}
    for s in range(2):
        for p in range(3):
            loads[0, s, p] = begin(pr.at[s, p * BS : p * BS + BS, :], row_in.at[s, p], r_sem.at[s, p])
            loads[1, s, p] = begin(pc.at[s, p], col_in.at[s, p], c_sem.at[s, p])
    zero[...] = jnp.zeros_like(zero)
    row_at = {}
    col_at = {}
    for s in range(2):
        for p in range(3):
            row_at[s, p] = lists[s, r * 3 + p] - 2 * (r * 3 + p)
            col_at[s, p] = lists[s, c * 3 + p] - 2 * (c * 3 + p)
            stores.append(begin(zero.at[0:128, :], column.at[s, span(2 * p + 1 - row_at[s, p])], z_sem.at[0, s, p]))
            stores.append(begin(zero.at[:, 0:128], mirror.at[s, :, span(2 * p + 1 - col_at[s, p])], z_sem.at[1, s, p]))
    for load in loads_d:
        load.wait()
    for s in range(2):
        upper = dg_in[s, 128:256, :]
        d_out[s, 0:128, 0:128] = diag_in[s, 0:128, 0:128] + dg_in[s, 0:128, :]
        d_out[s, 0:128, 128:256] = diag_in[s, 0:128, 128:256] + upper
        d_out[s, 128:256, 0:128] = diag_in[s, 128:256, 0:128] + jnp.transpose(upper)
        d_out[s, 128:256, 128:256] = diag_in[s, 128:256, 128:256] + dg_in[s, 256:384, :]
    stores.append(begin(d_out, diagonal, d_sem.at[2]))
    for s in range(2):
        for p in range(3):
            loads[0, s, p].wait()
            stores.append(begin(row_in.at[s, p], column.at[s, span(2 * p + row_at[s, p])], o_sem.at[0, s, p]))
            loads[1, s, p].wait()
            stores.append(begin(col_in.at[s, p], mirror.at[s, :, span(2 * p + col_at[s, p])], o_sem.at[1, s, p]))
    for store in stores:
        store.wait()


def expand(block_lists, col_packed, row_packed, upper, diag_inverse):
    dma = pltpu.SemaphoreType.DMA
    hbm = pl.BlockSpec(memory_space=pl.ANY)
    return pl.pallas_call(
        expand_kernel,
        out_shape=(
            jax.ShapeDtypeStruct((2, 768, W), F32),
            jax.ShapeDtypeStruct((2, W, 768), F32),
            jax.ShapeDtypeStruct((2, W, W), F32),
        ),
        in_specs=[pl.BlockSpec(memory_space=pltpu.SMEM)] + [hbm] * 4,
        out_specs=(hbm, hbm, hbm),
        scratch_shapes=[
            pltpu.VMEM((2, 3, W, BS), F32),
            pltpu.VMEM((2, 3, BS, W), F32),
            pltpu.VMEM((2, 384, 128), F32),
            pltpu.VMEM((2, W, W), F32),
            pltpu.VMEM((W, W), F32),
            pltpu.VMEM((2, W, W), F32),
            dma((2, 3)), dma((2, 3)), dma((3,)), dma((2, 2, 3)), dma((2, 2, 3)),
        ],
        name="expand",
    )(block_lists, col_packed, row_packed, upper, diag_inverse)


def local(blocks_inverse, factor_rows, block_lists, diag_inverse):
    col_packed, row_packed, upper = exchange(blocks_inverse, factor_rows, block_lists)
    return expand(
        block_lists, col_packed, row_packed, upper, diag_inverse
    )


def solution(mesh):
    return jax.shard_map(
        local,
        mesh=mesh,
        in_specs=(P("row", "col"), P(None, "row", None), P(), P()),
        out_specs=(P(None, "row", None), P(None, None, "col"), P()),
        check_vma=False,
    )
```

```python
import jax
import jax.numpy as jnp
from jax import lax
from jax.experimental import pallas as pl
from jax.experimental.pallas import tpu as pltpu
from jax.sharding import PartitionSpec as P

BS = 128
W = 256
CHIPS = 8
PIECE = 48
CODED = 112
TOP = 32000.0
MESH = pl.DeviceIdType.MESH
F32 = jnp.float32
BF16 = jnp.bfloat16


def dot_t(a, b):
    return lax.dot_general(a, b, (((0,), (0,)), ((), ())), preferred_element_type=F32)


def encode(piece):
    parts = []
    steps = []
    for half in range(2):
        part = piece[:, half * 128 : half * 128 + 128]
        most = jnp.max(jnp.abs(part), axis=0, keepdims=True)
        level = jnp.clip(jnp.ceil(8.0 * jnp.log2(jnp.maximum(most, 1e-30))), -800.0, 1000.0)
        factor = jnp.exp2(level * -0.125) * TOP
        parts.append(jnp.round(part * factor).astype(jnp.int32).astype(jnp.int16))
        steps.append(jnp.broadcast_to(level, (8, 128)))
    steps = jnp.concatenate(steps, axis=0).astype(jnp.int32).astype(jnp.int16)
    return jnp.concatenate(parts + [steps], axis=0)


def decode_half(coded, half):
    level = coded[96:112, :].astype(jnp.int32).astype(F32)[8 * half : 8 * half + 1, :]
    step = jnp.exp2(level * 0.125) * (-1.0 / TOP)
    return coded[PIECE * half : PIECE * half + PIECE, :].astype(jnp.int32).astype(F32) * step


def encode_rows(part):
    most = jnp.max(jnp.abs(part), axis=-2, keepdims=True)
    level = jnp.clip(jnp.ceil(8.0 * jnp.log2(jnp.maximum(most, 1e-30))), -800.0, 1000.0)
    coded = jnp.round(part * (jnp.exp2(level * -0.125) * TOP)).astype(jnp.int32)
    steps = jnp.broadcast_to(level, part.shape[:-2] + (8, 128)).astype(jnp.int32)
    return jnp.concatenate([coded, steps], axis=-2).astype(jnp.int16)


def decode_rows(coded):
    wide = coded.astype(jnp.int32).astype(F32)
    return wide[:24, :] * (jnp.exp2(wide[24:25, :] * 0.125) * (1.0 / TOP))


def comm_kernel(
    lists_hbm, a_hbm, f_hbm, pc, pr, dout, lists,
    a_v, f_v, asel, fp, pp, pcv, prv, half, rs, dp, dpc, dr, dz, dg, dgf, pcf, prf, pct,
    ld_sem, fs_send, fs_recv, on_send, on_recv, rs_send, rs_recv,
    ag_send, ag_recv, rl_send, rl_recv, tp_send, tp_recv,
    ys_send, ys_recv, dr_send, dr_recv, dz_send, dz_recv,
    dg_send, dg_recv, do_send, do_recv, out_sem, met_line, met_mate,
):
    r = lax.axis_index("row")
    c = lax.axis_index("col")
    k = lax.rem(r, 2)
    j = r // 2
    y = lax.rem(c, 4)
    zh = c // 4
    x = lax.rem(j, 4)
    zl = j // 4
    z = zh * 2 + zl
    q = x * 4 + y
    mate = r + 1 - 2 * k
    ck = lax.rem(c, 2)
    cj = c // 2

    def chip(d):
        return lax.rem(j + d, CHIPS)

    def rcopy(src, dst, ssem, rsem, row, col):
        return pltpu.make_async_remote_copy(
            src_ref=src, dst_ref=dst, send_sem=ssem, recv_sem=rsem,
            device_id=(row, col), device_id_type=MESH,
        )

    barrier = pltpu.get_barrier_semaphore()

    def line_y(d):
        return zh * 4 + lax.rem(y + d, 4)

    def line_z(d):
        return lax.rem(zh + d, 4) * 4 + y

    for d in range(1, 4):
        pl.semaphore_signal(barrier, inc=1, device_id=(r, line_z(d)), device_id_type=MESH)
        pl.semaphore_signal(barrier, inc=1, device_id=(r, line_y(d)), device_id_type=MESH)

    def greet(d, carry):
        pl.semaphore_signal(barrier, inc=1, device_id=(lax.rem(r + d, 16), c), device_id_type=MESH)
        return carry

    lax.fori_loop(1, 16, greet, 0)

    load_l = pltpu.make_async_copy(lists_hbm, lists, ld_sem.at[2])
    load_l.start()
    load_a = pltpu.make_async_copy(a_hbm, a_v, ld_sem.at[0])
    load_f = pltpu.make_async_copy(f_hbm, f_v, ld_sem.at[1])
    load_a.start()
    load_f.start()
    load_l.wait()
    load_a.wait()
    load_f.wait()

    def partial(s):
        for p in range(3):
            rb = lists[s, r * 3 + p] - 2 * (r * 3 + p)
            picked = jnp.where(
                rb == 0, a_v[p * 256 : p * 256 + 128, :], a_v[p * 256 + 128 : p * 256 + 256, :]
            )
            for q in range(3):
                cb = lists[s, c * 3 + q] - 2 * (c * 3 + q)
                asel[p * 128 : p * 128 + 128, q * 128 : q * 128 + 128] = jnp.where(
                    cb == 0, picked[:, q * 256 : q * 256 + 128], picked[:, q * 256 + 128 : q * 256 + 256]
                )
        got = dot_t(asel[...], f_v[s])
        pp[s] = got.reshape(CHIPS, PIECE, W)

    partial(1 - k)

    pl.semaphore_wait(barrier, 21)

    for d in range(1, 4):
        pl.semaphore_signal(met_line, inc=1, device_id=(r, line_y(d)), device_id_type=MESH)

    swap = rcopy(pp.at[1 - k], half, on_send, on_recv, mate, c)
    swap.start()

    def fcopy(o):
        return rcopy(
            f_hbm.at[lax.rem(o, 2), pl.ds(pl.multiple_of((o // 2) * PIECE, PIECE), PIECE)],
            fp, fs_send.at[o], fs_recv, o, c,
        )

    @pl.when(r == c)
    def _():
        def scatter(d, carry):
            fcopy(lax.rem(r + d, 16)).start()
            return carry

        lax.fori_loop(1, 16, scatter, 0)
        fp[...] = f_v[k, pl.ds(pl.multiple_of(j * PIECE, PIECE), PIECE), :]

    partial(k)
    pl.semaphore_wait(met_line, 3)
    pl.semaphore_signal(met_mate, inc=1, device_id=(mate, c), device_id_type=MESH)
    swap.wait_recv()
    pl.semaphore_wait(met_mate, 1)

    pp[k] = pp[k] + half[...]

    def rs_copy(d, slot):
        o = chip(d)
        return rcopy(pp.at[k, o], rs.at[slot], rs_send.at[o], rs_recv.at[slot], 2 * o + k, c)

    def rs_start(d, carry):
        rs_copy(d, j).start()
        return carry

    lax.fori_loop(1, CHIPS, rs_start, 0)
    total = pp[k, j]
    for d in range(1, CHIPS):
        o = chip(CHIPS - d)
        rs_copy(d, o).wait_recv()
        total = total + rs[o]
    @pl.when(r != c)
    def _():
        fcopy(r).wait_recv()

    high = total.astype(BF16)
    low = (total - high.astype(F32)).astype(BF16)
    left = fp[:, :128]
    right = fp[:, 128:]
    top = dot_t(left, high) + dot_t(left, low)
    dp[0:128, :] = top[:, :128]
    dp[128:256, :] = top[:, 128:]
    dp[256:384, :] = dot_t(right, high[:, 128:]) + dot_t(right, low[:, 128:])

    dpc[...] = encode_rows(dp[...].reshape(16, 24, 128))

    def around(d):
        return lax.rem(q + d, 16)

    def rows24(o):
        return pl.ds(pl.multiple_of(o * 24, 8), 24)

    def dr_copy(d, slot):
        o = around(d)
        return rcopy(
            dpc.at[o], dr.at[slot], dr_send.at[o], dr_recv.at[slot],
            zl * 8 + (o // 4) * 2 + k, zh * 4 + lax.rem(o, 4),
        )

    def dr_start(d, carry):
        dr_copy(d, q).start()
        return carry

    lax.fori_loop(1, 16, dr_start, 0)

    pcv[k, j] = encode(total)

    mine = k * CHIPS + j

    def cross_copy(w):
        return rcopy(pcv.at[k, j], prv.at[mine], tp_send.at[w], tp_recv.at[mine], c, w * 4 + lax.rem(r, 4))

    def is_self(w):
        return jnp.logical_and(r == c, w * 4 + lax.rem(r, 4) == c)

    for w in range(4):

        @pl.when(jnp.logical_not(is_self(w)))
        def _():
            cross_copy(w).start()

        @pl.when(is_self(w))
        def _():
            prv[mine] = pcv[k, j]

    def dr_add(d, acc):
        o = around(16 - d)
        dr_copy(d, o).wait_recv()
        return acc + decode_rows(dr[o])

    dz[z] = encode_rows(lax.fori_loop(1, 16, dr_add, dp[rows24(q), :]))

    def dz_copy(d, slot):
        o = lax.rem(z + d, 8)
        return rcopy(
            dz.at[slot], dz.at[slot], dz_send.at[o], dz_recv.at[slot],
            lax.rem(o, 2) * 8 + lax.rem(r, 8), (o // 2) * 4 + y,
        )

    def dz_start(d, carry):
        dz_copy(d, z).start()
        return carry

    lax.fori_loop(1, 8, dz_start, 0)

    def ag_copy(d, slot):
        return rcopy(pcv.at[k, slot], pcv.at[k, slot], ag_send.at[chip(d)], ag_recv.at[slot], 2 * chip(d) + k, c)

    def ag_start(d, carry):
        ag_copy(d, j).start()
        return carry

    lax.fori_loop(1, CHIPS, ag_start, 0)

    def slot_of(col):
        return lax.rem(col, 2) * CHIPS + col // 2

    def ys_copy(d, w, col):
        slot = slot_of(col)
        return rcopy(
            prv.at[slot], prv.at[slot], ys_send.at[w, lax.rem(y + d, 4)], ys_recv.at[w, lax.rem(col, 4)], r, line_y(d)
        )

    for w in range(4):
        slot = slot_of(w * 4 + y)

        @pl.when(jnp.logical_not(jnp.logical_and(r == c, w == zh)))
        def _():
            rcopy(pcv.at[k, j], prv.at[slot], tp_send.at[w], tp_recv.at[slot], c, c).wait_recv()

        for d in range(1, 4):
            ys_copy(d, w, w * 4 + y).start()

    def rl_copy(s, slot):
        return rcopy(pcv.at[s, slot], pcv.at[s, slot], rl_send.at[slot], rl_recv.at[slot], mate, c)

    rl_copy(k, j).start()

    def relay(d, carry):
        o = chip(CHIPS - d)
        ag_copy(d, o).wait_recv()
        rl_copy(k, o).start()
        return carry

    lax.fori_loop(1, CHIPS, relay, 0)

    def dz_wait(d, carry):
        dz_copy(d, lax.rem(z + 8 - d, 8)).wait_recv()
        return carry

    lax.fori_loop(1, 8, dz_wait, 0)
    both = [decode_rows(dz[2 * i]) + decode_rows(dz[2 * i + 1]) for i in range(4)]
    dg[k, q] = encode_rows((both[0] + both[1]) + (both[2] + both[3]))

    def dg_copy(d, slot):
        o = around(d)
        return rcopy(
            dg.at[k, slot], dg.at[k, slot], dg_send.at[o], dg_recv.at[slot],
            zl * 8 + (o // 4) * 2 + k, zh * 4 + lax.rem(o, 4),
        )

    def do_copy(s, slot):
        return rcopy(dg.at[s, slot], dg.at[s, slot], do_send.at[slot], do_recv.at[slot], mate, c)

    def dg_start(d, carry):
        dg_copy(d, q).start()
        return carry

    lax.fori_loop(1, 16, dg_start, 0)
    do_copy(k, q).start()

    for d in range(8):
        rl_copy(1 - k, d).wait_recv()

    def open_pc(o, carry):
        rows = pl.ds(pl.multiple_of(lax.rem(o, 8) * PIECE, 8), PIECE)
        coded = pcv[o // 8, lax.rem(o, 8)]
        pcf[o // 8, rows, 0:128] = decode_half(coded, 0)
        pcf[o // 8, rows, 128:256] = decode_half(coded, 1)
        return carry

    lax.fori_loop(0, 16, open_pc, 0)
    for s in range(2):
        for p in range(3):
            pct[s, p] = jnp.transpose(pcf[s, p * BS : p * BS + BS, :])
    out_pc = pltpu.make_async_copy(pct, pc, out_sem.at[0])
    out_pc.start()
    for w in range(4):
        for d in range(1, 4):
            ys_copy(d, w, w * 4 + lax.rem(y + 4 - d, 4)).wait_recv()

    def open_pr(o, carry):
        rows = pl.ds(pl.multiple_of(lax.rem(o, 8) * PIECE, 8), PIECE)
        coded = prv[o]
        prf[o // 8, rows, 0:128] = decode_half(coded, 0)
        prf[o // 8, rows, 128:256] = decode_half(coded, 1)
        return carry

    lax.fori_loop(0, 16, open_pr, 0)
    out_pr = pltpu.make_async_copy(prf, pr, out_sem.at[1])
    out_pr.start()

    def dg_relay(d, carry):
        o = around(16 - d)
        dg_copy(d, o).wait_recv()
        do_copy(k, o).start()
        dgf[k, rows24(o), :] = decode_rows(dg[k, o])
        return carry

    dgf[k, rows24(q), :] = decode_rows(dg[k, q])
    lax.fori_loop(1, 16, dg_relay, 0)

    def do_wait(d, carry):
        do_copy(1 - k, d).wait_recv()
        dgf[1 - k, rows24(d), :] = decode_rows(dg[1 - k, d])
        return carry

    lax.fori_loop(0, 16, do_wait, 0)
    out_d = pltpu.make_async_copy(dgf, dout, out_sem.at[2])
    out_d.start()

    swap.wait_send()

    for w in range(4):

        @pl.when(jnp.logical_not(is_self(w)))
        def _():
            cross_copy(w).wait_send()

    @pl.when(r == c)
    def _():
        def scattered(d, carry):
            fcopy(lax.rem(r + d, 16)).wait_send()
            return carry

        lax.fori_loop(1, 16, scattered, 0)

    def drain(d, carry):
        rs_copy(d, j).wait_send()
        ag_copy(d, j).wait_send()
        dz_copy(d, z).wait_send()
        return carry

    lax.fori_loop(1, CHIPS, drain, 0)
    for d in range(CHIPS):
        rl_copy(k, d).wait_send()
    for d in range(1, 4):
        for w in range(4):
            ys_copy(d, w, w * 4 + y).wait_send()

    def drain_plane(d, carry):
        dr_copy(d, q).wait_send()
        dg_copy(d, q).wait_send()
        return carry

    lax.fori_loop(1, 16, drain_plane, 0)

    def drain_relay(d, carry):
        do_copy(k, d).wait_send()
        return carry

    lax.fori_loop(0, 16, drain_relay, 0)
    out_pc.wait()
    out_pr.wait()
    out_d.wait()


def exchange(blocks_inverse, factor_rows, block_lists):
    dma = pltpu.SemaphoreType.DMA
    hbm = pl.BlockSpec(memory_space=pl.ANY)
    return pl.pallas_call(
        comm_kernel,
        out_shape=(
            jax.ShapeDtypeStruct((2, 3, W, BS), F32),
            jax.ShapeDtypeStruct((2, 384, W), F32),
            jax.ShapeDtypeStruct((2, 384, 128), F32),
        ),
        in_specs=[hbm, hbm, hbm],
        out_specs=(hbm, hbm, hbm),
        scratch_shapes=[
            pltpu.SMEM((2, 48), jnp.int32),
            pltpu.VMEM((768, 768), BF16),
            pltpu.VMEM((2, 384, W), BF16),
            pltpu.VMEM((384, 384), BF16),
            pltpu.VMEM((PIECE, W), BF16),
            pltpu.VMEM((2, CHIPS, PIECE, W), F32),
            pltpu.VMEM((2, CHIPS, CODED, 128), jnp.int16),
            pltpu.VMEM((16, CODED, 128), jnp.int16),
            pltpu.VMEM((CHIPS, PIECE, W), F32),
            pltpu.VMEM((CHIPS, PIECE, W), F32),
            pltpu.VMEM((384, 128), F32),
            pltpu.VMEM((16, 32, 128), jnp.int16),
            pltpu.VMEM((16, 32, 128), jnp.int16),
            pltpu.VMEM((8, 32, 128), jnp.int16),
            pltpu.VMEM((2, 16, 32, 128), jnp.int16),
            pltpu.VMEM((2, 384, 128), F32),
            pltpu.VMEM((2, 384, W), F32),
            pltpu.VMEM((2, 384, W), F32),
            pltpu.VMEM((2, 3, W, BS), F32),
            dma((3,)), dma((16,)), dma, dma, dma, dma((8,)), dma((8,)),
            dma((8,)), dma((8,)), dma((8,)), dma((8,)), dma((4,)), dma((16,)),
            dma((4, 4)), dma((4, 4)), dma((16,)), dma((16,)), dma((8,)), dma((8,)),
            dma((16,)), dma((16,)), dma((16,)), dma((16,)), dma((3,)),
            pltpu.SemaphoreType.REGULAR, pltpu.SemaphoreType.REGULAR,
        ],
        compiler_params=pltpu.CompilerParams(collective_id=0, has_side_effects=True),
        name="exchange",
    )(block_lists, blocks_inverse, factor_rows)


def expand_kernel(
    lists_hbm, pc, pr, dg, diag, column, mirror, diagonal, lists, col_in, row_in, dg_in, diag_in, zero, d_out,
    r_sem, c_sem, d_sem, z_sem, o_sem,
):
    r = lax.axis_index("row")
    c = lax.axis_index("col")
    stores = []

    def begin(src, dst, sem):
        copy = pltpu.make_async_copy(src, dst, sem)
        copy.start()
        return copy

    def span(block):
        return pl.ds(pl.multiple_of(block * BS, BS), BS)

    load_l = begin(lists_hbm, lists, d_sem.at[3])
    loads_d = [begin(dg, dg_in, d_sem.at[0]), begin(diag, diag_in, d_sem.at[1])]
    loads = {}
    for s in range(2):
        for p in range(3):
            loads[0, s, p] = begin(pr.at[s, p * BS : p * BS + BS, :], row_in.at[s, p], r_sem.at[s, p])
            loads[1, s, p] = begin(pc.at[s, p], col_in.at[s, p], c_sem.at[s, p])
    zero[...] = jnp.zeros_like(zero)
    load_l.wait()
    row_at = {}
    col_at = {}
    for s in range(2):
        for p in range(3):
            row_at[s, p] = lists[s, r * 3 + p] - 2 * (r * 3 + p)
            col_at[s, p] = lists[s, c * 3 + p] - 2 * (c * 3 + p)
            stores.append(begin(zero.at[0:128, :], column.at[s, span(2 * p + 1 - row_at[s, p])], z_sem.at[0, s, p]))
            stores.append(begin(zero.at[:, 0:128], mirror.at[s, :, span(2 * p + 1 - col_at[s, p])], z_sem.at[1, s, p]))
    for load in loads_d:
        load.wait()
    for s in range(2):
        upper = dg_in[s, 128:256, :]
        d_out[s, 0:128, 0:128] = diag_in[s, 0:128, 0:128] + dg_in[s, 0:128, :]
        d_out[s, 0:128, 128:256] = diag_in[s, 0:128, 128:256] + upper
        d_out[s, 128:256, 0:128] = diag_in[s, 128:256, 0:128] + jnp.transpose(upper)
        d_out[s, 128:256, 128:256] = diag_in[s, 128:256, 128:256] + dg_in[s, 256:384, :]
    stores.append(begin(d_out, diagonal, d_sem.at[2]))
    for s in range(2):
        for p in range(3):
            loads[0, s, p].wait()
            stores.append(begin(row_in.at[s, p], column.at[s, span(2 * p + row_at[s, p])], o_sem.at[0, s, p]))
            loads[1, s, p].wait()
            stores.append(begin(col_in.at[s, p], mirror.at[s, :, span(2 * p + col_at[s, p])], o_sem.at[1, s, p]))
    for store in stores:
        store.wait()


def expand(block_lists, col_packed, row_packed, upper, diag_inverse):
    dma = pltpu.SemaphoreType.DMA
    hbm = pl.BlockSpec(memory_space=pl.ANY)
    return pl.pallas_call(
        expand_kernel,
        out_shape=(
            jax.ShapeDtypeStruct((2, 768, W), F32),
            jax.ShapeDtypeStruct((2, W, 768), F32),
            jax.ShapeDtypeStruct((2, W, W), F32),
        ),
        in_specs=[hbm] * 5,
        out_specs=(hbm, hbm, hbm),
        scratch_shapes=[
            pltpu.SMEM((2, 48), jnp.int32),
            pltpu.VMEM((2, 3, W, BS), F32),
            pltpu.VMEM((2, 3, BS, W), F32),
            pltpu.VMEM((2, 384, 128), F32),
            pltpu.VMEM((2, W, W), F32),
            pltpu.VMEM((W, W), F32),
            pltpu.VMEM((2, W, W), F32),
            dma((2, 3)), dma((2, 3)), dma((4,)), dma((2, 2, 3)), dma((2, 2, 3)),
        ],
        name="expand",
    )(block_lists, col_packed, row_packed, upper, diag_inverse)


def local(blocks_inverse, factor_rows, block_lists, diag_inverse):
    col_packed, row_packed, upper = exchange(blocks_inverse, factor_rows, block_lists)
    return expand(
        block_lists, col_packed, row_packed, upper, diag_inverse
    )


def solution(mesh):
    return jax.shard_map(
        local,
        mesh=mesh,
        in_specs=(P("row", "col"), P(None, "row", None), P(), P()),
        out_specs=(P(None, "row", None), P(None, None, "col"), P()),
        check_vma=False,
    )
```

```python
import jax
import jax.numpy as jnp
from jax import lax
from jax.experimental import pallas as pl
from jax.experimental.pallas import tpu as pltpu
from jax.sharding import PartitionSpec as P

BS = 128
W = 256
CHIPS = 8
PIECE = 48
CODED = 112
TOP = 32000.0
MESH = pl.DeviceIdType.MESH
F32 = jnp.float32
BF16 = jnp.bfloat16


def dot_t(a, b):
    return lax.dot_general(a, b, (((0,), (0,)), ((), ())), preferred_element_type=F32)


def encode(piece):
    parts = []
    steps = []
    for half in range(2):
        part = piece[:, half * 128 : half * 128 + 128]
        most = jnp.max(jnp.abs(part), axis=0, keepdims=True)
        level = jnp.clip(jnp.ceil(8.0 * jnp.log2(jnp.maximum(most, 1e-30))), -800.0, 1000.0)
        factor = jnp.exp2(level * -0.125) * TOP
        parts.append(jnp.round(part * factor).astype(jnp.int32).astype(jnp.int16))
        steps.append(jnp.broadcast_to(level, (8, 128)))
    steps = jnp.concatenate(steps, axis=0).astype(jnp.int32).astype(jnp.int16)
    return jnp.concatenate(parts + [steps], axis=0)


def decode_half(coded, half):
    level = coded[96:112, :].astype(jnp.int32).astype(F32)[8 * half : 8 * half + 1, :]
    step = jnp.exp2(level * 0.125) * (-1.0 / TOP)
    return coded[PIECE * half : PIECE * half + PIECE, :].astype(jnp.int32).astype(F32) * step


def encode_rows(part):
    most = jnp.max(jnp.abs(part), axis=-2, keepdims=True)
    level = jnp.clip(jnp.ceil(8.0 * jnp.log2(jnp.maximum(most, 1e-30))), -800.0, 1000.0)
    coded = jnp.round(part * (jnp.exp2(level * -0.125) * TOP)).astype(jnp.int32)
    steps = jnp.broadcast_to(level, part.shape[:-2] + (8, 128)).astype(jnp.int32)
    return jnp.concatenate([coded, steps], axis=-2).astype(jnp.int16)


def decode_rows(coded):
    wide = coded.astype(jnp.int32).astype(F32)
    return wide[:24, :] * (jnp.exp2(wide[24:25, :] * 0.125) * (1.0 / TOP))


def comm_kernel(
    lists_hbm, a_hbm, f_hbm, diag_hbm, column, mirror, diagonal, lists, diag,
    a_v, f_v, asel, fp, pp, pcv, prv, half, rs, dp, dpc, dr, dz, dg, dgf, pcf, prf,
    ld_sem, fs_send, fs_recv, on_send, on_recv, rs_send, rs_recv,
    ag_send, ag_recv, rl_send, rl_recv, tp_send, tp_recv,
    ys_send, ys_recv, dr_send, dr_recv, dz_send, dz_recv,
    dg_send, dg_recv, do_send, do_recv, met_line, met_mate,
):
    r = lax.axis_index("row")
    c = lax.axis_index("col")
    k = lax.rem(r, 2)
    j = r // 2
    y = lax.rem(c, 4)
    zh = c // 4
    x = lax.rem(j, 4)
    zl = j // 4
    z = zh * 2 + zl
    q = x * 4 + y
    mate = r + 1 - 2 * k
    ck = lax.rem(c, 2)
    cj = c // 2

    def chip(d):
        return lax.rem(j + d, CHIPS)

    def rcopy(src, dst, ssem, rsem, row, col):
        return pltpu.make_async_remote_copy(
            src_ref=src, dst_ref=dst, send_sem=ssem, recv_sem=rsem,
            device_id=(row, col), device_id_type=MESH,
        )

    barrier = pltpu.get_barrier_semaphore()

    def line_y(d):
        return zh * 4 + lax.rem(y + d, 4)

    def line_z(d):
        return lax.rem(zh + d, 4) * 4 + y

    for d in range(1, 4):
        pl.semaphore_signal(barrier, inc=1, device_id=(r, line_z(d)), device_id_type=MESH)
        pl.semaphore_signal(barrier, inc=1, device_id=(r, line_y(d)), device_id_type=MESH)

    def greet(d, carry):
        pl.semaphore_signal(barrier, inc=1, device_id=(lax.rem(r + d, 16), c), device_id_type=MESH)
        return carry

    lax.fori_loop(1, 16, greet, 0)

    load_l = pltpu.make_async_copy(lists_hbm, lists, ld_sem.at[2])
    load_l.start()
    load_d = pltpu.make_async_copy(diag_hbm, diag, ld_sem.at[3])
    load_d.start()
    load_a = pltpu.make_async_copy(a_hbm, a_v, ld_sem.at[0])
    load_f = pltpu.make_async_copy(f_hbm, f_v, ld_sem.at[1])
    load_a.start()
    load_f.start()
    load_l.wait()
    load_a.wait()
    load_f.wait()

    def partial(s):
        for p in range(3):
            rb = lists[s, r * 3 + p] - 2 * (r * 3 + p)
            picked = jnp.where(
                rb == 0, a_v[p * 256 : p * 256 + 128, :], a_v[p * 256 + 128 : p * 256 + 256, :]
            )
            for q in range(3):
                cb = lists[s, c * 3 + q] - 2 * (c * 3 + q)
                asel[p * 128 : p * 128 + 128, q * 128 : q * 128 + 128] = jnp.where(
                    cb == 0, picked[:, q * 256 : q * 256 + 128], picked[:, q * 256 + 128 : q * 256 + 256]
                )
        got = dot_t(asel[...], f_v[s])
        pp[s] = got.reshape(CHIPS, PIECE, W)

    partial(1 - k)

    pl.semaphore_wait(barrier, 21)

    for d in range(1, 4):
        pl.semaphore_signal(met_line, inc=1, device_id=(r, line_y(d)), device_id_type=MESH)

    swap = rcopy(pp.at[1 - k], half, on_send, on_recv, mate, c)
    swap.start()

    def fcopy(o):
        return rcopy(
            f_hbm.at[lax.rem(o, 2), pl.ds(pl.multiple_of((o // 2) * PIECE, PIECE), PIECE)],
            fp, fs_send.at[o], fs_recv, o, c,
        )

    @pl.when(r == c)
    def _():
        def scatter(d, carry):
            fcopy(lax.rem(r + d, 16)).start()
            return carry

        lax.fori_loop(1, 16, scatter, 0)
        fp[...] = f_v[k, pl.ds(pl.multiple_of(j * PIECE, PIECE), PIECE), :]

    partial(k)
    pl.semaphore_wait(met_line, 3)
    pl.semaphore_signal(met_mate, inc=1, device_id=(mate, c), device_id_type=MESH)
    swap.wait_recv()
    pl.semaphore_wait(met_mate, 1)

    pp[k] = pp[k] + half[...]

    def rs_copy(d, slot):
        o = chip(d)
        return rcopy(pp.at[k, o], rs.at[slot], rs_send.at[o], rs_recv.at[slot], 2 * o + k, c)

    def rs_start(d, carry):
        rs_copy(d, j).start()
        return carry

    lax.fori_loop(1, CHIPS, rs_start, 0)
    total = pp[k, j]
    for d in range(1, CHIPS):
        o = chip(CHIPS - d)
        rs_copy(d, o).wait_recv()
        total = total + rs[o]
    @pl.when(r != c)
    def _():
        fcopy(r).wait_recv()

    high = total.astype(BF16)
    low = (total - high.astype(F32)).astype(BF16)
    left = fp[:, :128]
    right = fp[:, 128:]
    top = dot_t(left, high) + dot_t(left, low)
    dp[0:128, :] = top[:, :128]
    dp[128:256, :] = top[:, 128:]
    dp[256:384, :] = dot_t(right, high[:, 128:]) + dot_t(right, low[:, 128:])

    dpc[...] = encode_rows(dp[...].reshape(16, 24, 128))

    def around(d):
        return lax.rem(q + d, 16)

    def rows24(o):
        return pl.ds(pl.multiple_of(o * 24, 8), 24)

    def dr_copy(d, slot):
        o = around(d)
        return rcopy(
            dpc.at[o], dr.at[slot], dr_send.at[o], dr_recv.at[slot],
            zl * 8 + (o // 4) * 2 + k, zh * 4 + lax.rem(o, 4),
        )

    def dr_start(d, carry):
        dr_copy(d, q).start()
        return carry

    lax.fori_loop(1, 16, dr_start, 0)

    pcv[k, j] = encode(total)

    mine = k * CHIPS + j

    def cross_copy(w):
        return rcopy(pcv.at[k, j], prv.at[mine], tp_send.at[w], tp_recv.at[mine], c, w * 4 + lax.rem(r, 4))

    def is_self(w):
        return jnp.logical_and(r == c, w * 4 + lax.rem(r, 4) == c)

    for w in range(4):

        @pl.when(jnp.logical_not(is_self(w)))
        def _():
            cross_copy(w).start()

        @pl.when(is_self(w))
        def _():
            prv[mine] = pcv[k, j]

    def dr_add(d, acc):
        o = around(16 - d)
        dr_copy(d, o).wait_recv()
        return acc + decode_rows(dr[o])

    dz[z] = encode_rows(lax.fori_loop(1, 16, dr_add, dp[rows24(q), :]))

    def dz_copy(d, slot):
        o = lax.rem(z + d, 8)
        return rcopy(
            dz.at[slot], dz.at[slot], dz_send.at[o], dz_recv.at[slot],
            lax.rem(o, 2) * 8 + lax.rem(r, 8), (o // 2) * 4 + y,
        )

    def dz_start(d, carry):
        dz_copy(d, z).start()
        return carry

    lax.fori_loop(1, 8, dz_start, 0)

    def ag_copy(d, slot):
        return rcopy(pcv.at[k, slot], pcv.at[k, slot], ag_send.at[chip(d)], ag_recv.at[slot], 2 * chip(d) + k, c)

    def ag_start(d, carry):
        ag_copy(d, j).start()
        return carry

    lax.fori_loop(1, CHIPS, ag_start, 0)

    def slot_of(col):
        return lax.rem(col, 2) * CHIPS + col // 2

    def ys_copy(d, w, col):
        slot = slot_of(col)
        return rcopy(
            prv.at[slot], prv.at[slot], ys_send.at[w, lax.rem(y + d, 4)], ys_recv.at[w, lax.rem(col, 4)], r, line_y(d)
        )

    for w in range(4):
        slot = slot_of(w * 4 + y)

        @pl.when(jnp.logical_not(jnp.logical_and(r == c, w == zh)))
        def _():
            rcopy(pcv.at[k, j], prv.at[slot], tp_send.at[w], tp_recv.at[slot], c, c).wait_recv()

        for d in range(1, 4):
            ys_copy(d, w, w * 4 + y).start()

    def rl_copy(s, slot):
        return rcopy(pcv.at[s, slot], pcv.at[s, slot], rl_send.at[slot], rl_recv.at[slot], mate, c)

    rl_copy(k, j).start()

    def relay(d, carry):
        o = chip(CHIPS - d)
        ag_copy(d, o).wait_recv()
        rl_copy(k, o).start()
        return carry

    lax.fori_loop(1, CHIPS, relay, 0)

    def dz_wait(d, carry):
        dz_copy(d, lax.rem(z + 8 - d, 8)).wait_recv()
        return carry

    lax.fori_loop(1, 8, dz_wait, 0)
    both = [decode_rows(dz[2 * i]) + decode_rows(dz[2 * i + 1]) for i in range(4)]
    dg[k, q] = encode_rows((both[0] + both[1]) + (both[2] + both[3]))

    def dg_copy(d, slot):
        o = around(d)
        return rcopy(
            dg.at[k, slot], dg.at[k, slot], dg_send.at[o], dg_recv.at[slot],
            zl * 8 + (o // 4) * 2 + k, zh * 4 + lax.rem(o, 4),
        )

    def do_copy(s, slot):
        return rcopy(dg.at[s, slot], dg.at[s, slot], do_send.at[slot], do_recv.at[slot], mate, c)

    def dg_start(d, carry):
        dg_copy(d, q).start()
        return carry

    lax.fori_loop(1, 16, dg_start, 0)
    do_copy(k, q).start()

    for d in range(8):
        rl_copy(1 - k, d).wait_recv()

    def open_pc(o, carry):
        rows = pl.ds(pl.multiple_of(lax.rem(o, 8) * PIECE, 8), PIECE)
        coded = pcv[o // 8, lax.rem(o, 8)]
        pcf[o // 8, rows, 0:128] = decode_half(coded, 0)
        pcf[o // 8, rows, 128:256] = decode_half(coded, 1)
        return carry

    lax.fori_loop(0, 16, open_pc, 0)
    for s in range(2):
        for p in range(3):
            at = lists[s, c * 3 + p] - 2 * (c * 3 + p)
            block = jnp.transpose(pcf[s, p * BS : p * BS + BS, :])
            mirror[s, :, 2 * p * BS : 2 * p * BS + BS] = jnp.where(at == 0, block, 0.0)
            mirror[s, :, 2 * p * BS + BS : 2 * p * BS + 2 * BS] = jnp.where(at == 0, 0.0, block)
    for w in range(4):
        for d in range(1, 4):
            ys_copy(d, w, w * 4 + lax.rem(y + 4 - d, 4)).wait_recv()

    def open_pr(o, carry):
        rows = pl.ds(pl.multiple_of(lax.rem(o, 8) * PIECE, 8), PIECE)
        coded = prv[o]
        prf[o // 8, rows, 0:128] = decode_half(coded, 0)
        prf[o // 8, rows, 128:256] = decode_half(coded, 1)
        return carry

    lax.fori_loop(0, 16, open_pr, 0)
    for s in range(2):
        for p in range(3):
            at = lists[s, r * 3 + p] - 2 * (r * 3 + p)
            block = prf[s, p * BS : p * BS + BS, :]
            column[s, 2 * p * BS : 2 * p * BS + BS, :] = jnp.where(at == 0, block, 0.0)
            column[s, 2 * p * BS + BS : 2 * p * BS + 2 * BS, :] = jnp.where(at == 0, 0.0, block)
    load_d.wait()

    def dg_relay(d, carry):
        o = around(16 - d)
        dg_copy(d, o).wait_recv()
        do_copy(k, o).start()
        dgf[k, rows24(o), :] = decode_rows(dg[k, o])
        return carry

    dgf[k, rows24(q), :] = decode_rows(dg[k, q])
    lax.fori_loop(1, 16, dg_relay, 0)

    def do_wait(d, carry):
        do_copy(1 - k, d).wait_recv()
        dgf[1 - k, rows24(d), :] = decode_rows(dg[1 - k, d])
        return carry

    lax.fori_loop(0, 16, do_wait, 0)
    for s in range(2):
        upper = dgf[s, 128:256, :]
        diagonal[s, 0:128, 0:128] = diag[s, 0:128, 0:128] + dgf[s, 0:128, :]
        diagonal[s, 0:128, 128:256] = diag[s, 0:128, 128:256] + upper
        diagonal[s, 128:256, 0:128] = diag[s, 128:256, 0:128] + jnp.transpose(upper)
        diagonal[s, 128:256, 128:256] = diag[s, 128:256, 128:256] + dgf[s, 256:384, :]

    swap.wait_send()

    for w in range(4):

        @pl.when(jnp.logical_not(is_self(w)))
        def _():
            cross_copy(w).wait_send()

    @pl.when(r == c)
    def _():
        def scattered(d, carry):
            fcopy(lax.rem(r + d, 16)).wait_send()
            return carry

        lax.fori_loop(1, 16, scattered, 0)

    def drain(d, carry):
        rs_copy(d, j).wait_send()
        ag_copy(d, j).wait_send()
        dz_copy(d, z).wait_send()
        return carry

    lax.fori_loop(1, CHIPS, drain, 0)
    for d in range(CHIPS):
        rl_copy(k, d).wait_send()
    for d in range(1, 4):
        for w in range(4):
            ys_copy(d, w, w * 4 + y).wait_send()

    def drain_plane(d, carry):
        dr_copy(d, q).wait_send()
        dg_copy(d, q).wait_send()
        return carry

    lax.fori_loop(1, 16, drain_plane, 0)

    def drain_relay(d, carry):
        do_copy(k, d).wait_send()
        return carry

    lax.fori_loop(0, 16, drain_relay, 0)


def exchange(blocks_inverse, factor_rows, block_lists, diag_inverse):
    dma = pltpu.SemaphoreType.DMA
    hbm = pl.BlockSpec(memory_space=pl.ANY)
    vmem = pl.BlockSpec(memory_space=pltpu.VMEM)
    return pl.pallas_call(
        comm_kernel,
        out_shape=(pltpu.VMEM((2, 768, W), F32), pltpu.VMEM((2, W, 768), F32), pltpu.VMEM((2, W, W), F32)),
        in_specs=[hbm] * 4,
        out_specs=(vmem, vmem, vmem),
        scratch_shapes=[
            pltpu.SMEM((2, 48), jnp.int32),
            pltpu.VMEM((2, W, W), F32),
            pltpu.VMEM((768, 768), BF16),
            pltpu.VMEM((2, 384, W), BF16),
            pltpu.VMEM((384, 384), BF16),
            pltpu.VMEM((PIECE, W), BF16),
            pltpu.VMEM((2, CHIPS, PIECE, W), F32),
            pltpu.VMEM((2, CHIPS, CODED, 128), jnp.int16),
            pltpu.VMEM((16, CODED, 128), jnp.int16),
            pltpu.VMEM((CHIPS, PIECE, W), F32),
            pltpu.VMEM((CHIPS, PIECE, W), F32),
            pltpu.VMEM((384, 128), F32),
            pltpu.VMEM((16, 32, 128), jnp.int16),
            pltpu.VMEM((16, 32, 128), jnp.int16),
            pltpu.VMEM((8, 32, 128), jnp.int16),
            pltpu.VMEM((2, 16, 32, 128), jnp.int16),
            pltpu.VMEM((2, 384, 128), F32),
            pltpu.VMEM((2, 384, W), F32),
            pltpu.VMEM((2, 384, W), F32),
            dma((4,)), dma((16,)), dma, dma, dma, dma((8,)), dma((8,)),
            dma((8,)), dma((8,)), dma((8,)), dma((8,)), dma((4,)), dma((16,)),
            dma((4, 4)), dma((4, 4)), dma((16,)), dma((16,)), dma((8,)), dma((8,)),
            dma((16,)), dma((16,)), dma((16,)), dma((16,)),
            pltpu.SemaphoreType.REGULAR, pltpu.SemaphoreType.REGULAR,
        ],
        compiler_params=pltpu.CompilerParams(collective_id=0, has_side_effects=True, vmem_limit_bytes=63300000),
        name="exchange",
    )(block_lists, blocks_inverse, factor_rows, diag_inverse)


def store_kernel(column, mirror, diagonal, column_out, mirror_out, diagonal_out, sems):
    copies = [
        pltpu.make_async_copy(diagonal, diagonal_out, sems.at[0]),
        pltpu.make_async_copy(column, column_out, sems.at[1]),
        pltpu.make_async_copy(mirror, mirror_out, sems.at[2]),
    ]
    for copy in copies:
        copy.start()
    for copy in copies:
        copy.wait()


def store(column, mirror, diagonal):
    hbm = pl.BlockSpec(memory_space=pl.ANY)
    return pl.pallas_call(
        store_kernel,
        out_shape=tuple(jax.ShapeDtypeStruct(a.shape, F32) for a in (column, mirror, diagonal)),
        in_specs=[pl.BlockSpec(memory_space=pltpu.VMEM)] * 3,
        out_specs=(hbm, hbm, hbm),
        scratch_shapes=[pltpu.SemaphoreType.DMA((3,))],
        compiler_params=pltpu.CompilerParams(vmem_limit_bytes=8 << 20),
        name="store",
    )(column, mirror, diagonal)


def local(blocks_inverse, factor_rows, block_lists, diag_inverse):
    return store(*exchange(blocks_inverse, factor_rows, block_lists, diag_inverse))


def solution(mesh):
    return jax.shard_map(
        local,
        mesh=mesh,
        in_specs=(P("row", "col"), P(None, "row", None), P(), P()),
        out_specs=(P(None, "row", None), P(None, None, "col"), P()),
        check_vma=False,
    )
```

```python
import jax
import jax.numpy as jnp
from jax import lax
from jax.experimental import pallas as pl
from jax.experimental.pallas import tpu as pltpu
from jax.sharding import PartitionSpec as P

BS = 128
W = 256
CHIPS = 8
PIECE = 48
CODED = 112
TOP = 32000.0
MESH = pl.DeviceIdType.MESH
F32 = jnp.float32
BF16 = jnp.bfloat16


def dot_t(a, b):
    return lax.dot_general(a, b, (((0,), (0,)), ((), ())), preferred_element_type=F32)


def encode(piece):
    parts = []
    steps = []
    for half in range(2):
        part = piece[:, half * 128 : half * 128 + 128]
        most = jnp.max(jnp.abs(part), axis=0, keepdims=True)
        level = jnp.clip(jnp.ceil(8.0 * jnp.log2(jnp.maximum(most, 1e-30))), -800.0, 1000.0)
        factor = jnp.exp2(level * -0.125) * TOP
        parts.append(jnp.round(part * factor).astype(jnp.int32).astype(jnp.int16))
        steps.append(jnp.broadcast_to(level, (8, 128)))
    steps = jnp.concatenate(steps, axis=0).astype(jnp.int32).astype(jnp.int16)
    return jnp.concatenate(parts + [steps], axis=0)


def decode_half(coded, half):
    level = coded[96:112, :].astype(jnp.int32).astype(F32)[8 * half : 8 * half + 1, :]
    step = jnp.exp2(level * 0.125) * (-1.0 / TOP)
    return coded[PIECE * half : PIECE * half + PIECE, :].astype(jnp.int32).astype(F32) * step


def encode_rows(part):
    most = jnp.max(jnp.abs(part), axis=-2, keepdims=True)
    level = jnp.clip(jnp.ceil(8.0 * jnp.log2(jnp.maximum(most, 1e-30))), -800.0, 1000.0)
    coded = jnp.round(part * (jnp.exp2(level * -0.125) * TOP)).astype(jnp.int32)
    steps = jnp.broadcast_to(level, part.shape[:-2] + (8, 128)).astype(jnp.int32)
    return jnp.concatenate([coded, steps], axis=-2).astype(jnp.int16)


def decode_rows(coded):
    wide = coded.astype(jnp.int32).astype(F32)
    return wide[:24, :] * (jnp.exp2(wide[24:25, :] * 0.125) * (1.0 / TOP))


def comm_kernel(
    lists_hbm, a_hbm, f_hbm, diag_hbm, column, mirror, diagonal, lists, diag,
    a_v, f_v, asel, fp, pp, pcv, prv, half, rs, qc, dp, dpc, dr, dz, dg, dgf, pcf, prf,
    ld_sem, fs_send, fs_recv, on_send, on_recv, rs_send, rs_recv,
    ag_send, ag_recv, rl_send, rl_recv, tp_send, tp_recv,
    ys_send, ys_recv, dr_send, dr_recv, dz_send, dz_recv,
    dg_send, dg_recv, do_send, do_recv, met_line, met_mate,
):
    r = lax.axis_index("row")
    c = lax.axis_index("col")
    k = lax.rem(r, 2)
    j = r // 2
    y = lax.rem(c, 4)
    zh = c // 4
    x = lax.rem(j, 4)
    zl = j // 4
    z = zh * 2 + zl
    q = x * 4 + y
    mate = r + 1 - 2 * k
    ck = lax.rem(c, 2)
    cj = c // 2

    def chip(d):
        return lax.rem(j + d, CHIPS)

    def rcopy(src, dst, ssem, rsem, row, col):
        return pltpu.make_async_remote_copy(
            src_ref=src, dst_ref=dst, send_sem=ssem, recv_sem=rsem,
            device_id=(row, col), device_id_type=MESH,
        )

    barrier = pltpu.get_barrier_semaphore()

    def line_y(d):
        return zh * 4 + lax.rem(y + d, 4)

    def line_z(d):
        return lax.rem(zh + d, 4) * 4 + y

    for d in range(1, 4):
        pl.semaphore_signal(barrier, inc=1, device_id=(r, line_z(d)), device_id_type=MESH)
        pl.semaphore_signal(barrier, inc=1, device_id=(r, line_y(d)), device_id_type=MESH)

    def greet(d, carry):
        pl.semaphore_signal(barrier, inc=1, device_id=(lax.rem(r + d, 16), c), device_id_type=MESH)
        return carry

    lax.fori_loop(1, 16, greet, 0)

    load_l = pltpu.make_async_copy(lists_hbm, lists, ld_sem.at[2])
    load_l.start()
    load_d = pltpu.make_async_copy(diag_hbm, diag, ld_sem.at[3])
    load_d.start()
    load_a = pltpu.make_async_copy(a_hbm, a_v, ld_sem.at[0])
    load_f = pltpu.make_async_copy(f_hbm, f_v, ld_sem.at[1])
    load_a.start()
    load_f.start()
    load_l.wait()
    load_a.wait()
    load_f.wait()

    def partial(s):
        for p in range(3):
            rb = lists[s, r * 3 + p] - 2 * (r * 3 + p)
            picked = jnp.where(
                rb == 0, a_v[p * 256 : p * 256 + 128, :], a_v[p * 256 + 128 : p * 256 + 256, :]
            )
            for q in range(3):
                cb = lists[s, c * 3 + q] - 2 * (c * 3 + q)
                asel[p * 128 : p * 128 + 128, q * 128 : q * 128 + 128] = jnp.where(
                    cb == 0, picked[:, q * 256 : q * 256 + 128], picked[:, q * 256 + 128 : q * 256 + 256]
                )
        got = dot_t(asel[...], f_v[s])
        pp[s] = got.reshape(CHIPS, PIECE, W)

    partial(1 - k)

    pl.semaphore_wait(barrier, 21)

    for d in range(1, 4):
        pl.semaphore_signal(met_line, inc=1, device_id=(r, line_y(d)), device_id_type=MESH)

    def swap_copy(o):
        return rcopy(pp.at[1 - k, o], half.at[o], on_send.at[o], on_recv.at[o], mate, c)

    def swap_start(d, carry):
        swap_copy(chip(d)).start()
        return carry

    lax.fori_loop(1, CHIPS + 1, swap_start, 0)

    def fcopy(o):
        return rcopy(
            f_hbm.at[lax.rem(o, 2), pl.ds(pl.multiple_of((o // 2) * PIECE, PIECE), PIECE)],
            fp, fs_send.at[o], fs_recv, o, c,
        )

    @pl.when(r == c)
    def _():
        def scatter(d, carry):
            fcopy(lax.rem(r + d, 16)).start()
            return carry

        lax.fori_loop(1, 16, scatter, 0)
        fp[...] = f_v[k, pl.ds(pl.multiple_of(j * PIECE, PIECE), PIECE), :]

    partial(k)
    pl.semaphore_wait(met_line, 3)
    pl.semaphore_signal(met_mate, inc=1, device_id=(mate, c), device_id_type=MESH)
    pl.semaphore_wait(met_mate, 1)


    def rs_copy(d, slot):
        o = chip(d)
        return rcopy(qc.at[o], rs.at[slot], rs_send.at[o], rs_recv.at[slot], 2 * o + k, c)

    def rs_start(d, carry):
        o = chip(d)
        swap_copy(o).wait_recv()
        qc[o] = encode(pp[k, o] + half[o])
        rs_copy(d, j).start()
        return carry

    lax.fori_loop(1, CHIPS, rs_start, 0)
    swap_copy(j).wait_recv()
    total = pp[k, j] + half[j]
    for d in range(1, CHIPS):
        o = chip(CHIPS - d)
        rs_copy(d, o).wait_recv()
        coded = rs[o]
        total = total - jnp.concatenate([decode_half(coded, 0), decode_half(coded, 1)], axis=1)
    @pl.when(r != c)
    def _():
        fcopy(r).wait_recv()

    high = total.astype(BF16)
    low = (total - high.astype(F32)).astype(BF16)
    left = fp[:, :128]
    right = fp[:, 128:]
    top = dot_t(left, high) + dot_t(left, low)
    dp[0:128, :] = top[:, :128]
    dp[128:256, :] = top[:, 128:]
    dp[256:384, :] = dot_t(right, high[:, 128:]) + dot_t(right, low[:, 128:])

    dpc[...] = encode_rows(dp[...].reshape(16, 24, 128))

    def around(d):
        return lax.rem(q + d, 16)

    def rows24(o):
        return pl.ds(pl.multiple_of(o * 24, 8), 24)

    def dr_copy(d, slot):
        o = around(d)
        return rcopy(
            dpc.at[o], dr.at[slot], dr_send.at[o], dr_recv.at[slot],
            zl * 8 + (o // 4) * 2 + k, zh * 4 + lax.rem(o, 4),
        )

    def dr_start(d, carry):
        dr_copy(d, q).start()
        return carry

    lax.fori_loop(1, 16, dr_start, 0)

    pcv[k, j] = encode(total)

    mine = k * CHIPS + j

    def cross_copy(w):
        return rcopy(pcv.at[k, j], prv.at[mine], tp_send.at[w], tp_recv.at[mine], c, w * 4 + lax.rem(r, 4))

    def is_self(w):
        return jnp.logical_and(r == c, w * 4 + lax.rem(r, 4) == c)

    for w in range(4):

        @pl.when(jnp.logical_not(is_self(w)))
        def _():
            cross_copy(w).start()

        @pl.when(is_self(w))
        def _():
            prv[mine] = pcv[k, j]

    def dr_add(d, acc):
        o = around(16 - d)
        dr_copy(d, o).wait_recv()
        return acc + decode_rows(dr[o])

    dz[z] = encode_rows(lax.fori_loop(1, 16, dr_add, dp[rows24(q), :]))

    def dz_copy(d, slot):
        o = lax.rem(z + d, 8)
        return rcopy(
            dz.at[slot], dz.at[slot], dz_send.at[o], dz_recv.at[slot],
            lax.rem(o, 2) * 8 + lax.rem(r, 8), (o // 2) * 4 + y,
        )

    def dz_start(d, carry):
        dz_copy(d, z).start()
        return carry

    lax.fori_loop(1, 8, dz_start, 0)

    def ag_copy(d, slot):
        return rcopy(pcv.at[k, slot], pcv.at[k, slot], ag_send.at[chip(d)], ag_recv.at[slot], 2 * chip(d) + k, c)

    def ag_start(d, carry):
        ag_copy(d, j).start()
        return carry

    lax.fori_loop(1, CHIPS, ag_start, 0)

    def slot_of(col):
        return lax.rem(col, 2) * CHIPS + col // 2

    def ys_copy(d, w, col):
        slot = slot_of(col)
        return rcopy(
            prv.at[slot], prv.at[slot], ys_send.at[w, lax.rem(y + d, 4)], ys_recv.at[w, lax.rem(col, 4)], r, line_y(d)
        )

    for w in range(4):
        slot = slot_of(w * 4 + y)

        @pl.when(jnp.logical_not(jnp.logical_and(r == c, w == zh)))
        def _():
            rcopy(pcv.at[k, j], prv.at[slot], tp_send.at[w], tp_recv.at[slot], c, c).wait_recv()

        for d in range(1, 4):
            ys_copy(d, w, w * 4 + y).start()

    def rl_copy(s, slot):
        return rcopy(pcv.at[s, slot], pcv.at[s, slot], rl_send.at[slot], rl_recv.at[slot], mate, c)

    rl_copy(k, j).start()

    def relay(d, carry):
        o = chip(CHIPS - d)
        ag_copy(d, o).wait_recv()
        rl_copy(k, o).start()
        return carry

    lax.fori_loop(1, CHIPS, relay, 0)

    def dz_wait(d, carry):
        dz_copy(d, lax.rem(z + 8 - d, 8)).wait_recv()
        return carry

    lax.fori_loop(1, 8, dz_wait, 0)
    both = [decode_rows(dz[2 * i]) + decode_rows(dz[2 * i + 1]) for i in range(4)]
    dg[k, q] = encode_rows((both[0] + both[1]) + (both[2] + both[3]))

    def dg_copy(d, slot):
        o = around(d)
        return rcopy(
            dg.at[k, slot], dg.at[k, slot], dg_send.at[o], dg_recv.at[slot],
            zl * 8 + (o // 4) * 2 + k, zh * 4 + lax.rem(o, 4),
        )

    def do_copy(s, slot):
        return rcopy(dg.at[s, slot], dg.at[s, slot], do_send.at[slot], do_recv.at[slot], mate, c)

    def dg_start(d, carry):
        dg_copy(d, q).start()
        return carry

    lax.fori_loop(1, 16, dg_start, 0)
    do_copy(k, q).start()

    for d in range(8):
        rl_copy(1 - k, d).wait_recv()

    def open_pc(o, carry):
        rows = pl.ds(pl.multiple_of(lax.rem(o, 8) * PIECE, 8), PIECE)
        coded = pcv[o // 8, lax.rem(o, 8)]
        pcf[o // 8, rows, 0:128] = decode_half(coded, 0)
        pcf[o // 8, rows, 128:256] = decode_half(coded, 1)
        return carry

    lax.fori_loop(0, 16, open_pc, 0)
    for s in range(2):
        for p in range(3):
            at = lists[s, c * 3 + p] - 2 * (c * 3 + p)
            block = jnp.transpose(pcf[s, p * BS : p * BS + BS, :])
            mirror[s, :, 2 * p * BS : 2 * p * BS + BS] = jnp.where(at == 0, block, 0.0)
            mirror[s, :, 2 * p * BS + BS : 2 * p * BS + 2 * BS] = jnp.where(at == 0, 0.0, block)
    for w in range(4):
        for d in range(1, 4):
            ys_copy(d, w, w * 4 + lax.rem(y + 4 - d, 4)).wait_recv()

    def open_pr(o, carry):
        rows = pl.ds(pl.multiple_of(lax.rem(o, 8) * PIECE, 8), PIECE)
        coded = prv[o]
        prf[o // 8, rows, 0:128] = decode_half(coded, 0)
        prf[o // 8, rows, 128:256] = decode_half(coded, 1)
        return carry

    lax.fori_loop(0, 16, open_pr, 0)
    for s in range(2):
        for p in range(3):
            at = lists[s, r * 3 + p] - 2 * (r * 3 + p)
            block = prf[s, p * BS : p * BS + BS, :]
            column[s, 2 * p * BS : 2 * p * BS + BS, :] = jnp.where(at == 0, block, 0.0)
            column[s, 2 * p * BS + BS : 2 * p * BS + 2 * BS, :] = jnp.where(at == 0, 0.0, block)
    load_d.wait()

    def dg_relay(d, carry):
        o = around(16 - d)
        dg_copy(d, o).wait_recv()
        do_copy(k, o).start()
        dgf[k, rows24(o), :] = decode_rows(dg[k, o])
        return carry

    dgf[k, rows24(q), :] = decode_rows(dg[k, q])
    lax.fori_loop(1, 16, dg_relay, 0)

    def do_wait(d, carry):
        do_copy(1 - k, d).wait_recv()
        dgf[1 - k, rows24(d), :] = decode_rows(dg[1 - k, d])
        return carry

    lax.fori_loop(0, 16, do_wait, 0)
    for s in range(2):
        upper = dgf[s, 128:256, :]
        diagonal[s, 0:128, 0:128] = diag[s, 0:128, 0:128] + dgf[s, 0:128, :]
        diagonal[s, 0:128, 128:256] = diag[s, 0:128, 128:256] + upper
        diagonal[s, 128:256, 0:128] = diag[s, 128:256, 0:128] + jnp.transpose(upper)
        diagonal[s, 128:256, 128:256] = diag[s, 128:256, 128:256] + dgf[s, 256:384, :]

    def swap_drain(d, carry):
        swap_copy(d).wait_send()
        return carry

    lax.fori_loop(0, CHIPS, swap_drain, 0)

    for w in range(4):

        @pl.when(jnp.logical_not(is_self(w)))
        def _():
            cross_copy(w).wait_send()

    @pl.when(r == c)
    def _():
        def scattered(d, carry):
            fcopy(lax.rem(r + d, 16)).wait_send()
            return carry

        lax.fori_loop(1, 16, scattered, 0)

    def drain(d, carry):
        rs_copy(d, j).wait_send()
        ag_copy(d, j).wait_send()
        dz_copy(d, z).wait_send()
        return carry

    lax.fori_loop(1, CHIPS, drain, 0)
    for d in range(CHIPS):
        rl_copy(k, d).wait_send()
    for d in range(1, 4):
        for w in range(4):
            ys_copy(d, w, w * 4 + y).wait_send()

    def drain_plane(d, carry):
        dr_copy(d, q).wait_send()
        dg_copy(d, q).wait_send()
        return carry

    lax.fori_loop(1, 16, drain_plane, 0)

    def drain_relay(d, carry):
        do_copy(k, d).wait_send()
        return carry

    lax.fori_loop(0, 16, drain_relay, 0)


def exchange(blocks_inverse, factor_rows, block_lists, diag_inverse):
    dma = pltpu.SemaphoreType.DMA
    hbm = pl.BlockSpec(memory_space=pl.ANY)
    vmem = pl.BlockSpec(memory_space=pltpu.VMEM)
    return pl.pallas_call(
        comm_kernel,
        out_shape=(pltpu.VMEM((2, 768, W), F32), pltpu.VMEM((2, W, 768), F32), pltpu.VMEM((2, W, W), F32)),
        in_specs=[hbm] * 4,
        out_specs=(vmem, vmem, vmem),
        scratch_shapes=[
            pltpu.SMEM((2, 48), jnp.int32),
            pltpu.VMEM((2, W, W), F32),
            pltpu.VMEM((768, 768), BF16),
            pltpu.VMEM((2, 384, W), BF16),
            pltpu.VMEM((384, 384), BF16),
            pltpu.VMEM((PIECE, W), BF16),
            pltpu.VMEM((2, CHIPS, PIECE, W), F32),
            pltpu.VMEM((2, CHIPS, CODED, 128), jnp.int16),
            pltpu.VMEM((16, CODED, 128), jnp.int16),
            pltpu.VMEM((CHIPS, PIECE, W), F32),
            pltpu.VMEM((CHIPS, CODED, 128), jnp.int16),
            pltpu.VMEM((CHIPS, CODED, 128), jnp.int16),
            pltpu.VMEM((384, 128), F32),
            pltpu.VMEM((16, 32, 128), jnp.int16),
            pltpu.VMEM((16, 32, 128), jnp.int16),
            pltpu.VMEM((8, 32, 128), jnp.int16),
            pltpu.VMEM((2, 16, 32, 128), jnp.int16),
            pltpu.VMEM((2, 384, 128), F32),
            pltpu.VMEM((2, 384, W), F32),
            pltpu.VMEM((2, 384, W), F32),
            dma((4,)), dma((16,)), dma, dma((8,)), dma((8,)), dma((8,)), dma((8,)),
            dma((8,)), dma((8,)), dma((8,)), dma((8,)), dma((4,)), dma((16,)),
            dma((4, 4)), dma((4, 4)), dma((16,)), dma((16,)), dma((8,)), dma((8,)),
            dma((16,)), dma((16,)), dma((16,)), dma((16,)),
            pltpu.SemaphoreType.REGULAR, pltpu.SemaphoreType.REGULAR,
        ],
        compiler_params=pltpu.CompilerParams(collective_id=0, has_side_effects=True, vmem_limit_bytes=63300000),
        name="exchange",
    )(block_lists, blocks_inverse, factor_rows, diag_inverse)


def store_kernel(column, mirror, diagonal, column_out, mirror_out, diagonal_out, sems):
    copies = [
        pltpu.make_async_copy(diagonal, diagonal_out, sems.at[0]),
        pltpu.make_async_copy(column, column_out, sems.at[1]),
        pltpu.make_async_copy(mirror, mirror_out, sems.at[2]),
    ]
    for copy in copies:
        copy.start()
    for copy in copies:
        copy.wait()


def store(column, mirror, diagonal):
    hbm = pl.BlockSpec(memory_space=pl.ANY)
    return pl.pallas_call(
        store_kernel,
        out_shape=tuple(jax.ShapeDtypeStruct(a.shape, F32) for a in (column, mirror, diagonal)),
        in_specs=[pl.BlockSpec(memory_space=pltpu.VMEM)] * 3,
        out_specs=(hbm, hbm, hbm),
        scratch_shapes=[pltpu.SemaphoreType.DMA((3,))],
        compiler_params=pltpu.CompilerParams(vmem_limit_bytes=8 << 20),
        name="store",
    )(column, mirror, diagonal)


def local(blocks_inverse, factor_rows, block_lists, diag_inverse):
    return store(*exchange(blocks_inverse, factor_rows, block_lists, diag_inverse))


def solution(mesh):
    return jax.shard_map(
        local,
        mesh=mesh,
        in_specs=(P("row", "col"), P(None, "row", None), P(), P()),
        out_specs=(P(None, "row", None), P(None, None, "col"), P()),
        check_vma=False,
    )
```

```python
import jax
import jax.numpy as jnp
from jax import lax
from jax.experimental import pallas as pl
from jax.experimental.pallas import tpu as pltpu
from jax.sharding import PartitionSpec as P

BS = 128
W = 256
CHIPS = 8
PIECE = 48
CODED = 112
TOP = 32000.0
MESH = pl.DeviceIdType.MESH
F32 = jnp.float32
BF16 = jnp.bfloat16


def dot_t(a, b):
    return lax.dot_general(a, b, (((0,), (0,)), ((), ())), preferred_element_type=F32)


def ring(d, n):
    return min(d, n - d)


PLANE = sorted(((i, e) for i in range(4) for e in range(4) if i + e), key=lambda t: ring(t[0], 4) + ring(t[1], 4))
GROUP = sorted(((i, e) for i in range(2) for e in range(4) if i + e), key=lambda t: t[0] + ring(t[1], 4))
RING_Z = sorted(range(1, 8), key=lambda d: ring(d, 8))


def encode(piece):
    parts = []
    steps = []
    for half in range(2):
        part = piece[:, half * 128 : half * 128 + 128]
        most = jnp.max(jnp.abs(part), axis=0, keepdims=True)
        level = jnp.clip(jnp.ceil(8.0 * jnp.log2(jnp.maximum(most, 1e-30))), -800.0, 1000.0)
        factor = jnp.exp2(level * -0.125) * TOP
        parts.append(jnp.round(part * factor).astype(jnp.int32).astype(jnp.int16))
        steps.append(jnp.broadcast_to(level, (8, 128)))
    steps = jnp.concatenate(steps, axis=0).astype(jnp.int32).astype(jnp.int16)
    return jnp.concatenate(parts + [steps], axis=0)


def decode_half(coded, half):
    level = coded[96:112, :].astype(jnp.int32).astype(F32)[8 * half : 8 * half + 1, :]
    step = jnp.exp2(level * 0.125) * (-1.0 / TOP)
    return coded[PIECE * half : PIECE * half + PIECE, :].astype(jnp.int32).astype(F32) * step


def encode_rows(part):
    most = jnp.max(jnp.abs(part), axis=-2, keepdims=True)
    level = jnp.clip(jnp.ceil(8.0 * jnp.log2(jnp.maximum(most, 1e-30))), -800.0, 1000.0)
    coded = jnp.round(part * (jnp.exp2(level * -0.125) * TOP)).astype(jnp.int32)
    steps = jnp.broadcast_to(level, part.shape[:-2] + (8, 128)).astype(jnp.int32)
    return jnp.concatenate([coded, steps], axis=-2).astype(jnp.int16)


def decode_rows(coded):
    wide = coded.astype(jnp.int32).astype(F32)
    return wide[:24, :] * (jnp.exp2(wide[24:25, :] * 0.125) * (1.0 / TOP))


def comm_kernel(
    lists_hbm, a_hbm, f_hbm, diag_hbm, column, mirror, diagonal, lists, diag,
    a_v, f_v, asel, fp, pp, pcv, prv, half, rs, qc, dp, dpc, dr, dz, dg, dgf, pcf, prf,
    ld_sem, fs_send, fs_recv, on_send, on_recv, rs_send, rs_recv,
    ag_send, ag_recv, rl_send, rl_recv, tp_send, tp_recv,
    ys_send, ys_recv, dr_send, dr_recv, dz_send, dz_recv,
    dg_send, dg_recv, do_send, do_recv, met_a, met_b, met_c,
):
    r = lax.axis_index("row")
    c = lax.axis_index("col")
    k = lax.rem(r, 2)
    j = r // 2
    y = lax.rem(c, 4)
    zh = c // 4
    x = lax.rem(j, 4)
    zl = j // 4
    z = zh * 2 + zl
    q = x * 4 + y
    mate = r + 1 - 2 * k
    ck = lax.rem(c, 2)
    cj = c // 2

    def chip(d):
        return lax.rem(j + d, CHIPS)

    def group_to(off):
        return lax.rem(zl + off[0], 2) * 4 + lax.rem(x + off[1], 4)

    def group_from(off):
        return lax.rem(zl + off[0], 2) * 4 + lax.rem(x + 4 - off[1], 4)

    def plane_to(off):
        return lax.rem(x + off[0], 4) * 4 + lax.rem(y + off[1], 4)

    def plane_from(off):
        return lax.rem(x + 4 - off[0], 4) * 4 + lax.rem(y + 4 - off[1], 4)

    def rcopy(src, dst, ssem, rsem, row, col):
        return pltpu.make_async_remote_copy(
            src_ref=src, dst_ref=dst, send_sem=ssem, recv_sem=rsem,
            device_id=(row, col), device_id_type=MESH,
        )

    barrier = pltpu.get_barrier_semaphore()

    def line_y(d):
        return zh * 4 + lax.rem(y + d, 4)

    def line_z(d):
        return lax.rem(zh + d, 4) * 4 + y

    for d in (1, 3):
        pl.semaphore_signal(barrier, inc=1, device_id=(r, line_z(d)), device_id_type=MESH)
    for d in range(1, 4):
        pl.semaphore_signal(barrier, inc=1, device_id=(r, line_y(d)), device_id_type=MESH)

    def greet(d, carry):
        pl.semaphore_signal(barrier, inc=1, device_id=(lax.rem(r + d, 16), c), device_id_type=MESH)
        return carry

    lax.fori_loop(1, 16, greet, 0)

    load_l = pltpu.make_async_copy(lists_hbm, lists, ld_sem.at[2])
    load_l.start()
    load_d = pltpu.make_async_copy(diag_hbm, diag, ld_sem.at[3])
    load_d.start()
    load_a = pltpu.make_async_copy(a_hbm, a_v, ld_sem.at[0])
    load_f = pltpu.make_async_copy(f_hbm, f_v, ld_sem.at[1])
    load_a.start()
    load_f.start()
    load_l.wait()
    load_a.wait()
    load_f.wait()

    def partial(s):
        for p in range(3):
            rb = lists[s, r * 3 + p] - 2 * (r * 3 + p)
            picked = jnp.where(
                rb == 0, a_v[p * 256 : p * 256 + 128, :], a_v[p * 256 + 128 : p * 256 + 256, :]
            )
            for q in range(3):
                cb = lists[s, c * 3 + q] - 2 * (c * 3 + q)
                asel[p * 128 : p * 128 + 128, q * 128 : q * 128 + 128] = jnp.where(
                    cb == 0, picked[:, q * 256 : q * 256 + 128], picked[:, q * 256 + 128 : q * 256 + 256]
                )
        got = dot_t(asel[...], f_v[s])
        pp[s] = got.reshape(CHIPS, PIECE, W)

    partial(1 - k)

    pl.semaphore_wait(barrier, 20)

    for d in (1, 3):
        pl.semaphore_signal(met_a, inc=1, device_id=(r, line_z(d)), device_id_type=MESH)
    for d in range(1, 4):
        pl.semaphore_signal(met_a, inc=1, device_id=(r, line_y(d)), device_id_type=MESH)

    def swap_copy(o):
        return rcopy(pp.at[1 - k, o], half.at[o], on_send.at[o], on_recv.at[o], mate, c)

    for off in GROUP[::-1]:
        swap_copy(group_to(off)).start()
    swap_copy(j).start()

    def fcopy(o):
        return rcopy(
            f_hbm.at[lax.rem(o, 2), pl.ds(pl.multiple_of((o // 2) * PIECE, PIECE), PIECE)],
            fp, fs_send.at[o], fs_recv, o, c,
        )

    @pl.when(r == c)
    def _():
        def scatter(d, carry):
            fcopy(lax.rem(r + d, 16)).start()
            return carry

        lax.fori_loop(1, 16, scatter, 0)
        fp[...] = f_v[k, pl.ds(pl.multiple_of(j * PIECE, PIECE), PIECE), :]

    partial(k)

    def rs_copy(o, slot):
        return rcopy(qc.at[o], rs.at[slot], rs_send.at[o], rs_recv.at[slot], 2 * o + k, c)

    for off in GROUP[::-1]:
        o = group_to(off)
        swap_copy(o).wait_recv()
        qc[o] = encode(pp[k, o] + half[o])
        rs_copy(o, j).start()
    pl.semaphore_wait(met_a, 5)
    for d in range(1, 4):
        pl.semaphore_signal(met_b, inc=1, device_id=(r, line_y(d)), device_id_type=MESH)
    swap_copy(j).wait_recv()
    total = pp[k, j] + half[j]
    pl.semaphore_wait(met_b, 3)

    def tell(d, carry):
        pl.semaphore_signal(met_c, inc=1, device_id=(lax.rem(r + d, 16), c), device_id_type=MESH)
        return carry

    lax.fori_loop(1, 16, tell, 0)
    for off in GROUP:
        o = group_from(off)
        rs_copy(o, o).wait_recv()
        coded = rs[o]
        total = total - jnp.concatenate([decode_half(coded, 0), decode_half(coded, 1)], axis=1)

    @pl.when(r != c)
    def _():
        fcopy(r).wait_recv()

    high = total.astype(BF16)
    low = (total - high.astype(F32)).astype(BF16)
    left = fp[:, :128]
    right = fp[:, 128:]
    top = dot_t(left, high) + dot_t(left, low)
    dp[0:128, :] = top[:, :128]
    dp[128:256, :] = top[:, 128:]
    dp[256:384, :] = dot_t(right, high[:, 128:]) + dot_t(right, low[:, 128:])

    dpc[...] = encode_rows(dp[...].reshape(16, 24, 128))

    def around(d):
        return lax.rem(q + d, 16)

    def rows24(o):
        return pl.ds(pl.multiple_of(o * 24, 8), 24)

    def dr_copy(o, slot):
        return rcopy(
            dpc.at[o], dr.at[slot], dr_send.at[o], dr_recv.at[slot],
            zl * 8 + (o // 4) * 2 + k, zh * 4 + lax.rem(o, 4),
        )

    for off in PLANE[::-1]:
        dr_copy(plane_to(off), q).start()

    pcv[k, j] = encode(total)
    pl.semaphore_wait(met_c, 15)

    mine = k * CHIPS + j

    def cross_copy(w):
        return rcopy(pcv.at[k, j], prv.at[mine], tp_send.at[w], tp_recv.at[mine], c, w * 4 + lax.rem(r, 4))

    def is_self(w):
        return jnp.logical_and(r == c, w * 4 + lax.rem(r, 4) == c)

    for w in range(4):

        @pl.when(jnp.logical_not(is_self(w)))
        def _():
            cross_copy(w).start()

        @pl.when(is_self(w))
        def _():
            prv[mine] = pcv[k, j]

    acc = dp[rows24(q), :]
    for off in PLANE:
        o = plane_from(off)
        dr_copy(o, o).wait_recv()
        acc = acc + decode_rows(dr[o])
    dz[z] = encode_rows(acc)

    def dz_copy(d, slot):
        o = lax.rem(z + d, 8)
        return rcopy(
            dz.at[slot], dz.at[slot], dz_send.at[o], dz_recv.at[slot],
            lax.rem(o, 2) * 8 + lax.rem(r, 8), (o // 2) * 4 + y,
        )

    for d in RING_Z[::-1]:
        dz_copy(d, z).start()

    def ag_copy(d, slot):
        return rcopy(pcv.at[k, slot], pcv.at[k, slot], ag_send.at[chip(d)], ag_recv.at[slot], 2 * chip(d) + k, c)

    def ag_start(d, carry):
        ag_copy(d, j).start()
        return carry

    lax.fori_loop(1, CHIPS, ag_start, 0)

    def slot_of(col):
        return lax.rem(col, 2) * CHIPS + col // 2

    def ys_copy(d, w, col):
        slot = slot_of(col)
        return rcopy(
            prv.at[slot], prv.at[slot], ys_send.at[w, lax.rem(y + d, 4)], ys_recv.at[w, lax.rem(col, 4)], r, line_y(d)
        )

    for w in range(4):
        slot = slot_of(w * 4 + y)

        @pl.when(jnp.logical_not(jnp.logical_and(r == c, w == zh)))
        def _():
            rcopy(pcv.at[k, j], prv.at[slot], tp_send.at[w], tp_recv.at[slot], c, c).wait_recv()

        for d in range(1, 4):
            ys_copy(d, w, w * 4 + y).start()

    def rl_copy(s, slot):
        return rcopy(pcv.at[s, slot], pcv.at[s, slot], rl_send.at[slot], rl_recv.at[slot], mate, c)

    rl_copy(k, j).start()

    def relay(d, carry):
        o = chip(CHIPS - d)
        ag_copy(d, o).wait_recv()
        rl_copy(k, o).start()
        return carry

    lax.fori_loop(1, CHIPS, relay, 0)

    def dz_wait(d, carry):
        dz_copy(d, lax.rem(z + 8 - d, 8)).wait_recv()
        return carry

    lax.fori_loop(1, 8, dz_wait, 0)
    both = [decode_rows(dz[2 * i]) + decode_rows(dz[2 * i + 1]) for i in range(4)]
    dg[k, q] = encode_rows((both[0] + both[1]) + (both[2] + both[3]))

    def dg_copy(o, slot):
        return rcopy(
            dg.at[k, slot], dg.at[k, slot], dg_send.at[o], dg_recv.at[slot],
            zl * 8 + (o // 4) * 2 + k, zh * 4 + lax.rem(o, 4),
        )

    def do_copy(s, slot):
        return rcopy(dg.at[s, slot], dg.at[s, slot], do_send.at[slot], do_recv.at[slot], mate, c)

    for off in PLANE[::-1]:
        dg_copy(plane_to(off), q).start()
    do_copy(k, q).start()

    for d in range(8):
        rl_copy(1 - k, d).wait_recv()

    def open_pc(o, carry):
        rows = pl.ds(pl.multiple_of(lax.rem(o, 8) * PIECE, 8), PIECE)
        coded = pcv[o // 8, lax.rem(o, 8)]
        pcf[o // 8, rows, 0:128] = decode_half(coded, 0)
        pcf[o // 8, rows, 128:256] = decode_half(coded, 1)
        return carry

    lax.fori_loop(0, 16, open_pc, 0)
    for s in range(2):
        for p in range(3):
            at = lists[s, c * 3 + p] - 2 * (c * 3 + p)
            block = jnp.transpose(pcf[s, p * BS : p * BS + BS, :])
            mirror[s, :, 2 * p * BS : 2 * p * BS + BS] = jnp.where(at == 0, block, 0.0)
            mirror[s, :, 2 * p * BS + BS : 2 * p * BS + 2 * BS] = jnp.where(at == 0, 0.0, block)
    for w in range(4):
        for d in range(1, 4):
            ys_copy(d, w, w * 4 + lax.rem(y + 4 - d, 4)).wait_recv()

    def open_pr(o, carry):
        rows = pl.ds(pl.multiple_of(lax.rem(o, 8) * PIECE, 8), PIECE)
        coded = prv[o]
        prf[o // 8, rows, 0:128] = decode_half(coded, 0)
        prf[o // 8, rows, 128:256] = decode_half(coded, 1)
        return carry

    lax.fori_loop(0, 16, open_pr, 0)
    for s in range(2):
        for p in range(3):
            at = lists[s, r * 3 + p] - 2 * (r * 3 + p)
            block = prf[s, p * BS : p * BS + BS, :]
            column[s, 2 * p * BS : 2 * p * BS + BS, :] = jnp.where(at == 0, block, 0.0)
            column[s, 2 * p * BS + BS : 2 * p * BS + 2 * BS, :] = jnp.where(at == 0, 0.0, block)
    load_d.wait()

    dgf[k, rows24(q), :] = decode_rows(dg[k, q])
    for off in PLANE:
        o = plane_from(off)
        dg_copy(o, o).wait_recv()
        do_copy(k, o).start()
        dgf[k, rows24(o), :] = decode_rows(dg[k, o])
    for off in [(0, 0)] + PLANE:
        o = plane_from(off)
        do_copy(1 - k, o).wait_recv()
        dgf[1 - k, rows24(o), :] = decode_rows(dg[1 - k, o])
    for s in range(2):
        upper = dgf[s, 128:256, :]
        diagonal[s, 0:128, 0:128] = diag[s, 0:128, 0:128] + dgf[s, 0:128, :]
        diagonal[s, 0:128, 128:256] = diag[s, 0:128, 128:256] + upper
        diagonal[s, 128:256, 0:128] = diag[s, 128:256, 0:128] + jnp.transpose(upper)
        diagonal[s, 128:256, 128:256] = diag[s, 128:256, 128:256] + dgf[s, 256:384, :]

    def swap_drain(d, carry):
        swap_copy(d).wait_send()
        return carry

    lax.fori_loop(0, CHIPS, swap_drain, 0)

    for w in range(4):

        @pl.when(jnp.logical_not(is_self(w)))
        def _():
            cross_copy(w).wait_send()

    @pl.when(r == c)
    def _():
        def scattered(d, carry):
            fcopy(lax.rem(r + d, 16)).wait_send()
            return carry

        lax.fori_loop(1, 16, scattered, 0)

    def drain(d, carry):
        rs_copy(chip(d), j).wait_send()
        ag_copy(d, j).wait_send()
        dz_copy(d, z).wait_send()
        return carry

    lax.fori_loop(1, CHIPS, drain, 0)
    for d in range(CHIPS):
        rl_copy(k, d).wait_send()
    for d in range(1, 4):
        for w in range(4):
            ys_copy(d, w, w * 4 + y).wait_send()

    def drain_plane(d, carry):
        dr_copy(around(d), q).wait_send()
        dg_copy(around(d), q).wait_send()
        return carry

    lax.fori_loop(1, 16, drain_plane, 0)

    def drain_relay(d, carry):
        do_copy(k, d).wait_send()
        return carry

    lax.fori_loop(0, 16, drain_relay, 0)


def exchange(blocks_inverse, factor_rows, block_lists, diag_inverse):
    dma = pltpu.SemaphoreType.DMA
    hbm = pl.BlockSpec(memory_space=pl.ANY)
    vmem = pl.BlockSpec(memory_space=pltpu.VMEM)
    return pl.pallas_call(
        comm_kernel,
        out_shape=(pltpu.VMEM((2, 768, W), F32), pltpu.VMEM((2, W, 768), F32), pltpu.VMEM((2, W, W), F32)),
        in_specs=[hbm] * 4,
        out_specs=(vmem, vmem, vmem),
        scratch_shapes=[
            pltpu.SMEM((2, 48), jnp.int32),
            pltpu.VMEM((2, W, W), F32),
            pltpu.VMEM((768, 768), BF16),
            pltpu.VMEM((2, 384, W), BF16),
            pltpu.VMEM((384, 384), BF16),
            pltpu.VMEM((PIECE, W), BF16),
            pltpu.VMEM((2, CHIPS, PIECE, W), F32),
            pltpu.VMEM((2, CHIPS, CODED, 128), jnp.int16),
            pltpu.VMEM((16, CODED, 128), jnp.int16),
            pltpu.VMEM((CHIPS, PIECE, W), F32),
            pltpu.VMEM((CHIPS, CODED, 128), jnp.int16),
            pltpu.VMEM((CHIPS, CODED, 128), jnp.int16),
            pltpu.VMEM((384, 128), F32),
            pltpu.VMEM((16, 32, 128), jnp.int16),
            pltpu.VMEM((16, 32, 128), jnp.int16),
            pltpu.VMEM((8, 32, 128), jnp.int16),
            pltpu.VMEM((2, 16, 32, 128), jnp.int16),
            pltpu.VMEM((2, 384, 128), F32),
            pltpu.VMEM((2, 384, W), F32),
            pltpu.VMEM((2, 384, W), F32),
            dma((4,)), dma((16,)), dma, dma((8,)), dma((8,)), dma((8,)), dma((8,)),
            dma((8,)), dma((8,)), dma((8,)), dma((8,)), dma((4,)), dma((16,)),
            dma((4, 4)), dma((4, 4)), dma((16,)), dma((16,)), dma((8,)), dma((8,)),
            dma((16,)), dma((16,)), dma((16,)), dma((16,)),
            pltpu.SemaphoreType.REGULAR, pltpu.SemaphoreType.REGULAR, pltpu.SemaphoreType.REGULAR,
        ],
        compiler_params=pltpu.CompilerParams(collective_id=0, has_side_effects=True, vmem_limit_bytes=63300000),
        name="exchange",
    )(block_lists, blocks_inverse, factor_rows, diag_inverse)


def store_kernel(column, mirror, diagonal, column_out, mirror_out, diagonal_out, sems):
    copies = [
        pltpu.make_async_copy(diagonal, diagonal_out, sems.at[0]),
        pltpu.make_async_copy(column, column_out, sems.at[1]),
        pltpu.make_async_copy(mirror, mirror_out, sems.at[2]),
    ]
    for copy in copies:
        copy.start()
    for copy in copies:
        copy.wait()


def store(column, mirror, diagonal):
    hbm = pl.BlockSpec(memory_space=pl.ANY)
    return pl.pallas_call(
        store_kernel,
        out_shape=tuple(jax.ShapeDtypeStruct(a.shape, F32) for a in (column, mirror, diagonal)),
        in_specs=[pl.BlockSpec(memory_space=pltpu.VMEM)] * 3,
        out_specs=(hbm, hbm, hbm),
        scratch_shapes=[pltpu.SemaphoreType.DMA((3,))],
        compiler_params=pltpu.CompilerParams(vmem_limit_bytes=8 << 20),
        name="store",
    )(column, mirror, diagonal)


def local(blocks_inverse, factor_rows, block_lists, diag_inverse):
    return store(*exchange(blocks_inverse, factor_rows, block_lists, diag_inverse))


def solution(mesh):
    return jax.shard_map(
        local,
        mesh=mesh,
        in_specs=(P("row", "col"), P(None, "row", None), P(), P()),
        out_specs=(P(None, "row", None), P(None, None, "col"), P()),
        check_vma=False,
    )
```

```python
import jax
import jax.numpy as jnp
from jax import lax
from jax.experimental import pallas as pl
from jax.experimental.pallas import tpu as pltpu
from jax.sharding import PartitionSpec as P

BS = 128
W = 256
CHIPS = 8
PIECE = 48
CODED = 112
TOP = 32000.0
MESH = pl.DeviceIdType.MESH
F32 = jnp.float32
BF16 = jnp.bfloat16


def dot_t(a, b):
    return lax.dot_general(a, b, (((0,), (0,)), ((), ())), preferred_element_type=F32)


def ring(d, n):
    return min(d, n - d)


PLANE = sorted(((i, e) for i in range(4) for e in range(4) if i + e), key=lambda t: ring(t[0], 4) + ring(t[1], 4))
GROUP = sorted(((i, e) for i in range(2) for e in range(4) if i + e), key=lambda t: t[0] + ring(t[1], 4))
RING_Z = sorted(range(1, 8), key=lambda d: ring(d, 8))


def encode(piece):
    parts = []
    steps = []
    for half in range(2):
        part = piece[:, half * 128 : half * 128 + 128]
        most = jnp.max(jnp.abs(part), axis=0, keepdims=True)
        level = jnp.clip(jnp.ceil(8.0 * jnp.log2(jnp.maximum(most, 1e-30))), -800.0, 1000.0)
        factor = jnp.exp2(level * -0.125) * TOP
        parts.append(jnp.round(part * factor).astype(jnp.int32).astype(jnp.int16))
        steps.append(jnp.broadcast_to(level, (8, 128)))
    steps = jnp.concatenate(steps, axis=0).astype(jnp.int32).astype(jnp.int16)
    return jnp.concatenate(parts + [steps], axis=0)


def decode_half(coded, half):
    level = coded[96:112, :].astype(jnp.int32).astype(F32)[8 * half : 8 * half + 1, :]
    step = jnp.exp2(level * 0.125) * (-1.0 / TOP)
    return coded[PIECE * half : PIECE * half + PIECE, :].astype(jnp.int32).astype(F32) * step


def encode_rows(part):
    most = jnp.max(jnp.abs(part), axis=-2, keepdims=True)
    level = jnp.clip(jnp.ceil(8.0 * jnp.log2(jnp.maximum(most, 1e-30))), -800.0, 1000.0)
    coded = jnp.round(part * (jnp.exp2(level * -0.125) * TOP)).astype(jnp.int32)
    steps = jnp.broadcast_to(level, part.shape[:-2] + (8, 128)).astype(jnp.int32)
    return jnp.concatenate([coded, steps], axis=-2).astype(jnp.int16)


def decode_rows(coded):
    wide = coded.astype(jnp.int32).astype(F32)
    return wide[:24, :] * (jnp.exp2(wide[24:25, :] * 0.125) * (1.0 / TOP))


def comm_kernel(
    lists_hbm, a_hbm, f_hbm, diag_hbm, column, mirror, diagonal, lists, diag,
    a_v, f_v, asel, fp, pp, pcv, prv, half, rs, qc, dp, dpc, dr, dz, dg, dgf, pcf, prf,
    ld_sem, fs_send, fs_recv, on_send, on_recv, rs_send, rs_recv,
    ag_send, ag_recv, rl_send, rl_recv, tp_send, tp_recv,
    ys_send, ys_recv, dr_send, dr_recv, dz_send, dz_recv,
    dg_send, dg_recv, do_send, do_recv, met_a, met_b, met_c,
):
    r = lax.axis_index("row")
    c = lax.axis_index("col")
    k = lax.rem(r, 2)
    j = r // 2
    y = lax.rem(c, 4)
    zh = c // 4
    x = lax.rem(j, 4)
    zl = j // 4
    z = zh * 2 + zl
    q = x * 4 + y
    mate = r + 1 - 2 * k
    ck = lax.rem(c, 2)
    cj = c // 2

    def chip(d):
        return lax.rem(j + d, CHIPS)

    def group_to(off):
        return lax.rem(zl + off[0], 2) * 4 + lax.rem(x + off[1], 4)

    def group_from(off):
        return lax.rem(zl + off[0], 2) * 4 + lax.rem(x + 4 - off[1], 4)

    def plane_to(off):
        return lax.rem(x + off[0], 4) * 4 + lax.rem(y + off[1], 4)

    def plane_from(off):
        return lax.rem(x + 4 - off[0], 4) * 4 + lax.rem(y + 4 - off[1], 4)

    def rcopy(src, dst, ssem, rsem, row, col):
        return pltpu.make_async_remote_copy(
            src_ref=src, dst_ref=dst, send_sem=ssem, recv_sem=rsem,
            device_id=(row, col), device_id_type=MESH,
        )

    barrier = pltpu.get_barrier_semaphore()

    def line_y(d):
        return zh * 4 + lax.rem(y + d, 4)

    def line_z(d):
        return lax.rem(zh + d, 4) * 4 + y

    for d in (1, 3):
        pl.semaphore_signal(barrier, inc=1, device_id=(r, line_z(d)), device_id_type=MESH)
    for d in range(1, 4):
        pl.semaphore_signal(barrier, inc=1, device_id=(r, line_y(d)), device_id_type=MESH)

    def greet(d, carry):
        pl.semaphore_signal(barrier, inc=1, device_id=(lax.rem(r + d, 16), c), device_id_type=MESH)
        return carry

    lax.fori_loop(1, 16, greet, 0)

    load_l = pltpu.make_async_copy(lists_hbm, lists, ld_sem.at[2])
    load_l.start()
    load_d = pltpu.make_async_copy(diag_hbm, diag, ld_sem.at[3])
    load_d.start()
    load_a = pltpu.make_async_copy(a_hbm, a_v, ld_sem.at[0])
    load_f = pltpu.make_async_copy(f_hbm, f_v, ld_sem.at[1])
    load_a.start()
    load_f.start()
    load_l.wait()
    load_a.wait()
    load_f.wait()

    def partial(s):
        for p in range(3):
            rb = lists[s, r * 3 + p] - 2 * (r * 3 + p)
            picked = jnp.where(
                rb == 0, a_v[p * 256 : p * 256 + 128, :], a_v[p * 256 + 128 : p * 256 + 256, :]
            )
            for q in range(3):
                cb = lists[s, c * 3 + q] - 2 * (c * 3 + q)
                asel[p * 128 : p * 128 + 128, q * 128 : q * 128 + 128] = jnp.where(
                    cb == 0, picked[:, q * 256 : q * 256 + 128], picked[:, q * 256 + 128 : q * 256 + 256]
                )
        got = dot_t(asel[...], f_v[s])
        pp[s] = got.reshape(CHIPS, PIECE, W)

    partial(1 - k)

    pl.semaphore_wait(barrier, 20)

    for d in (1, 3):
        pl.semaphore_signal(met_a, inc=1, device_id=(r, line_z(d)), device_id_type=MESH)
    for d in range(1, 4):
        pl.semaphore_signal(met_a, inc=1, device_id=(r, line_y(d)), device_id_type=MESH)

    def swap_copy(o):
        return rcopy(pp.at[1 - k, o], half.at[o], on_send.at[o], on_recv.at[o], mate, c)

    for off in GROUP[::-1]:
        swap_copy(group_to(off)).start()
    swap_copy(j).start()

    def fcopy(o):
        return rcopy(
            f_hbm.at[lax.rem(o, 2), pl.ds(pl.multiple_of((o // 2) * PIECE, PIECE), PIECE)],
            fp, fs_send.at[o], fs_recv, o, c,
        )

    @pl.when(r == c)
    def _():
        def scatter(d, carry):
            fcopy(lax.rem(r + d, 16)).start()
            return carry

        lax.fori_loop(1, 16, scatter, 0)
        fp[...] = f_v[k, pl.ds(pl.multiple_of(j * PIECE, PIECE), PIECE), :]

    partial(k)

    def rs_copy(o, slot):
        return rcopy(qc.at[o], rs.at[slot], rs_send.at[o], rs_recv.at[slot], 2 * o + k, c)

    for off in GROUP[::-1]:
        o = group_to(off)
        swap_copy(o).wait_recv()
        qc[o] = encode(pp[k, o] + half[o])
        rs_copy(o, j).start()
    pl.semaphore_wait(met_a, 5)
    for d in range(1, 4):
        pl.semaphore_signal(met_b, inc=1, device_id=(r, line_y(d)), device_id_type=MESH)
    swap_copy(j).wait_recv()
    total = pp[k, j] + half[j]
    pl.semaphore_wait(met_b, 3)

    def tell(d, carry):
        pl.semaphore_signal(met_c, inc=1, device_id=(lax.rem(r + d, 16), c), device_id_type=MESH)
        return carry

    lax.fori_loop(1, 16, tell, 0)
    for off in GROUP:
        o = group_from(off)
        rs_copy(o, o).wait_recv()
        coded = rs[o]
        total = total - jnp.concatenate([decode_half(coded, 0), decode_half(coded, 1)], axis=1)

    @pl.when(r != c)
    def _():
        fcopy(r).wait_recv()

    high = total.astype(BF16)
    low = (total - high.astype(F32)).astype(BF16)
    left = fp[:, :128]
    right = fp[:, 128:]
    top = dot_t(left, high) + dot_t(left, low)
    dp[0:128, :] = top[:, :128]
    dp[128:256, :] = top[:, 128:]
    dp[256:384, :] = dot_t(right, high[:, 128:]) + dot_t(right, low[:, 128:])

    dpc[...] = encode_rows(dp[...].reshape(16, 24, 128))

    def around(d):
        return lax.rem(q + d, 16)

    def rows24(o):
        return pl.ds(pl.multiple_of(o * 24, 8), 24)

    def dr_copy(o, slot):
        return rcopy(
            dpc.at[o], dr.at[slot], dr_send.at[o], dr_recv.at[slot],
            zl * 8 + (o // 4) * 2 + k, zh * 4 + lax.rem(o, 4),
        )

    for off in PLANE[::-1]:
        dr_copy(plane_to(off), q).start()

    pcv[k, j] = encode(total)
    pl.semaphore_wait(met_c, 15)

    mine = k * CHIPS + j

    def cross_copy(w):
        return rcopy(pcv.at[k, j], prv.at[mine], tp_send.at[w], tp_recv.at[mine], c, w * 4 + lax.rem(r, 4))

    def is_self(w):
        return jnp.logical_and(r == c, w * 4 + lax.rem(r, 4) == c)

    for w in range(4):

        @pl.when(jnp.logical_not(is_self(w)))
        def _():
            cross_copy(w).start()

        @pl.when(is_self(w))
        def _():
            prv[mine] = pcv[k, j]

    acc = dp[rows24(q), :]
    for off in PLANE:
        o = plane_from(off)
        dr_copy(o, o).wait_recv()
        acc = acc + decode_rows(dr[o])
    dz[z] = encode_rows(acc)

    def dz_copy(d, slot):
        o = lax.rem(z + d, 8)
        return rcopy(
            dz.at[slot], dz.at[slot], dz_send.at[o], dz_recv.at[slot],
            lax.rem(o, 2) * 8 + lax.rem(r, 8), (o // 2) * 4 + y,
        )

    for d in RING_Z[::-1]:
        dz_copy(d, z).start()

    def ag_copy(d, slot):
        return rcopy(pcv.at[k, slot], pcv.at[k, slot], ag_send.at[chip(d)], ag_recv.at[slot], 2 * chip(d) + k, c)

    def ag_start(d, carry):
        ag_copy(d, j).start()
        return carry

    lax.fori_loop(1, CHIPS, ag_start, 0)

    def slot_of(col):
        return lax.rem(col, 2) * CHIPS + col // 2

    def ys_copy(d, w, col):
        slot = slot_of(col)
        return rcopy(
            prv.at[slot], prv.at[slot], ys_send.at[w, lax.rem(y + d, 4)], ys_recv.at[w, lax.rem(col, 4)], r, line_y(d)
        )

    for w in range(4):
        slot = slot_of(w * 4 + y)

        @pl.when(jnp.logical_not(jnp.logical_and(r == c, w == zh)))
        def _():
            rcopy(pcv.at[k, j], prv.at[slot], tp_send.at[w], tp_recv.at[slot], c, c).wait_recv()

        for d in range(1, 4):
            ys_copy(d, w, w * 4 + y).start()

    def dz_wait(d, carry):
        dz_copy(d, lax.rem(z + 8 - d, 8)).wait_recv()
        return carry

    lax.fori_loop(1, 8, dz_wait, 0)
    both = [decode_rows(dz[2 * i]) + decode_rows(dz[2 * i + 1]) for i in range(4)]
    dg[k, q] = encode_rows((both[0] + both[1]) + (both[2] + both[3]))

    def dg_copy(o, slot):
        return rcopy(
            dg.at[k, slot], dg.at[k, slot], dg_send.at[o], dg_recv.at[slot],
            zl * 8 + (o // 4) * 2 + k, zh * 4 + lax.rem(o, 4),
        )

    def do_copy(o, s, slot):
        return rcopy(
            dg.at[s, slot], dg.at[s, slot], do_send.at[o], do_recv.at[slot],
            zl * 8 + (o // 4) * 2 + 1 - k, zh * 4 + lax.rem(o, 4),
        )

    for off in PLANE[::-1]:
        dg_copy(plane_to(off), q).start()
        do_copy(plane_to(off), k, q).start()
    do_copy(q, k, q).start()

    def rl_copy(s, slot):
        return rcopy(pcv.at[s, slot], pcv.at[s, slot], rl_send.at[slot], rl_recv.at[slot], mate, c)

    rl_copy(k, j).start()

    def relay(d, carry):
        o = chip(CHIPS - d)
        ag_copy(d, o).wait_recv()
        rl_copy(k, o).start()
        return carry

    lax.fori_loop(1, CHIPS, relay, 0)

    for d in range(8):
        rl_copy(1 - k, d).wait_recv()

    def open_pc(o, carry):
        rows = pl.ds(pl.multiple_of(lax.rem(o, 8) * PIECE, 8), PIECE)
        coded = pcv[o // 8, lax.rem(o, 8)]
        pcf[o // 8, rows, 0:128] = decode_half(coded, 0)
        pcf[o // 8, rows, 128:256] = decode_half(coded, 1)
        return carry

    lax.fori_loop(0, 16, open_pc, 0)
    for s in range(2):
        for p in range(3):
            at = lists[s, c * 3 + p] - 2 * (c * 3 + p)
            block = jnp.transpose(pcf[s, p * BS : p * BS + BS, :])
            mirror[s, :, 2 * p * BS : 2 * p * BS + BS] = jnp.where(at == 0, block, 0.0)
            mirror[s, :, 2 * p * BS + BS : 2 * p * BS + 2 * BS] = jnp.where(at == 0, 0.0, block)
    for w in range(4):
        for d in range(1, 4):
            ys_copy(d, w, w * 4 + lax.rem(y + 4 - d, 4)).wait_recv()

    def open_pr(o, carry):
        rows = pl.ds(pl.multiple_of(lax.rem(o, 8) * PIECE, 8), PIECE)
        coded = prv[o]
        prf[o // 8, rows, 0:128] = decode_half(coded, 0)
        prf[o // 8, rows, 128:256] = decode_half(coded, 1)
        return carry

    lax.fori_loop(0, 16, open_pr, 0)
    for s in range(2):
        for p in range(3):
            at = lists[s, r * 3 + p] - 2 * (r * 3 + p)
            block = prf[s, p * BS : p * BS + BS, :]
            column[s, 2 * p * BS : 2 * p * BS + BS, :] = jnp.where(at == 0, block, 0.0)
            column[s, 2 * p * BS + BS : 2 * p * BS + 2 * BS, :] = jnp.where(at == 0, 0.0, block)
    load_d.wait()

    dgf[k, rows24(q), :] = decode_rows(dg[k, q])
    for off in PLANE:
        o = plane_from(off)
        dg_copy(o, o).wait_recv()
        dgf[k, rows24(o), :] = decode_rows(dg[k, o])
    for off in [(0, 0)] + PLANE:
        o = plane_from(off)
        do_copy(o, 1 - k, o).wait_recv()
        dgf[1 - k, rows24(o), :] = decode_rows(dg[1 - k, o])
    for s in range(2):
        upper = dgf[s, 128:256, :]
        diagonal[s, 0:128, 0:128] = diag[s, 0:128, 0:128] + dgf[s, 0:128, :]
        diagonal[s, 0:128, 128:256] = diag[s, 0:128, 128:256] + upper
        diagonal[s, 128:256, 0:128] = diag[s, 128:256, 0:128] + jnp.transpose(upper)
        diagonal[s, 128:256, 128:256] = diag[s, 128:256, 128:256] + dgf[s, 256:384, :]

    def swap_drain(d, carry):
        swap_copy(d).wait_send()
        return carry

    lax.fori_loop(0, CHIPS, swap_drain, 0)

    for w in range(4):

        @pl.when(jnp.logical_not(is_self(w)))
        def _():
            cross_copy(w).wait_send()

    @pl.when(r == c)
    def _():
        def scattered(d, carry):
            fcopy(lax.rem(r + d, 16)).wait_send()
            return carry

        lax.fori_loop(1, 16, scattered, 0)

    def drain(d, carry):
        rs_copy(chip(d), j).wait_send()
        ag_copy(d, j).wait_send()
        dz_copy(d, z).wait_send()
        return carry

    lax.fori_loop(1, CHIPS, drain, 0)
    for d in range(CHIPS):
        rl_copy(k, d).wait_send()
    for d in range(1, 4):
        for w in range(4):
            ys_copy(d, w, w * 4 + y).wait_send()

    def drain_plane(d, carry):
        dr_copy(around(d), q).wait_send()
        dg_copy(around(d), q).wait_send()
        return carry

    lax.fori_loop(1, 16, drain_plane, 0)

    def drain_relay(d, carry):
        do_copy(d, k, q).wait_send()
        return carry

    lax.fori_loop(0, 16, drain_relay, 0)


def exchange(blocks_inverse, factor_rows, block_lists, diag_inverse):
    dma = pltpu.SemaphoreType.DMA
    hbm = pl.BlockSpec(memory_space=pl.ANY)
    vmem = pl.BlockSpec(memory_space=pltpu.VMEM)
    return pl.pallas_call(
        comm_kernel,
        out_shape=(pltpu.VMEM((2, 768, W), F32), pltpu.VMEM((2, W, 768), F32), pltpu.VMEM((2, W, W), F32)),
        in_specs=[hbm] * 4,
        out_specs=(vmem, vmem, vmem),
        scratch_shapes=[
            pltpu.SMEM((2, 48), jnp.int32),
            pltpu.VMEM((2, W, W), F32),
            pltpu.VMEM((768, 768), BF16),
            pltpu.VMEM((2, 384, W), BF16),
            pltpu.VMEM((384, 384), BF16),
            pltpu.VMEM((PIECE, W), BF16),
            pltpu.VMEM((2, CHIPS, PIECE, W), F32),
            pltpu.VMEM((2, CHIPS, CODED, 128), jnp.int16),
            pltpu.VMEM((16, CODED, 128), jnp.int16),
            pltpu.VMEM((CHIPS, PIECE, W), F32),
            pltpu.VMEM((CHIPS, CODED, 128), jnp.int16),
            pltpu.VMEM((CHIPS, CODED, 128), jnp.int16),
            pltpu.VMEM((384, 128), F32),
            pltpu.VMEM((16, 32, 128), jnp.int16),
            pltpu.VMEM((16, 32, 128), jnp.int16),
            pltpu.VMEM((8, 32, 128), jnp.int16),
            pltpu.VMEM((2, 16, 32, 128), jnp.int16),
            pltpu.VMEM((2, 384, 128), F32),
            pltpu.VMEM((2, 384, W), F32),
            pltpu.VMEM((2, 384, W), F32),
            dma((4,)), dma((16,)), dma, dma((8,)), dma((8,)), dma((8,)), dma((8,)),
            dma((8,)), dma((8,)), dma((8,)), dma((8,)), dma((4,)), dma((16,)),
            dma((4, 4)), dma((4, 4)), dma((16,)), dma((16,)), dma((8,)), dma((8,)),
            dma((16,)), dma((16,)), dma((16,)), dma((16,)),
            pltpu.SemaphoreType.REGULAR, pltpu.SemaphoreType.REGULAR, pltpu.SemaphoreType.REGULAR,
        ],
        compiler_params=pltpu.CompilerParams(collective_id=0, has_side_effects=True, vmem_limit_bytes=63300000),
        name="exchange",
    )(block_lists, blocks_inverse, factor_rows, diag_inverse)


def store_kernel(column, mirror, diagonal, column_out, mirror_out, diagonal_out, sems):
    copies = [
        pltpu.make_async_copy(diagonal, diagonal_out, sems.at[0]),
        pltpu.make_async_copy(column, column_out, sems.at[1]),
        pltpu.make_async_copy(mirror, mirror_out, sems.at[2]),
    ]
    for copy in copies:
        copy.start()
    for copy in copies:
        copy.wait()


def store(column, mirror, diagonal):
    hbm = pl.BlockSpec(memory_space=pl.ANY)
    return pl.pallas_call(
        store_kernel,
        out_shape=tuple(jax.ShapeDtypeStruct(a.shape, F32) for a in (column, mirror, diagonal)),
        in_specs=[pl.BlockSpec(memory_space=pltpu.VMEM)] * 3,
        out_specs=(hbm, hbm, hbm),
        scratch_shapes=[pltpu.SemaphoreType.DMA((3,))],
        compiler_params=pltpu.CompilerParams(vmem_limit_bytes=8 << 20),
        name="store",
    )(column, mirror, diagonal)


def local(blocks_inverse, factor_rows, block_lists, diag_inverse):
    return store(*exchange(blocks_inverse, factor_rows, block_lists, diag_inverse))


def solution(mesh):
    return jax.shard_map(
        local,
        mesh=mesh,
        in_specs=(P("row", "col"), P(None, "row", None), P(), P()),
        out_specs=(P(None, "row", None), P(None, None, "col"), P()),
        check_vma=False,
    )
```

```python
import jax
import jax.numpy as jnp
from jax import lax
from jax.experimental import pallas as pl
from jax.experimental.pallas import tpu as pltpu
from jax.sharding import PartitionSpec as P

BS = 128
W = 256
CHIPS = 8
PIECE = 48
CODED = 112
TOP = 32000.0
MESH = pl.DeviceIdType.MESH
F32 = jnp.float32
BF16 = jnp.bfloat16


def dot_t(a, b):
    return lax.dot_general(a, b, (((0,), (0,)), ((), ())), preferred_element_type=F32)


def ring(d, n):
    return min(d, n - d)


PLANE = sorted(((i, e) for i in range(4) for e in range(4) if i + e), key=lambda t: ring(t[0], 4) + ring(t[1], 4))
GROUP = sorted(((i, e) for i in range(2) for e in range(4) if i + e), key=lambda t: t[0] + ring(t[1], 4))
RING_Z = sorted(range(1, 8), key=lambda d: ring(d, 8))


def encode(piece):
    parts = []
    steps = []
    for half in range(2):
        part = piece[:, half * 128 : half * 128 + 128]
        most = jnp.max(jnp.abs(part), axis=0, keepdims=True)
        level = jnp.clip(jnp.ceil(8.0 * jnp.log2(jnp.maximum(most, 1e-30))), -800.0, 1000.0)
        factor = jnp.exp2(level * -0.125) * TOP
        parts.append(jnp.round(part * factor).astype(jnp.int32).astype(jnp.int16))
        steps.append(jnp.broadcast_to(level, (8, 128)))
    steps = jnp.concatenate(steps, axis=0).astype(jnp.int32).astype(jnp.int16)
    return jnp.concatenate(parts + [steps], axis=0)


def decode_half(coded, half):
    level = coded[96:112, :].astype(jnp.int32).astype(F32)[8 * half : 8 * half + 1, :]
    step = jnp.exp2(level * 0.125) * (-1.0 / TOP)
    return coded[PIECE * half : PIECE * half + PIECE, :].astype(jnp.int32).astype(F32) * step


def encode_rows(part):
    most = jnp.max(jnp.abs(part), axis=-2, keepdims=True)
    level = jnp.clip(jnp.ceil(8.0 * jnp.log2(jnp.maximum(most, 1e-30))), -800.0, 1000.0)
    coded = jnp.round(part * (jnp.exp2(level * -0.125) * TOP)).astype(jnp.int32)
    steps = jnp.broadcast_to(level, part.shape[:-2] + (8, 128)).astype(jnp.int32)
    return jnp.concatenate([coded, steps], axis=-2).astype(jnp.int16)


def decode_rows(coded):
    wide = coded.astype(jnp.int32).astype(F32)
    return wide[:24, :] * (jnp.exp2(wide[24:25, :] * 0.125) * (1.0 / TOP))


def comm_kernel(
    lists_hbm, a_hbm, f_hbm, diag_hbm, column, mirror, diagonal, lists, diag,
    a_v, f_v, asel, fp, pp, pcv, prv, half, rs, qc, dp, dpc, dr, dz, dg, dgf, pcf, prf,
    ld_sem, fs_send, fs_recv, on_send, on_recv, rs_send, rs_recv,
    ag_send, ag_recv, rl_send, rl_recv, tp_send, tp_recv,
    ys_send, ys_recv, dr_send, dr_recv, dz_send, dz_recv,
    dg_send, dg_recv, do_send, do_recv, met_a, met_b, met_c,
):
    r = lax.axis_index("row")
    c = lax.axis_index("col")
    k = lax.rem(r, 2)
    j = r // 2
    y = lax.rem(c, 4)
    zh = c // 4
    x = lax.rem(j, 4)
    zl = j // 4
    z = zh * 2 + zl
    q = x * 4 + y
    mate = r + 1 - 2 * k
    ck = lax.rem(c, 2)
    cj = c // 2

    def chip(d):
        return lax.rem(j + d, CHIPS)

    def group_to(off):
        return lax.rem(zl + off[0], 2) * 4 + lax.rem(x + off[1], 4)

    def group_from(off):
        return lax.rem(zl + off[0], 2) * 4 + lax.rem(x + 4 - off[1], 4)

    def plane_to(off):
        return lax.rem(x + off[0], 4) * 4 + lax.rem(y + off[1], 4)

    def plane_from(off):
        return lax.rem(x + 4 - off[0], 4) * 4 + lax.rem(y + 4 - off[1], 4)

    def rcopy(src, dst, ssem, rsem, row, col):
        return pltpu.make_async_remote_copy(
            src_ref=src, dst_ref=dst, send_sem=ssem, recv_sem=rsem,
            device_id=(row, col), device_id_type=MESH,
        )

    barrier = pltpu.get_barrier_semaphore()

    def line_y(d):
        return zh * 4 + lax.rem(y + d, 4)

    def line_z(d):
        return lax.rem(zh + d, 4) * 4 + y

    for d in (1, 3):
        pl.semaphore_signal(barrier, inc=1, device_id=(r, line_z(d)), device_id_type=MESH)
    for d in range(1, 4):
        pl.semaphore_signal(barrier, inc=1, device_id=(r, line_y(d)), device_id_type=MESH)

    def greet(d, carry):
        pl.semaphore_signal(barrier, inc=1, device_id=(lax.rem(r + d, 16), c), device_id_type=MESH)
        return carry

    lax.fori_loop(1, 16, greet, 0)

    load_l = pltpu.make_async_copy(lists_hbm, lists, ld_sem.at[2])
    load_l.start()
    load_d = pltpu.make_async_copy(diag_hbm, diag, ld_sem.at[3])
    load_d.start()
    load_a = pltpu.make_async_copy(a_hbm, a_v, ld_sem.at[0])
    load_f = pltpu.make_async_copy(f_hbm, f_v, ld_sem.at[1])
    load_a.start()
    load_f.start()
    load_l.wait()
    load_a.wait()
    load_f.wait()

    def partial(s):
        for p in range(3):
            rb = lists[s, r * 3 + p] - 2 * (r * 3 + p)
            picked = jnp.where(
                rb == 0, a_v[p * 256 : p * 256 + 128, :], a_v[p * 256 + 128 : p * 256 + 256, :]
            )
            for q in range(3):
                cb = lists[s, c * 3 + q] - 2 * (c * 3 + q)
                asel[p * 128 : p * 128 + 128, q * 128 : q * 128 + 128] = jnp.where(
                    cb == 0, picked[:, q * 256 : q * 256 + 128], picked[:, q * 256 + 128 : q * 256 + 256]
                )
        got = dot_t(asel[...], f_v[s])
        pp[s] = got.reshape(CHIPS, PIECE, W)

    partial(1 - k)

    pl.semaphore_wait(barrier, 20)

    for d in (1, 3):
        pl.semaphore_signal(met_a, inc=1, device_id=(r, line_z(d)), device_id_type=MESH)
    for d in range(1, 4):
        pl.semaphore_signal(met_a, inc=1, device_id=(r, line_y(d)), device_id_type=MESH)

    def swap_copy(o):
        return rcopy(pp.at[1 - k, o], half.at[o], on_send.at[o], on_recv.at[o], mate, c)

    for off in GROUP[::-1]:
        swap_copy(group_to(off)).start()
    swap_copy(j).start()

    def fcopy(o):
        return rcopy(
            f_hbm.at[lax.rem(o, 2), pl.ds(pl.multiple_of((o // 2) * PIECE, PIECE), PIECE)],
            fp, fs_send.at[o], fs_recv, o, c,
        )

    @pl.when(r == c)
    def _():
        def scatter(d, carry):
            fcopy(lax.rem(r + d, 16)).start()
            return carry

        lax.fori_loop(1, 16, scatter, 0)
        fp[...] = f_v[k, pl.ds(pl.multiple_of(j * PIECE, PIECE), PIECE), :]

    partial(k)

    def rs_copy(o, slot):
        return rcopy(qc.at[o], rs.at[slot], rs_send.at[o], rs_recv.at[slot], 2 * o + k, c)

    for off in GROUP[::-1]:
        o = group_to(off)
        swap_copy(o).wait_recv()
        qc[o] = encode(pp[k, o] + half[o])
        rs_copy(o, j).start()
    pl.semaphore_wait(met_a, 5)
    for d in range(1, 4):
        pl.semaphore_signal(met_b, inc=1, device_id=(r, line_y(d)), device_id_type=MESH)
    swap_copy(j).wait_recv()
    total = pp[k, j] + half[j]
    pl.semaphore_wait(met_b, 3)

    def tell(d, carry):
        pl.semaphore_signal(met_c, inc=1, device_id=(lax.rem(r + d, 16), c), device_id_type=MESH)
        return carry

    lax.fori_loop(1, 16, tell, 0)
    for off in GROUP:
        o = group_from(off)
        rs_copy(o, o).wait_recv()
        coded = rs[o]
        total = total - jnp.concatenate([decode_half(coded, 0), decode_half(coded, 1)], axis=1)

    @pl.when(r != c)
    def _():
        fcopy(r).wait_recv()

    high = total.astype(BF16)
    low = (total - high.astype(F32)).astype(BF16)
    left = fp[:, :128]
    right = fp[:, 128:]
    top = dot_t(left, high) + dot_t(left, low)
    dp[0:128, :] = top[:, :128]
    dp[128:256, :] = top[:, 128:]
    dp[256:384, :] = dot_t(right, high[:, 128:]) + dot_t(right, low[:, 128:])

    dpc[...] = encode_rows(dp[...].reshape(16, 24, 128))

    def around(d):
        return lax.rem(q + d, 16)

    def rows24(o):
        return pl.ds(pl.multiple_of(o * 24, 8), 24)

    def dr_copy(o, slot):
        return rcopy(
            dpc.at[o], dr.at[slot], dr_send.at[o], dr_recv.at[slot],
            zl * 8 + (o // 4) * 2 + k, zh * 4 + lax.rem(o, 4),
        )

    for off in PLANE[::-1]:
        dr_copy(plane_to(off), q).start()

    pcv[k, j] = encode(total)
    pl.semaphore_wait(met_c, 15)

    mine = k * CHIPS + j

    def cross_copy(w):
        return rcopy(pcv.at[k, j], prv.at[mine], tp_send.at[w], tp_recv.at[mine], c, w * 4 + lax.rem(r, 4))

    def is_self(w):
        return jnp.logical_and(r == c, w * 4 + lax.rem(r, 4) == c)

    for w in range(4):

        @pl.when(jnp.logical_not(is_self(w)))
        def _():
            cross_copy(w).start()

        @pl.when(is_self(w))
        def _():
            prv[mine] = pcv[k, j]

    acc = dp[rows24(q), :]
    for off in PLANE:
        o = plane_from(off)
        dr_copy(o, o).wait_recv()
        acc = acc + decode_rows(dr[o])
    dz[z] = encode_rows(acc)

    def dz_copy(d, slot):
        o = lax.rem(z + d, 8)
        return rcopy(
            dz.at[slot], dz.at[slot], dz_send.at[o], dz_recv.at[slot],
            lax.rem(o, 2) * 8 + lax.rem(r, 8), (o // 2) * 4 + y,
        )

    for d in RING_Z[::-1]:
        dz_copy(d, z).start()

    def slot_of(col):
        return lax.rem(col, 2) * CHIPS + col // 2

    def ys_copy(d, w, col):
        slot = slot_of(col)
        return rcopy(
            prv.at[slot], prv.at[slot], ys_send.at[w, lax.rem(y + d, 4)], ys_recv.at[w, lax.rem(col, 4)], r, line_y(d)
        )

    for w in range(4):
        slot = slot_of(w * 4 + y)

        @pl.when(jnp.logical_not(jnp.logical_and(r == c, w == zh)))
        def _():
            rcopy(pcv.at[k, j], prv.at[slot], tp_send.at[w], tp_recv.at[slot], c, c).wait_recv()

        for d in range(1, 4):
            ys_copy(d, w, w * 4 + y).start()

    def ag_copy(d, slot):
        return rcopy(pcv.at[k, slot], pcv.at[k, slot], ag_send.at[chip(d)], ag_recv.at[slot], 2 * chip(d) + k, c)

    def ag_start(d, carry):
        ag_copy(d, j).start()
        return carry

    lax.fori_loop(1, CHIPS, ag_start, 0)

    def dz_wait(d, carry):
        dz_copy(d, lax.rem(z + 8 - d, 8)).wait_recv()
        return carry

    lax.fori_loop(1, 8, dz_wait, 0)
    both = [decode_rows(dz[2 * i]) + decode_rows(dz[2 * i + 1]) for i in range(4)]
    dg[k, q] = encode_rows((both[0] + both[1]) + (both[2] + both[3]))

    def dg_copy(o, slot):
        return rcopy(
            dg.at[k, slot], dg.at[k, slot], dg_send.at[o], dg_recv.at[slot],
            zl * 8 + (o // 4) * 2 + k, zh * 4 + lax.rem(o, 4),
        )

    def do_copy(o, s, slot):
        return rcopy(
            dg.at[s, slot], dg.at[s, slot], do_send.at[o], do_recv.at[slot],
            zl * 8 + (o // 4) * 2 + 1 - k, zh * 4 + lax.rem(o, 4),
        )

    for off in PLANE[::-1]:
        dg_copy(plane_to(off), q).start()
        do_copy(plane_to(off), k, q).start()
    do_copy(q, k, q).start()

    def rl_copy(s, slot):
        return rcopy(pcv.at[s, slot], pcv.at[s, slot], rl_send.at[slot], rl_recv.at[slot], mate, c)

    rl_copy(k, j).start()

    def relay(d, carry):
        o = chip(CHIPS - d)
        ag_copy(d, o).wait_recv()
        rl_copy(k, o).start()
        return carry

    lax.fori_loop(1, CHIPS, relay, 0)

    for d in range(8):
        rl_copy(1 - k, d).wait_recv()

    def open_pc(o, carry):
        rows = pl.ds(pl.multiple_of(lax.rem(o, 8) * PIECE, 8), PIECE)
        coded = pcv[o // 8, lax.rem(o, 8)]
        pcf[o // 8, rows, 0:128] = decode_half(coded, 0)
        pcf[o // 8, rows, 128:256] = decode_half(coded, 1)
        return carry

    lax.fori_loop(0, 16, open_pc, 0)
    for s in range(2):
        for p in range(3):
            at = lists[s, c * 3 + p] - 2 * (c * 3 + p)
            block = jnp.transpose(pcf[s, p * BS : p * BS + BS, :])
            mirror[s, :, 2 * p * BS : 2 * p * BS + BS] = jnp.where(at == 0, block, 0.0)
            mirror[s, :, 2 * p * BS + BS : 2 * p * BS + 2 * BS] = jnp.where(at == 0, 0.0, block)
    for w in range(4):
        for d in range(1, 4):
            ys_copy(d, w, w * 4 + lax.rem(y + 4 - d, 4)).wait_recv()

    def open_pr(o, carry):
        rows = pl.ds(pl.multiple_of(lax.rem(o, 8) * PIECE, 8), PIECE)
        coded = prv[o]
        prf[o // 8, rows, 0:128] = decode_half(coded, 0)
        prf[o // 8, rows, 128:256] = decode_half(coded, 1)
        return carry

    lax.fori_loop(0, 16, open_pr, 0)
    for s in range(2):
        for p in range(3):
            at = lists[s, r * 3 + p] - 2 * (r * 3 + p)
            block = prf[s, p * BS : p * BS + BS, :]
            column[s, 2 * p * BS : 2 * p * BS + BS, :] = jnp.where(at == 0, block, 0.0)
            column[s, 2 * p * BS + BS : 2 * p * BS + 2 * BS, :] = jnp.where(at == 0, 0.0, block)
    load_d.wait()

    dgf[k, rows24(q), :] = decode_rows(dg[k, q])
    for off in PLANE:
        o = plane_from(off)
        dg_copy(o, o).wait_recv()
        dgf[k, rows24(o), :] = decode_rows(dg[k, o])
    for off in [(0, 0)] + PLANE:
        o = plane_from(off)
        do_copy(o, 1 - k, o).wait_recv()
        dgf[1 - k, rows24(o), :] = decode_rows(dg[1 - k, o])
    for s in range(2):
        upper = dgf[s, 128:256, :]
        diagonal[s, 0:128, 0:128] = diag[s, 0:128, 0:128] + dgf[s, 0:128, :]
        diagonal[s, 0:128, 128:256] = diag[s, 0:128, 128:256] + upper
        diagonal[s, 128:256, 0:128] = diag[s, 128:256, 0:128] + jnp.transpose(upper)
        diagonal[s, 128:256, 128:256] = diag[s, 128:256, 128:256] + dgf[s, 256:384, :]

    def swap_drain(d, carry):
        swap_copy(d).wait_send()
        return carry

    lax.fori_loop(0, CHIPS, swap_drain, 0)

    for w in range(4):

        @pl.when(jnp.logical_not(is_self(w)))
        def _():
            cross_copy(w).wait_send()

    @pl.when(r == c)
    def _():
        def scattered(d, carry):
            fcopy(lax.rem(r + d, 16)).wait_send()
            return carry

        lax.fori_loop(1, 16, scattered, 0)

    def drain(d, carry):
        rs_copy(chip(d), j).wait_send()
        ag_copy(d, j).wait_send()
        dz_copy(d, z).wait_send()
        return carry

    lax.fori_loop(1, CHIPS, drain, 0)
    for d in range(CHIPS):
        rl_copy(k, d).wait_send()
    for d in range(1, 4):
        for w in range(4):
            ys_copy(d, w, w * 4 + y).wait_send()

    def drain_plane(d, carry):
        dr_copy(around(d), q).wait_send()
        dg_copy(around(d), q).wait_send()
        return carry

    lax.fori_loop(1, 16, drain_plane, 0)

    def drain_relay(d, carry):
        do_copy(d, k, q).wait_send()
        return carry

    lax.fori_loop(0, 16, drain_relay, 0)


def exchange(blocks_inverse, factor_rows, block_lists, diag_inverse):
    dma = pltpu.SemaphoreType.DMA
    hbm = pl.BlockSpec(memory_space=pl.ANY)
    vmem = pl.BlockSpec(memory_space=pltpu.VMEM)
    return pl.pallas_call(
        comm_kernel,
        out_shape=(pltpu.VMEM((2, 768, W), F32), pltpu.VMEM((2, W, 768), F32), pltpu.VMEM((2, W, W), F32)),
        in_specs=[hbm] * 4,
        out_specs=(vmem, vmem, vmem),
        scratch_shapes=[
            pltpu.SMEM((2, 48), jnp.int32),
            pltpu.VMEM((2, W, W), F32),
            pltpu.VMEM((768, 768), BF16),
            pltpu.VMEM((2, 384, W), BF16),
            pltpu.VMEM((384, 384), BF16),
            pltpu.VMEM((PIECE, W), BF16),
            pltpu.VMEM((2, CHIPS, PIECE, W), F32),
            pltpu.VMEM((2, CHIPS, CODED, 128), jnp.int16),
            pltpu.VMEM((16, CODED, 128), jnp.int16),
            pltpu.VMEM((CHIPS, PIECE, W), F32),
            pltpu.VMEM((CHIPS, CODED, 128), jnp.int16),
            pltpu.VMEM((CHIPS, CODED, 128), jnp.int16),
            pltpu.VMEM((384, 128), F32),
            pltpu.VMEM((16, 32, 128), jnp.int16),
            pltpu.VMEM((16, 32, 128), jnp.int16),
            pltpu.VMEM((8, 32, 128), jnp.int16),
            pltpu.VMEM((2, 16, 32, 128), jnp.int16),
            pltpu.VMEM((2, 384, 128), F32),
            pltpu.VMEM((2, 384, W), F32),
            pltpu.VMEM((2, 384, W), F32),
            dma((4,)), dma((16,)), dma, dma((8,)), dma((8,)), dma((8,)), dma((8,)),
            dma((8,)), dma((8,)), dma((8,)), dma((8,)), dma((4,)), dma((16,)),
            dma((4, 4)), dma((4, 4)), dma((16,)), dma((16,)), dma((8,)), dma((8,)),
            dma((16,)), dma((16,)), dma((16,)), dma((16,)),
            pltpu.SemaphoreType.REGULAR, pltpu.SemaphoreType.REGULAR, pltpu.SemaphoreType.REGULAR,
        ],
        compiler_params=pltpu.CompilerParams(collective_id=0, has_side_effects=True, vmem_limit_bytes=63300000),
        name="exchange",
    )(block_lists, blocks_inverse, factor_rows, diag_inverse)


def store_kernel(column, mirror, diagonal, column_out, mirror_out, diagonal_out, sems):
    copies = [
        pltpu.make_async_copy(diagonal, diagonal_out, sems.at[0]),
        pltpu.make_async_copy(column, column_out, sems.at[1]),
        pltpu.make_async_copy(mirror, mirror_out, sems.at[2]),
    ]
    for copy in copies:
        copy.start()
    for copy in copies:
        copy.wait()


def store(column, mirror, diagonal):
    hbm = pl.BlockSpec(memory_space=pl.ANY)
    return pl.pallas_call(
        store_kernel,
        out_shape=tuple(jax.ShapeDtypeStruct(a.shape, F32) for a in (column, mirror, diagonal)),
        in_specs=[pl.BlockSpec(memory_space=pltpu.VMEM)] * 3,
        out_specs=(hbm, hbm, hbm),
        scratch_shapes=[pltpu.SemaphoreType.DMA((3,))],
        compiler_params=pltpu.CompilerParams(vmem_limit_bytes=8 << 20),
        name="store",
    )(column, mirror, diagonal)


def local(blocks_inverse, factor_rows, block_lists, diag_inverse):
    return store(*exchange(blocks_inverse, factor_rows, block_lists, diag_inverse))


def solution(mesh):
    return jax.shard_map(
        local,
        mesh=mesh,
        in_specs=(P("row", "col"), P(None, "row", None), P(), P()),
        out_specs=(P(None, "row", None), P(None, None, "col"), P()),
        check_vma=False,
    )
```
